32 devices in a mesh: rep: 8 (over y, x, core), fsdp: 4 (over z).
Axes of the slice: x: 2, y: 2, z: 4, core: 2. Of those that a mesh axis runs over, the one named last changes fastest.
Arguments:
- inputs: bfloat16 [24576, 768], P(('rep', 'fsdp')), may hold values from -6 to 6
- first_values: bfloat16 [24576, 384], P(('rep', 'fsdp')), may hold values from -6 to 6
- cotangent: bfloat16 [24576, 768], P(('rep', 'fsdp')), may hold values from -6 to 6
- tree_ids: int32 [24576], P('rep'), may hold values from 0 to 2, as said below
- segment_ids: int32 [24576], P('rep'), may hold values from 0 to 12, as said below
- path_table: int32 [24, 13, 3], P('rep'), may hold values from 0 to 12, as said below
- attn_gain: bfloat16 [768], P('fsdp'), may hold values from 0.5 to 1.5
- attn_shift: bfloat16 [768], P('fsdp'), may hold values from -3 to 3
- w_query: bfloat16 [768, 768], P('fsdp'), may hold values from -0.21875 to 0.21875
- w_key: bfloat16 [768, 768], P('fsdp'), may hold values from -0.21875 to 0.21875
- w_value: bfloat16 [768, 384], P('fsdp'), may hold values from -0.21875 to 0.21875
- w_out: bfloat16 [768, 768], P('fsdp'), may hold values from -1.75 to 1.75
- mlp_gain: bfloat16 [768], P('fsdp'), may hold values from 0.5 to 1.5
- mlp_shift: bfloat16 [768], P('fsdp'), may hold values from -3 to 3
- w_in: bfloat16 [768, 3072], P('fsdp'), may hold values from -0.21875 to 0.21875
- w_down: bfloat16 [3072, 768], P('fsdp'), may hold values from -0.109375 to 0.109375
Outputs:
- outputs: bfloat16 [24576, 768], P(('rep', 'fsdp'))
- input_grad: float32 [24576, 768], P(('rep', 'fsdp'))
- first_values_grad: float32 [24576, 384], P(('rep', 'fsdp'))
- attn_gain_grad: float32 [768], P('fsdp')
- attn_shift_grad: float32 [768], P('fsdp')
- w_query_grad: float32 [768, 768], P('fsdp')
- w_key_grad: float32 [768, 768], P('fsdp')
- w_value_grad: float32 [768, 384], P('fsdp')
- w_out_grad: float32 [768, 768], P('fsdp')
- mlp_gain_grad: float32 [768], P('fsdp')
- mlp_shift_grad: float32 [768], P('fsdp')
- w_in_grad: float32 [768, 3072], P('fsdp')
- w_down_grad: float32 [3072, 768], P('fsdp')
The draws below stay inside these ranges and needn't reach their ends.
Inputs may be any that keep to these rules, and one draw needn't show every extreme that they name: `tree_ids`: within each aligned block of 3072 tokens every tree number 0 to 2 covers exactly one aligned run of 1024 consecutive tokens. `segment_ids`: each tree's tokens are its trunk (segment 0, 512 tokens), then 4 branches of 64 tokens numbered 1 to 4 in some order, then 4 * 2 leaves of 32 tokens numbered 4 + 1 and up in some order. `path_table`: row t, s lists the trunk, the branch and the leaf on the path to segment s of tree t, repeating the segment itself where it is shallower; every branch is the parent of 2 leaves. Tree t of group r is row r * 3 + t.
All inputs are finite; a program needn't handle non-finite values.
Results may differ from the reference program's by a relative error of at most 0.013.
Values may be sent and summed in bfloat16 or wider, within the bound.
A program may use at most 192 MiB of HBM per device.

```python
import jax
import jax.numpy as jnp
from jax import lax

D = 768
HEADS = 12
HEAD = 64
FF = 3072
TREES_GRP = 3
TRUNK = 512
BRANCH = 64
LEAF = 32
BRANCHES = 4
LEAVES = 2
SEGS = 13
TREE_LEN = 1024
TREES = 24
TOKENS = 24576
N_REP = 8


def draw_tree_ids(key, part):
    group_count = TOKENS // (TREES_GRP * TREE_LEN)
    group_keys = jax.random.split(key, group_count)
    orders = jax.vmap(lambda single: jax.random.permutation(single, TREES_GRP))(group_keys)
    return jnp.repeat(orders.astype(jnp.int32), TREE_LEN, axis=1).reshape(-1)


def draw_segment_ids(key, part):
    tree_count = TOKENS // TREE_LEN
    tree_keys = jax.random.split(key, tree_count)

    def one_tree(single):
        branch_key, leaf_key = jax.random.split(single)
        branch_labels = jax.random.permutation(branch_key, BRANCHES).astype(jnp.int32) + 1
        leaf_labels = jax.random.permutation(leaf_key, BRANCHES * LEAVES).astype(jnp.int32) + 1 + BRANCHES
        trunk_part = jnp.zeros((TRUNK,), jnp.int32)
        return jnp.concatenate([trunk_part, jnp.repeat(branch_labels, BRANCH), jnp.repeat(leaf_labels, LEAF)])
    return jax.vmap(one_tree)(tree_keys).reshape(-1)


def draw_path_table(key, part):
    tree_keys = jax.random.split(key, TREES)

    def one_tree(single):
        parents = jax.random.permutation(single, jnp.repeat(jnp.arange(1, BRANCHES + 1, dtype=jnp.int32), LEAVES)).astype(jnp.int32)
        depth_zero = jnp.zeros((SEGS,), jnp.int32)
        depth_one = jnp.concatenate([jnp.zeros((1,), jnp.int32), jnp.arange(1, BRANCHES + 1, dtype=jnp.int32), parents])
        depth_two = jnp.arange(SEGS, dtype=jnp.int32)
        return jnp.stack([depth_zero, depth_one, depth_two], axis=1)
    return jax.vmap(one_tree)(tree_keys)


def with_spikes(array, own_key, source, target, shards_of, factor):
    owner, partner = [(jnp.arange(array.shape[axis_at]) // (array.shape[axis_at] // shards_of)).reshape([-1 if axis == axis_at else 1 for axis in range(array.ndim)]) for axis_at in (source, target)]
    chosen = jax.random.permutation(own_key, shards_of)[partner]
    strong = (owner == chosen) | (owner == (partner + shards_of // 2) % shards_of)
    return jnp.where(strong, factor * array, array)


def block_levels(stream_key, shape, cuts, smallest, high):
    gain, own = 1.0, jax.random.fold_in(stream_key, 6)
    for axis_at, parts in cuts:
        draws = jnp.exp(jax.random.uniform(jax.random.fold_in(own, axis_at), (parts,), jnp.float32, smallest / len(cuts), high / len(cuts)))
        gain = gain * jnp.repeat(draws, shape[axis_at] // parts).reshape([-1 if axis == axis_at else 1 for axis in range(len(shape))])
    return gain


def centred(key, shape, width, limit, cuts=(), kind=jnp.bfloat16):
    level = block_levels(key, shape, cuts, -0.22, 0.18) if cuts else 1.0
    array = jax.random.normal(key, shape, jnp.float32) * width * level
    return jnp.minimum(jnp.maximum(array, -limit), limit).astype(kind)


def bell_draw_with(rng, shape, scale, most, pieces, heavy, kind=jnp.bfloat16):
    values = scale * jax.random.normal(rng, shape, jnp.float32)
    if pieces:
        values = values * block_levels(rng, shape, pieces, -0.22, 0.18)
    return jnp.clip(with_spikes(values, jax.random.fold_in(rng, 3), *heavy), -most, most).astype(kind)


def setup_inputs(seed: int = 0) -> dict:
    streams_of = jax.random.split(jax.random.key(seed), 17)
    inputs = centred(streams_of[0], (TOKENS, D), 1.0, 6.0, ((0, 32),))
    first_values = centred(streams_of[1], (TOKENS, D // 2), 1.0, 6.0, ((0, 32),))
    cotangent = bell_draw_with(streams_of[2], (TOKENS, D), 1.0, 6.0, ((0, 32),), (0, 1, 32, 2.75))
    tree_ids = draw_tree_ids(jax.random.fold_in(streams_of[16], 71), 0)
    segment_ids = draw_segment_ids(jax.random.fold_in(streams_of[16], 71), 0)
    path_table = draw_path_table(jax.random.fold_in(streams_of[16], 71), 0)
    attn_gain = jnp.clip(0.5 + 1.0 * jax.random.uniform(streams_of[6], (D,), jnp.float32) ** block_levels(streams_of[6], (D,), ((0, 4),), -0.2, 0.2), 0.5, 1.5).astype(jnp.bfloat16)
    attn_shift = centred(streams_of[7], (D,), 0.5, 3.0, ((0, 4),))
    w_query = centred(streams_of[8], (D, D), D ** -0.5, 0.21875, ((0, 4),))
    w_key = centred(streams_of[9], (D, D), D ** -0.5, 0.21875, ((0, 4),))
    w_value = centred(streams_of[10], (D, D // 2), D ** -0.5, 0.21875, ((0, 4),))
    w_out = centred(streams_of[11], (D, D), (D // 64) ** -0.5, 1.75, ((0, 4),))
    mlp_gain = jnp.clip(0.5 + 1.0 * jax.random.uniform(streams_of[12], (D,), jnp.float32) ** block_levels(streams_of[12], (D,), ((0, 4),), -0.2, 0.2), 0.5, 1.5).astype(jnp.bfloat16)
    mlp_shift = centred(streams_of[13], (D,), 0.5, 3.0, ((0, 4),))
    w_in = centred(streams_of[14], (D, FF), D ** -0.5, 0.21875, ((0, 4),))
    w_down = centred(streams_of[15], (FF, D), FF ** -0.5, 0.109375, ((0, 4),))
    return dict(inputs=inputs, first_values=first_values, cotangent=cotangent, tree_ids=tree_ids, segment_ids=segment_ids, path_table=path_table, attn_gain=attn_gain, attn_shift=attn_shift, w_query=w_query, w_key=w_key, w_value=w_value, w_out=w_out, mlp_gain=mlp_gain, mlp_shift=mlp_shift, w_in=w_in, w_down=w_down)


@jax.custom_vjp
def low(v):
    return lax.optimization_barrier(v.astype(jnp.bfloat16)).astype(jnp.float32)

@jax.custom_vjp
def low_back(v):
    return v

def low_keep(v):
    return (low(v), None)

def low_pass(kept, grad):
    return (grad,)

def back_keep(v):
    return (v, None)

def back_low(kept, grad):
    return (low(grad),)
low.defvjp(low_keep, low_pass)
low_back.defvjp(back_keep, back_low)
epsilon = 1e-05
far_below = -1e+30

def product(left, right):
    return jnp.dot(left, right, precision=lax.Precision.HIGHEST)

def affine_norm(values_in, gain_vec, shift_vec):
    center = values_in - lax.optimization_barrier(jnp.mean(values_in, axis=1, keepdims=True))
    spread = lax.optimization_barrier(jnp.mean(center * center, axis=1, keepdims=True))
    return center * lax.rsqrt(spread + epsilon) * gain_vec + shift_vec

def path_rows(tree_ids, segment_ids, path_table):
    seg_count = path_table.shape[1]
    flat_table = path_table.reshape(-1, 3)
    lookup = tree_ids * seg_count + segment_ids
    onehot = (lookup[:, None] == jnp.arange(flat_table.shape[0], dtype=jnp.int32)[None, :]).astype(jnp.int32)
    return lax.optimization_barrier(jnp.sum(onehot[:, :, None] * flat_table[None, :, :], axis=1))

def visible_mask(tree_ids, segment_ids, path_table, row_start, row_count):
    paths = path_rows(tree_ids, segment_ids, path_table)
    query_tree = lax.dynamic_slice_in_dim(tree_ids, row_start, row_count, 0)
    query_path = lax.dynamic_slice_in_dim(paths, row_start, row_count, 0)
    query_pos = row_start + jnp.arange(row_count, dtype=jnp.int32)
    key_pos = jnp.arange(tree_ids.shape[0], dtype=jnp.int32)
    same_tree = query_tree[:, None] == tree_ids[None, :]
    earlier = key_pos[None, :] <= query_pos[:, None]
    on_path = (segment_ids[None, :] == query_path[:, 0:1]) | (segment_ids[None, :] == query_path[:, 1:2]) | (segment_ids[None, :] == query_path[:, 2:3])
    return same_tree & earlier & on_path

def attend(queries, key_rows, value_rows, visible):
    token_count = queries.shape[0]
    scale = HEAD ** (-0.5)

    def split_heads(block):
        return block.reshape(token_count, HEADS, HEAD).transpose(1, 0, 2)

    def one_head(head_args):
        query_head, key_head, value_head = head_args
        scores = low_back(product(query_head, key_head.T) * scale)
        scores = jnp.where(visible, scores, far_below)
        probs = low(jax.nn.softmax(scores, axis=1))
        return product(probs, value_head)
    mixed = lax.map(jax.checkpoint(one_head), (split_heads(queries), split_heads(key_rows), split_heads(value_rows)))
    return mixed.transpose(1, 0, 2).reshape(token_count, D)

def layer(inputs, first_values, params, visible):
    gain1, shift1, query_w, key_w, value_w, out_w, gain2, shift2, inner_w, down_w = params
    normed1 = low(affine_norm(inputs, gain1, shift1))
    queries = low(low_back(product(normed1, query_w)))
    key_rows = low(low_back(product(normed1, key_w)))
    fresh = low(low_back(product(normed1, value_w)))
    value_rows = jnp.concatenate([fresh, first_values], axis=1)
    mixed = low(low_back(attend(queries, key_rows, value_rows, visible)))
    resid = inputs + low_back(product(mixed, out_w))
    normed2 = low(affine_norm(resid, gain2, shift2))
    hidden = low(jax.nn.gelu(low_back(product(normed2, inner_w)), approximate=True))
    return resid + product(hidden, down_w)

def reference(inputs, first_values, cotangent, tree_ids, segment_ids, path_table, attn_gain, attn_shift, w_query, w_key, w_value, w_out, mlp_gain, mlp_shift, w_in, w_down):
    params = tuple((p.astype(jnp.float32) for p in (attn_gain, attn_shift, w_query, w_key, w_value, w_out, mlp_gain, mlp_shift, w_in, w_down)))
    group_data = (inputs.astype(jnp.float32).reshape(N_REP, -1, D), first_values.astype(jnp.float32).reshape(N_REP, -1, D // 2), cotangent.astype(jnp.float32).reshape(N_REP, -1, D), tree_ids.reshape(N_REP, -1), segment_ids.reshape(N_REP, -1), path_table.reshape(N_REP, -1, SEGS, 3))

    def group_step(totals, group_item):
        group_in, group_first, group_cot, group_trees, group_segs, group_table = group_item
        visible = visible_mask(group_trees, group_segs, group_table, 0, group_trees.shape[0])

        def forward(layer_in, first_in, *layer_params):
            return layer(layer_in, first_in, layer_params, visible)
        result, pullback = jax.vjp(forward, group_in, group_first, *params)
        grad_list = pullback(group_cot)
        totals = tuple((a + b for a, b in zip(totals, grad_list[2:])))
        return (totals, (result.astype(jnp.bfloat16), grad_list[0], grad_list[1]))
    start_totals = tuple((jnp.zeros_like(p) for p in params))
    totals, (result, input_grad, first_grad) = lax.scan(group_step, start_totals, group_data)
    return (result.reshape(-1, D), input_grad.reshape(-1, D), first_grad.reshape(-1, D // 2), totals[0], totals[1], totals[2], totals[3], totals[4], totals[5], totals[6], totals[7], totals[8], totals[9])
```

```python
import functools

import jax
import jax.numpy as jnp
from jax import lax
from jax.experimental import pallas as pl
from jax.experimental.pallas import tpu as pltpu
from jax.sharding import PartitionSpec as P

MESH = pl.DeviceIdType.MESH

class Place:
    def __init__(self, fsdp):
        self.fsdp = fsdp
        r = lax.axis_index("rep")
        self.f = lax.axis_index("fsdp")
        self.k = lax.rem(r, 2)
        self.x = lax.rem(r // 2, 2)
        self.y = r // 4
        def rid(y, x, k): return (y * 2 + x) * 2 + k
        self.core = (rid(self.y, self.x, 1 - self.k), self.f)
        self.xn = (rid(self.y, 1 - self.x, self.k), self.f)
        self.yn = (rid(1 - self.y, self.x, self.k), self.f)
        self.r = r
        self.others = [lax.rem(self.f + j, fsdp) for j in range(1, fsdp)]
    def zdev(self, fo): return (self.r, fo)
    def barrier(self):
        bar = pltpu.get_barrier_semaphore()
        devs = [self.core, self.xn, self.yn] + [self.zdev(o) for o in self.others]
        for d in devs:
            pl.semaphore_signal(bar, inc=1, device_id=d, device_id_type=MESH)
        pl.semaphore_wait(bar, len(devs))

def drain(view, sem):
    pltpu.make_async_copy(view, view, sem).wait()

class Gather:
    def __init__(self, pc, buf, send, recv, xfirst):
        self.pc, self.buf, self.s, self.r, self.xf = pc, buf, send, recv, xfirst
        self.H = buf.shape[-1] // 2
        self.cols = pl.ds(pl.multiple_of(pc.k * self.H, 128), self.H)
    def push(self, view, stage, dev):
        pltpu.make_async_remote_copy(src_ref=view, dst_ref=view, send_sem=self.s.at[stage], recv_sem=self.r.at[stage], device_id=dev, device_id_type=MESH).start()
    def z_start(self):
        pc = self.pc
        v = self.buf.at[pc.f, pc.y, pc.x, :, self.cols]
        for o in pc.others: self.push(v, 0, pc.zdev(o))
    def three(self): return self.buf.at[pl.ds(0, self.pc.fsdp - 1), 0, 0, :, self.cols]
    def z_wait(self): drain(self.three(), self.r.at[0])
    def a_start(self):
        pc = self.pc
        for o in pc.others:
            v = self.buf.at[o, pc.y, pc.x, :, self.cols]
            self.push(v, 1, pc.xn); self.push(v, 2, pc.yn)
    def a_wait(self):
        drain(self.three(), self.r.at[1]); drain(self.three(), self.r.at[2])
    def b_start(self):
        pc = self.pc
        for o in pc.others:
            if self.xf: self.push(self.buf.at[o, 1 - pc.y, pc.x, :, self.cols], 3, pc.xn)
            else: self.push(self.buf.at[o, pc.y, 1 - pc.x, :, self.cols], 3, pc.yn)
    def b_wait(self): drain(self.three(), self.r.at[3])
    def c_start(self):
        pc = self.pc
        for o in pc.others: self.push(self.buf.at[o, :, :, :, self.cols], 4, pc.core)
    def big(self): return self.buf.at[pl.ds(0, self.pc.fsdp - 1), :, :, :, self.cols]
    def c_wait(self): drain(self.big(), self.r.at[4])
    def finish(self):
        for st in range(4): drain(self.three(), self.s.at[st])
        drain(self.big(), self.s.at[4])

def run_pipeline(items, stages):
    n, d = len(items), len(stages)
    for t in range(n + d - 1):
        for s in range(d):
            i = t - s
            if 0 <= i < n: stages[s](items[i])

GST = [lambda g: (g.z_wait(), g.a_start()), lambda g: (g.a_wait(), g.b_start()), lambda g: (g.b_wait(), g.c_start()), lambda g: g.c_wait()]

def gather_kernel(fsdp, n_ff, qkv, wo, win, wdn, vec, oqkv, oo, oin, odn, ovec, lsem, ssem, rsem):
    pc = Place(fsdp)
    f = pc.f
    loc = []
    def local(src, dst):
        c = pltpu.make_async_copy(src, dst, lsem.at[len(loc)]); c.start(); loc.append(c)
    for j in range(2): local(qkv.at[:, :, :, pl.ds(j * 1024, 1024)], oqkv.at[j, f])
    local(wo, oo.at[f])
    W = win.shape[-1] // fsdp
    for c in range(n_ff):
        for g in range(fsdp): local(win.at[:, :, :, pl.ds(g * W + c * 128, 128)], oin.at[c, f, :, :, :, pl.ds(g * 128, 128)])
        local(wdn.at[c], odn.at[c, f])
    local(vec, ovec.at[f])
    pc.barrier()
    items, lc = [], []
    def item(buf, xf, locs):
        i = len(items)
        items.append(Gather(pc, buf, ssem.at[i], rsem.at[i], xf)); lc.append(locs)
    item(oqkv.at[0], True, loc[0:1]); item(oqkv.at[1], False, loc[1:2]); item(oo, True, loc[2:3])
    p = 3
    for c in range(n_ff):
        item(oin.at[c], True, loc[p:p + fsdp]); p += fsdp
        item(odn.at[c], False, loc[p:p + 1]); p += 1
    loc[p].wait()
    nv = len(items)
    for o in pc.others:
        pltpu.make_async_remote_copy(src_ref=ovec.at[f], dst_ref=ovec.at[f], send_sem=ssem.at[nv, 0], recv_sem=rsem.at[nv, 0], device_id=pc.zdev(o), device_id_type=MESH).start()
    for it, l in zip(items, lc):
        for c in l: c.wait()
        it.z_start()
    run_pipeline(items, GST)
    v3 = ovec.at[pl.ds(0, fsdp - 1)]
    drain(v3, rsem.at[nv, 0]); drain(v3, ssem.at[nv, 0])
    for it in items: it.finish()

def gather_call(fsdp, qkv, wo, win, wdn, vec):
    d = qkv.shape[0]; m = d // 4
    n_ff = wdn.shape[0] // 128
    sh = lambda a: a.reshape(2, 2, m, a.shape[1])
    bf = jnp.bfloat16
    outs = (jax.ShapeDtypeStruct((2, fsdp, 2, 2, m, 1024), bf), jax.ShapeDtypeStruct((fsdp, 2, 2, m, wo.shape[1]), bf),
            jax.ShapeDtypeStruct((n_ff, fsdp, 2, 2, m, fsdp * 128), bf), jax.ShapeDtypeStruct((n_ff, fsdp, 2, 2, 32, wdn.shape[1]), bf),
            jax.ShapeDtypeStruct((fsdp, 8, vec.shape[1]), jnp.float32))
    nit = 3 + 2 * n_ff
    nloc = 4 + n_ff * (fsdp + 1)
    any_ = pl.BlockSpec(memory_space=pl.ANY)
    return pl.pallas_call(functools.partial(gather_kernel, fsdp, n_ff), out_shape=outs, in_specs=[any_] * 5, out_specs=[any_] * 5,
        scratch_shapes=[pltpu.SemaphoreType.DMA((nloc,)), pltpu.SemaphoreType.DMA((nit + 1, 5)), pltpu.SemaphoreType.DMA((nit + 1, 5))],
        compiler_params=pltpu.CompilerParams(collective_id=1, has_side_effects=True))(
        sh(qkv), sh(wo), sh(win), wdn.reshape(n_ff, 2, 2, 32, -1), vec)

class Reduce:
    def __init__(self, pc, buf, r1, r2, r3, r4, res, send, recv, xfirst):
        self.pc, self.buf, self.r1, self.r2, self.r3, self.r4, self.res = pc, buf, r1, r2, r3, r4, res
        self.s, self.r, self.xf = send, recv, xfirst
        self.H = H = buf.shape[-1] // 2
        self.cols = pl.ds(pl.multiple_of(pc.k * H, 128), H)
        self.ocols = pl.ds(pl.multiple_of((1 - pc.k) * H, 128), H)
        self.F = buf.shape[0]
    def send(self, src, dst, stage, dev):
        pltpu.make_async_remote_copy(src_ref=src, dst_ref=dst, send_sem=self.s.at[stage], recv_sem=self.r.at[stage], device_id=dev, device_id_type=MESH).start()
    def p1(self):
        self.send(self.buf.at[:, :, :, :, self.ocols], self.r1, 0, self.pc.core)
    def p2(self):
        pc = self.pc
        drain(self.r1, self.r.at[0])
        @pl.loop(0, self.F * 4)
        def _(i):
            a, b, c = i // 4, lax.rem(i // 2, 2), lax.rem(i, 2)
            self.r1[a, b, c] = (self.r1[a, b, c].astype(jnp.float32) + self.buf[a, b, c, :, self.cols].astype(jnp.float32)).astype(jnp.bfloat16)
        if self.xf: self.send(self.r1.at[:, :, 1 - pc.x], self.r2, 1, pc.xn)
        else: self.send(self.r1.at[:, 1 - pc.y], self.r2, 1, pc.yn)
    def p3(self):
        pc = self.pc
        drain(self.r2, self.r.at[1])
        @pl.loop(0, self.F * 2)
        def _(i):
            a, b = i // 2, lax.rem(i, 2)
            mine = self.r1[a, b, pc.x] if self.xf else self.r1[a, pc.y, b]
            self.r2[a, b] = (self.r2[a, b].astype(jnp.float32) + mine.astype(jnp.float32)).astype(jnp.bfloat16)
        if self.xf: self.send(self.r2.at[:, 1 - pc.y], self.r3, 2, pc.yn)
        else: self.send(self.r2.at[:, 1 - pc.x], self.r3, 2, pc.xn)
    def p4(self):
        pc = self.pc
        drain(self.r3, self.r.at[2])
        q = pc.y if self.xf else pc.x
        @pl.loop(0, self.F)
        def _(a):
            self.r3[a] = (self.r3[a].astype(jnp.float32) + self.r2[a, q].astype(jnp.float32)).astype(jnp.bfloat16)
        for o in pc.others: self.send(self.r3.at[o], self.r4.at[pc.f], 3, pc.zdev(o))
    def p5(self):
        pc = self.pc
        drain(self.r4.at[pl.ds(0, self.F - 1)], self.r.at[3])
        tot = self.r3[pc.f].astype(jnp.float32)
        for o in pc.others: tot = tot + self.r4[o].astype(jnp.float32)
        self.res[pc.y, pc.x, :, self.cols] = tot.astype(jnp.bfloat16)
        v = self.res.at[pc.y, pc.x, :, self.cols]
        self.send(v, v, 4, pc.xn); self.send(v, v, 5, pc.yn)
    def p6(self):
        pc = self.pc
        v = self.res.at[0, 0, :, self.cols]
        drain(v, self.r.at[4]); drain(v, self.r.at[5])
        if self.xf:
            v = self.res.at[1 - pc.y, pc.x, :, self.cols]; self.send(v, v, 6, pc.xn)
        else:
            v = self.res.at[pc.y, 1 - pc.x, :, self.cols]; self.send(v, v, 6, pc.yn)
    def p7(self):
        drain(self.res.at[0, 0, :, self.cols], self.r.at[6])
        v = self.res.at[:, :, :, self.cols]
        self.send(v, v, 7, self.pc.core)
    def p8(self):
        drain(self.res.at[:, :, :, self.cols], self.r.at[7])
    def finish(self):
        drain(self.r1, self.s.at[0]); drain(self.r2, self.s.at[1]); drain(self.r3, self.s.at[2])
        drain(self.r4.at[pl.ds(0, self.F - 1)], self.s.at[3])
        v = self.res.at[0, 0, :, self.cols]
        for i in (4, 5, 6): drain(v, self.s.at[i])
        drain(self.res.at[:, :, :, self.cols], self.s.at[7])
    STAGES = None

Reduce.STAGES = [Reduce.p1, Reduce.p2, Reduce.p3, Reduce.p4, Reduce.p5, Reduce.p6, Reduce.p7, Reduce.p8]

def red_scratch(shape):
    F, _, _, m, C = shape; H = C // 2; bf = jnp.bfloat16
    return [pltpu.VMEM((F, 2, 2, m, H), bf), pltpu.VMEM((F, 2, m, H), bf), pltpu.VMEM((F, m, H), bf), pltpu.VMEM((F, m, H), bf)]

def reduce_kernel(fsdp, n_ff, gqkv, go, gin, gdn, gvec, oq, oo, oi, od, ov, *scr):
    pc = Place(fsdp)
    bq, bo, bi, bd, rq, ro, ri, rd, vr, vz, lsem, ssem, rsem, vs, vrs = scr
    srcs = [(gqkv.at[j], bq.at[j]) for j in range(2)] + [(go, bo)]
    for c in range(n_ff): srcs += [(gin.at[c], bi.at[c]), (gdn.at[c], bd.at[c])]
    cps = []
    for i, (a, b) in enumerate(srcs):
        c = pltpu.make_async_copy(a, b, lsem.at[i]); c.start(); cps.append(c)
    pc.barrier()
    def ex(src, dst, i, dev):
        c = pltpu.make_async_remote_copy(src_ref=src, dst_ref=dst, send_sem=vs.at[i], recv_sem=vrs.at[i], device_id=dev, device_id_type=MESH); c.start(); return c
    items = []
    def item(buf, r, res, xf):
        i = len(items)
        items.append(Reduce(pc, buf, *r, res, ssem.at[i], rsem.at[i], xf))
    item(bq.at[0], [a.at[0] for a in rq], oq.at[0], True); item(bq.at[1], [a.at[1] for a in rq], oq.at[1], False); item(bo, ro, oo, True)
    for c in range(n_ff):
        item(bi.at[c], [a.at[c] for a in ri], oi.at[c], True); item(bd.at[c], [a.at[c] for a in rd], od.at[c], False)
    order = list(range(3, len(items))) + [2, 0, 1]
    def first(i):
        cps[i].wait(); items[i].p1()
    run_pipeline(order, [first] + [(lambda i, p=p: p(items[i])) for p in Reduce.STAGES[1:]])
    cur = gvec
    for i, dev in enumerate((pc.core, pc.xn, pc.yn)):
        c = ex(cur, vr.at[i], i, dev); c.wait()
        vr[i] = vr[i] + cur[...]
        cur = vr.at[i]
    for o in pc.others: ex(cur, vz.at[pc.f], 3, pc.zdev(o))
    v3 = vz.at[pl.ds(0, fsdp - 1)]
    drain(v3, vrs.at[3]); drain(v3, vs.at[3])
    vz[pc.f] = cur[...]
    tot = vz[0]
    for j in range(1, fsdp): tot = tot + vz[j]
    ov[...] = tot
    for it in items: it.finish()

def reduce_call(fsdp, gqkv, go, gin, gdn, gvec):
    bf = jnp.bfloat16
    n_ff = gin.shape[0]
    def stack(shape, lead): return [pltpu.VMEM((lead,) + tuple(s.inner_aval.shape if hasattr(s, "inner_aval") else s.shape), bf) for s in red_scratch(shape)]
    outs = tuple(jax.ShapeDtypeStruct(s, bf) for s in (gqkv.shape[:1] + gqkv.shape[2:], go.shape[1:], gin.shape[:1] + gin.shape[2:], gdn.shape[:1] + gdn.shape[2:])) + (jax.ShapeDtypeStruct(gvec.shape, jnp.float32),)
    nit = 3 + 2 * n_ff
    any_ = pl.BlockSpec(memory_space=pl.ANY); vm = pl.BlockSpec(memory_space=pltpu.VMEM)
    scr = [pltpu.VMEM(a.shape, bf) for a in (gqkv, go, gin, gdn)]
    flat = scr + []
    groups = [stack(gqkv.shape[1:], 2), red_scratch(go.shape), stack(gin.shape[1:], n_ff), stack(gdn.shape[1:], n_ff)]
    D = pltpu.SemaphoreType.DMA
    tail = [pltpu.VMEM((3,) + gvec.shape, jnp.float32), pltpu.VMEM((fsdp,) + gvec.shape, jnp.float32), D((nit,)), D((nit, 8)), D((nit, 8)), D((4,)), D((4,))]
    def body(a, b, c, d, e, o1, o2, o3, o4, o5, *s):
        base, rest = list(s[:4]), list(s[4:])
        g = [rest[i * 4:(i + 1) * 4] for i in range(4)]
        reduce_kernel(fsdp, n_ff, a, b, c, d, e, o1, o2, o3, o4, o5, *base, *g, *rest[16:])
    return pl.pallas_call(body, out_shape=outs, in_specs=[any_] * 4 + [vm], out_specs=[vm] * 5,
        scratch_shapes=flat + [x for g in groups for x in g] + tail,
        compiler_params=pltpu.CompilerParams(collective_id=2, has_side_effects=True, vmem_limit_bytes=56 << 20))(gqkv, go, gin, gdn, gvec)


HEAD = 64
TREE_LEN = 1024


epsilon = 1e-05
far_below = -1e30


def shifted(block, axis, distance):
    devices = range(lax.axis_size(axis))
    route = [(i - distance, i) for i in devices if i - distance in devices]
    return lax.ppermute(block, axis, route)


def affine_norm(values_in, gain_vec, shift_vec):
    center = values_in - jnp.mean(values_in, axis=1, keepdims=True)
    spread = jnp.mean(center * center, axis=1, keepdims=True)
    return center * lax.rsqrt(spread + epsilon) * gain_vec + shift_vec


def gelu_tanh(values_in):
    return jax.nn.gelu(values_in, approximate=True)


def path_rows(tree_ids, segment_ids, path_table):
    seg_count = path_table.shape[1]
    flat_table = path_table.reshape(-1, 3)
    lookup = tree_ids * seg_count + segment_ids
    onehot = (lookup[:, None] == jnp.arange(flat_table.shape[0], dtype=jnp.int32)[None, :]).astype(
        jnp.int32
    )
    return jnp.sum(onehot[:, :, None] * flat_table[None, :, :], axis=1)


def visible_mask(tree_ids, segment_ids, path_table, row_start, row_count, key_start, window_len):
    paths = path_rows(tree_ids, segment_ids, path_table)
    query_tree = lax.dynamic_slice_in_dim(tree_ids, row_start, row_count, 0)
    query_path = lax.dynamic_slice_in_dim(paths, row_start, row_count, 0)
    query_pos = row_start + jnp.arange(row_count, dtype=jnp.int32)
    key_pos = key_start + jnp.arange(window_len, dtype=jnp.int32)
    inside = key_pos >= 0
    safe_pos = jnp.clip(key_pos, 0, tree_ids.shape[0] - 1)
    key_tree = jnp.take(tree_ids, safe_pos)
    key_seg = jnp.take(segment_ids, safe_pos)
    same_tree = query_tree[:, None] == key_tree[None, :]
    earlier = key_pos[None, :] <= query_pos[:, None]
    on_path = (
        (key_seg[None, :] == query_path[:, 0:1])
        | (key_seg[None, :] == query_path[:, 1:2])
        | (key_seg[None, :] == query_path[:, 2:3])
    )
    return inside[None, :] & same_tree & earlier & on_path


def pair_slice(block, pair_index):
    return lax.dynamic_slice_in_dim(block, pair_index * 2 * HEAD, 2 * HEAD, 1).reshape(
        block.shape[0], 2, HEAD
    )


def pair_scores(query_pair, key_pair, visible):
    scores = jnp.einsum(
        "qhd,khd->hqk", query_pair, key_pair, preferred_element_type=jnp.float32
    ) * HEAD ** (-0.5)
    return jnp.where(visible[None, :, :], scores, far_below)


def reorder_rows(grad_block, fsdp_count, rep_count):
    return grad_block.reshape(fsdp_count, rep_count, -1).transpose(1, 0, 2).reshape(-1)


def fetch_earlier(both_rows, distance):
    return shifted(both_rows, "fsdp", distance)


def return_earlier(grad_rows, distance):
    return shifted(grad_rows.astype(jnp.bfloat16), "fsdp", -distance).astype(grad_rows.dtype)


def packed_qkv(query, key, value):
    h, pad = query.shape[1] * 2 // 3, jnp.zeros_like(value[:, : value.shape[1] // 3])
    n = value.shape[1] * 2 // 3
    return jnp.concatenate([query[:, :h], key[:, :h], query[:, h:], value[:, :n], key[:, h:], value[:, n:], pad], axis=1)


def unpacked_qkv(first, second):
    h = first.shape[-1] // 2
    q = h // 2
    return (
        jnp.concatenate([first[..., :h], second[..., :q]], axis=-1),
        jnp.concatenate([first[..., h:], second[..., h : h + q]], axis=-1),
        jnp.concatenate([second[..., q:h], second[..., h + q : h + q + q // 2]], axis=-1),
    )


def gathered(fsdp, gain1, shift1, gain2, shift2, w_query, w_key, w_value, w_out, w_in, w_down):
    rows, width = w_query.shape
    vec = jnp.stack([gain1, shift1, gain2, shift2]).astype(jnp.float32)
    vec = jnp.zeros((8, width), jnp.float32).at[:4, :rows].set(vec)
    vec = jnp.roll(vec, lax.axis_index("fsdp") * rows, axis=1)
    oq, oo, oi, od, ov = gather_call(fsdp, packed_qkv(w_query, w_key, w_value), w_out, w_in, w_down, vec)
    vecs = jnp.sum(ov, axis=0).astype(jnp.bfloat16)
    qkv = oq.reshape(2, width, -1)
    query_w, key_w, value_w = unpacked_qkv(qkv[0], qkv[1])
    n_ff = oi.shape[0]
    inner = oi.reshape(n_ff, width, fsdp, 128).transpose(1, 2, 0, 3).reshape(width, -1)
    down = od.reshape(n_ff, fsdp, 128, width).transpose(1, 0, 2, 3).reshape(-1, width)
    return (*vecs[:4], query_w, key_w, value_w, oo.reshape(width, width), inner, down)


def reduced(fsdp, g1, b1, g2, b2, dq, dk, dv, do, din, ddn):
    width = dq.shape[0]
    rows = width // fsdp
    n_ff = din.shape[1] // (fsdp * 128)
    bf = jnp.bfloat16
    vec = jnp.zeros((8, width), jnp.float32).at[:4].set(jnp.stack([g1, b1, g2, b2]))
    qkv = packed_qkv(dq, dk, dv).astype(bf)
    qkv = qkv.reshape(width, 2, -1).transpose(1, 0, 2).reshape(2, fsdp, 2, 2, rows // 4, -1)
    gin = din.astype(bf).reshape(width, fsdp, n_ff, 128).transpose(2, 0, 1, 3).reshape(n_ff, fsdp, 2, 2, rows // 4, -1)
    gdn = ddn.astype(bf).reshape(fsdp, n_ff, 128, width).transpose(1, 0, 2, 3).reshape(n_ff, fsdp, 2, 2, 32, width)
    rq, ro, ri, rd, rv = reduce_call(fsdp, qkv, do.astype(bf).reshape(fsdp, 2, 2, rows // 4, width), gin, gdn, vec)
    rv = lax.dynamic_slice_in_dim(rv, lax.axis_index("fsdp") * rows, rows, 1)
    f32 = jnp.float32
    rq = rq.reshape(2, rows, -1)
    q, k, v = unpacked_qkv(rq[0], rq[1])
    ri = ri.reshape(n_ff, rows, fsdp, 128).transpose(1, 2, 0, 3).reshape(rows, -1)
    return (
        *rv[:4], q.astype(f32), k.astype(f32), v.astype(f32), ro.reshape(rows, width).astype(f32),
        ri.astype(f32), rd.reshape(-1, width).astype(f32),
    )


def on_device(
    inputs,
    first_values,
    cotangent,
    tree_ids,
    segment_ids,
    path_table,
    attn_gain,
    attn_shift,
    w_query,
    w_key,
    w_value,
    w_out,
    mlp_gain,
    mlp_shift,
    w_in,
    w_down,
):
    row_count, feat_width = inputs.shape
    scale = HEAD ** (-0.5)
    fsdp_count = lax.axis_size("fsdp")
    reach = 0
    for device_pos in range(fsdp_count):
        offset = device_pos * row_count % TREE_LEN
        reach = max(reach, (offset + row_count - 1) // row_count)
    window_len = (reach + 1) * row_count
    row_start = lax.axis_index("fsdp") * row_count
    rep_count = lax.axis_size("rep")
    fast = rep_count == 8 and attn_gain.shape[0] % 64 == 0
    if fast:
        gain1, shift1, gain2, shift2, query_w, key_w, value_w, out_w, inner_w, down_w = gathered(
            fsdp_count, attn_gain, attn_shift, mlp_gain, mlp_shift, w_query, w_key, w_value, w_out, w_in, w_down
        )
    else:
        gain1, shift1, query_w, key_w, value_w, out_w, gain2, shift2, inner_w, down_w = (
            lax.all_gather(v, "fsdp", axis=0, tiled=True)
            for v in (attn_gain, attn_shift, w_query, w_key, w_value, w_out, mlp_gain, mlp_shift, w_in, w_down)
        )
    resid_in = inputs.astype(jnp.float32)
    normed1_f, norm1_back = jax.vjp(
        affine_norm, resid_in, gain1.astype(jnp.float32), shift1.astype(jnp.float32)
    )
    normed1 = normed1_f.astype(jnp.bfloat16)
    queries = jnp.dot(normed1, query_w, preferred_element_type=jnp.float32).astype(jnp.bfloat16)
    key_rows = jnp.dot(normed1, key_w, preferred_element_type=jnp.float32).astype(jnp.bfloat16)
    fresh = jnp.dot(normed1, value_w, preferred_element_type=jnp.float32).astype(jnp.bfloat16)
    value_rows = jnp.concatenate([fresh, first_values], axis=1)
    both_rows = jnp.concatenate([key_rows, value_rows], axis=1)
    near_parts = []
    for distance in range(reach, 0, -1):
        near_parts.append(fetch_earlier(both_rows, distance))
    near_parts.append(both_rows)
    window_rows = jnp.concatenate(near_parts, axis=0)
    win_keys = window_rows[:, :feat_width]
    win_values = window_rows[:, feat_width:]
    key_start = row_start - reach * row_count
    visible = visible_mask(
        tree_ids, segment_ids, path_table, row_start, row_count, key_start, window_len
    )
    head_count = feat_width // HEAD
    pair_count = head_count // 2

    def forward_pair(pair_index, carry):
        mixed_acc, lse_acc = carry
        query_pair = pair_slice(queries, pair_index)
        key_pair = pair_slice(win_keys, pair_index)
        value_pair = pair_slice(win_values, pair_index)
        scores = pair_scores(query_pair, key_pair, visible)
        row_max = jnp.max(scores, axis=2, keepdims=True)
        expo = jnp.exp(scores - row_max)
        denom_sum = jnp.sum(expo, axis=2, keepdims=True)
        probs = expo / denom_sum
        lse_pair = (row_max + jnp.log(denom_sum))[:, :, 0]
        weights_b = probs.astype(jnp.bfloat16)
        pair_out = jnp.einsum(
            "hqk,khd->qhd", weights_b, value_pair, preferred_element_type=jnp.float32
        )
        pair_out = pair_out.reshape(row_count, 2 * HEAD).astype(jnp.bfloat16)
        mixed_acc = lax.dynamic_update_slice_in_dim(mixed_acc, pair_out, pair_index * 2 * HEAD, 1)
        lse_acc = lax.dynamic_update_slice_in_dim(lse_acc, lse_pair, pair_index * 2, 0)
        return (mixed_acc, lse_acc)

    mixed, lse_all = lax.fori_loop(
        0,
        pair_count,
        forward_pair,
        (
            jnp.zeros((row_count, feat_width), jnp.bfloat16),
            jnp.zeros((head_count, row_count), jnp.float32),
        ),
    )
    resid = resid_in + jnp.dot(mixed, out_w, preferred_element_type=jnp.float32)
    normed2_f, norm2_back = jax.vjp(
        affine_norm, resid, gain2.astype(jnp.float32), shift2.astype(jnp.float32)
    )
    normed2 = normed2_f.astype(jnp.bfloat16)
    act = jnp.dot(normed2, inner_w, preferred_element_type=jnp.float32)
    hidden_f, gelu_back = jax.vjp(gelu_tanh, act)
    hidden = hidden_f.astype(jnp.bfloat16)
    outputs = (resid + jnp.dot(hidden, down_w, preferred_element_type=jnp.float32)).astype(
        jnp.bfloat16
    )
    grad_hidden = jnp.dot(cotangent, down_w.T, preferred_element_type=jnp.float32)
    down_grad = jnp.dot(hidden.T, cotangent, preferred_element_type=jnp.float32)
    grad_act = gelu_back(grad_hidden)[0].astype(jnp.bfloat16)
    inner_grad = jnp.dot(normed2.T, grad_act, preferred_element_type=jnp.float32)
    grad_normed2 = jnp.dot(grad_act, inner_w.T, preferred_element_type=jnp.float32)
    grad_ln2, gain2_grad, shift2_grad = norm2_back(grad_normed2)
    grad_resid = cotangent.astype(jnp.float32) + grad_ln2
    grad_branch = grad_resid.astype(jnp.bfloat16)
    out_grad = jnp.dot(mixed.T, grad_branch, preferred_element_type=jnp.float32)
    grad_mixed = jnp.dot(grad_branch, out_w.T, preferred_element_type=jnp.float32).astype(
        jnp.bfloat16
    )

    def backward_pair(pair_index, carry):
        query_acc, key_acc, value_acc = carry
        query_pair = pair_slice(queries, pair_index)
        key_pair = pair_slice(win_keys, pair_index)
        value_pair = pair_slice(win_values, pair_index)
        grad_pair = pair_slice(grad_mixed, pair_index)
        scores = pair_scores(query_pair, key_pair, visible)
        lse_pair = lax.dynamic_slice_in_dim(lse_all, pair_index * 2, 2, 0)
        probs = jnp.exp(scores - lse_pair[:, :, None])
        weights_b = probs.astype(jnp.bfloat16)
        grad_weights = jnp.einsum(
            "qhd,khd->hqk", grad_pair, value_pair, preferred_element_type=jnp.float32
        )
        inner_sum = jnp.sum(probs * grad_weights, axis=2, keepdims=True)
        grad_scores = (probs * (grad_weights - inner_sum)).astype(jnp.bfloat16)
        query_part = (
            jnp.einsum("hqk,khd->qhd", grad_scores, key_pair, preferred_element_type=jnp.float32)
            * scale
        )
        key_part = (
            jnp.einsum("hqk,qhd->khd", grad_scores, query_pair, preferred_element_type=jnp.float32)
            * scale
        )
        value_part = jnp.einsum(
            "hqk,qhd->khd", weights_b, grad_pair, preferred_element_type=jnp.float32
        )
        query_acc = lax.dynamic_update_slice_in_dim(
            query_acc, query_part.reshape(row_count, 2 * HEAD), pair_index * 2 * HEAD, 1
        )
        key_acc = lax.dynamic_update_slice_in_dim(
            key_acc, key_part.reshape(window_len, 2 * HEAD), pair_index * 2 * HEAD, 1
        )
        value_acc = lax.dynamic_update_slice_in_dim(
            value_acc, value_part.reshape(window_len, 2 * HEAD), pair_index * 2 * HEAD, 1
        )
        return (query_acc, key_acc, value_acc)

    query_full, key_win, value_win = lax.fori_loop(
        0,
        pair_count,
        backward_pair,
        (
            jnp.zeros((row_count, feat_width), jnp.float32),
            jnp.zeros((window_len, feat_width), jnp.float32),
            jnp.zeros((window_len, feat_width), jnp.float32),
        ),
    )
    grad_window = jnp.concatenate([key_win, value_win], axis=1).reshape(
        reach + 1, row_count, 2 * feat_width
    )
    own_grad = grad_window[reach]
    for distance in range(1, reach + 1):
        own_grad = own_grad + return_earlier(grad_window[reach - distance], distance)
    key_total = own_grad[:, :feat_width]
    value_total = own_grad[:, feat_width:]
    half_width = feat_width // 2
    grad_queries = query_full.astype(jnp.bfloat16)
    grad_keys = key_total.astype(jnp.bfloat16)
    grad_fresh = value_total[:, :half_width].astype(jnp.bfloat16)
    first_grad = value_total[:, half_width:]
    query_grad = jnp.dot(normed1.T, grad_queries, preferred_element_type=jnp.float32)
    key_grad = jnp.dot(normed1.T, grad_keys, preferred_element_type=jnp.float32)
    value_grad = jnp.dot(normed1.T, grad_fresh, preferred_element_type=jnp.float32)
    grad_normed1 = (
        jnp.dot(grad_queries, query_w.T, preferred_element_type=jnp.float32)
        + jnp.dot(grad_keys, key_w.T, preferred_element_type=jnp.float32)
        + jnp.dot(grad_fresh, value_w.T, preferred_element_type=jnp.float32)
    )
    grad_ln1, gain1_grad, shift1_grad = norm1_back(grad_normed1)
    input_grad = grad_resid + grad_ln1
    if fast:
        g1, b1, g2, b2, dq, dk, dv, do, din, ddn = reduced(
            fsdp_count, gain1_grad, shift1_grad, gain2_grad, shift2_grad, query_grad, key_grad, value_grad, out_grad, inner_grad, down_grad
        )
        return (outputs, input_grad, first_grad, g1, b1, dq, dk, dv, do, g2, b2, din, ddn)
    norm_grads = jnp.stack([gain1_grad, shift1_grad, gain2_grad, shift2_grad], axis=1)
    partial_list = (norm_grads, query_grad, key_grad, value_grad, out_grad, inner_grad, down_grad)
    pieces = (
        lax.psum_scatter(
            reorder_rows(norm_grads, fsdp_count, rep_count),
            ("rep", "fsdp"),
            scatter_dimension=0,
            tiled=True,
        ),
        lax.psum_scatter(
            reorder_rows(query_grad, fsdp_count, rep_count),
            ("rep", "fsdp"),
            scatter_dimension=0,
            tiled=True,
        ),
        lax.psum_scatter(
            reorder_rows(key_grad, fsdp_count, rep_count),
            ("rep", "fsdp"),
            scatter_dimension=0,
            tiled=True,
        ),
        lax.psum_scatter(
            reorder_rows(value_grad, fsdp_count, rep_count),
            ("rep", "fsdp"),
            scatter_dimension=0,
            tiled=True,
        ),
        lax.psum_scatter(
            reorder_rows(out_grad, fsdp_count, rep_count),
            ("rep", "fsdp"),
            scatter_dimension=0,
            tiled=True,
        ),
        lax.psum_scatter(
            reorder_rows(inner_grad, fsdp_count, rep_count),
            ("rep", "fsdp"),
            scatter_dimension=0,
            tiled=True,
        ),
        lax.psum_scatter(
            reorder_rows(down_grad, fsdp_count, rep_count),
            ("rep", "fsdp"),
            scatter_dimension=0,
            tiled=True,
        ),
    )
    spread = (
        lax.all_gather(pieces[0].astype(jnp.bfloat16), "rep", axis=0, tiled=True).astype(
            jnp.float32
        ),
        lax.all_gather(pieces[1].astype(jnp.bfloat16), "rep", axis=0, tiled=True).astype(
            jnp.float32
        ),
        lax.all_gather(pieces[2].astype(jnp.bfloat16), "rep", axis=0, tiled=True).astype(
            jnp.float32
        ),
        lax.all_gather(pieces[3].astype(jnp.bfloat16), "rep", axis=0, tiled=True).astype(
            jnp.float32
        ),
        lax.all_gather(pieces[4].astype(jnp.bfloat16), "rep", axis=0, tiled=True).astype(
            jnp.float32
        ),
        lax.all_gather(pieces[5].astype(jnp.bfloat16), "rep", axis=0, tiled=True).astype(
            jnp.float32
        ),
        lax.all_gather(pieces[6].astype(jnp.bfloat16), "rep", axis=0, tiled=True).astype(
            jnp.float32
        ),
    )
    summed = tuple(
        (
            piece_sum.reshape((whole.shape[0] // fsdp_count,) + whole.shape[1:])
            for piece_sum, whole in zip(spread, partial_list)
        )
    )
    norm_shard = summed[0]
    return (
        outputs,
        input_grad,
        first_grad,
        norm_shard[:, 0],
        norm_shard[:, 1],
        summed[1],
        summed[2],
        summed[3],
        summed[4],
        norm_shard[:, 2],
        norm_shard[:, 3],
        summed[5],
        summed[6],
    )


def solution(mesh):
    placed = (
        P(("rep", "fsdp"), None),
        P(("rep", "fsdp"), None),
        P(("rep", "fsdp"), None),
        P("rep"),
        P("rep"),
        P("rep", None, None),
        P("fsdp"),
        P("fsdp"),
        P("fsdp", None),
        P("fsdp", None),
        P("fsdp", None),
        P("fsdp", None),
        P("fsdp"),
        P("fsdp"),
        P("fsdp", None),
        P("fsdp", None),
    )
    return jax.shard_map(
        on_device,
        mesh=mesh,
        in_specs=placed,
        out_specs=(
            P(("rep", "fsdp"), None),
            P(("rep", "fsdp"), None),
            P(("rep", "fsdp"), None),
            P("fsdp"),
            P("fsdp"),
            P("fsdp", None),
            P("fsdp", None),
            P("fsdp", None),
            P("fsdp", None),
            P("fsdp"),
            P("fsdp"),
            P("fsdp", None),
            P("fsdp", None),
        ),
        check_vma=False,
    )
```

```python
import functools

import jax
import jax.numpy as jnp
from jax import lax
from jax.experimental import pallas as pl
from jax.experimental.pallas import tpu as pltpu
from jax.sharding import PartitionSpec as P

MESH = pl.DeviceIdType.MESH

class Place:
    def __init__(self, fsdp):
        self.fsdp = fsdp
        r = lax.axis_index("rep")
        self.f = lax.axis_index("fsdp")
        self.k = lax.rem(r, 2)
        self.x = lax.rem(r // 2, 2)
        self.y = r // 4
        def rid(y, x, k): return (y * 2 + x) * 2 + k
        self.core = (rid(self.y, self.x, 1 - self.k), self.f)
        self.xn = (rid(self.y, 1 - self.x, self.k), self.f)
        self.yn = (rid(1 - self.y, self.x, self.k), self.f)
        self.r = r
        self.others = [lax.rem(self.f + j, fsdp) for j in range(1, fsdp)]
    def zdev(self, fo): return (self.r, fo)
    def barrier(self):
        bar = pltpu.get_barrier_semaphore()
        devs = [self.core, self.xn, self.yn] + [self.zdev(o) for o in self.others]
        for d in devs:
            pl.semaphore_signal(bar, inc=1, device_id=d, device_id_type=MESH)
        pl.semaphore_wait(bar, len(devs))

def drain(view, sem):
    pltpu.make_async_copy(view, view, sem).wait()

class Gather:
    def __init__(self, pc, buf, send, recv, xfirst):
        self.pc, self.buf, self.s, self.r, self.xf = pc, buf, send, recv, xfirst
        self.H = buf.shape[-1] // 2
        self.cols = pl.ds(pl.multiple_of(pc.k * self.H, 128), self.H)
    def push(self, view, stage, dev):
        pltpu.make_async_remote_copy(src_ref=view, dst_ref=view, send_sem=self.s.at[stage], recv_sem=self.r.at[stage], device_id=dev, device_id_type=MESH).start()
    def z_start(self):
        pc = self.pc
        v = self.buf.at[pc.f, pc.y, pc.x, :, self.cols]
        for o in pc.others: self.push(v, 0, pc.zdev(o))
    def three(self): return self.buf.at[pl.ds(0, self.pc.fsdp - 1), 0, 0, :, self.cols]
    def z_wait(self): drain(self.three(), self.r.at[0])
    def a_start(self):
        pc = self.pc
        for o in pc.others:
            v = self.buf.at[o, pc.y, pc.x, :, self.cols]
            self.push(v, 1, pc.xn); self.push(v, 2, pc.yn)
    def a_wait(self):
        drain(self.three(), self.r.at[1]); drain(self.three(), self.r.at[2])
    def b_start(self):
        pc = self.pc
        for o in pc.others:
            if self.xf: self.push(self.buf.at[o, 1 - pc.y, pc.x, :, self.cols], 3, pc.xn)
            else: self.push(self.buf.at[o, pc.y, 1 - pc.x, :, self.cols], 3, pc.yn)
    def b_wait(self): drain(self.three(), self.r.at[3])
    def c_start(self):
        pc = self.pc
        for o in pc.others: self.push(self.buf.at[o, :, :, :, self.cols], 4, pc.core)
    def big(self): return self.buf.at[pl.ds(0, self.pc.fsdp - 1), :, :, :, self.cols]
    def c_wait(self): drain(self.big(), self.r.at[4])
    def finish(self):
        for st in range(4): drain(self.three(), self.s.at[st])
        drain(self.big(), self.s.at[4])

Gather.STAGES = [
    lambda g: (g.z_wait(), g.a_start()),
    lambda g: (g.a_wait(), g.b_start()),
    lambda g: (g.b_wait(), g.c_start()),
    lambda g: (g.c_wait(), g.finish()),
]


class Reduce:
    def __init__(self, pc, buf, r1, r2, r3, r4, res, send, recv, xfirst):
        self.pc, self.buf, self.r1, self.r2, self.r3, self.r4, self.res = pc, buf, r1, r2, r3, r4, res
        self.s, self.r, self.xf = send, recv, xfirst
        self.H = H = buf.shape[-1] // 2
        self.cols = pl.ds(pl.multiple_of(pc.k * H, 128), H)
        self.ocols = pl.ds(pl.multiple_of((1 - pc.k) * H, 128), H)
        self.F = buf.shape[0]
    def send(self, src, dst, stage, dev):
        pltpu.make_async_remote_copy(src_ref=src, dst_ref=dst, send_sem=self.s.at[stage], recv_sem=self.r.at[stage], device_id=dev, device_id_type=MESH).start()
    def p1(self):
        self.send(self.buf.at[:, :, :, :, self.ocols], self.r1, 0, self.pc.core)
    def p2(self):
        pc = self.pc
        drain(self.r1, self.r.at[0])
        @pl.loop(0, self.F * 4)
        def _(i):
            a, b, c = i // 4, lax.rem(i // 2, 2), lax.rem(i, 2)
            self.r1[a, b, c] = (self.r1[a, b, c].astype(jnp.float32) + self.buf[a, b, c, :, self.cols].astype(jnp.float32)).astype(jnp.bfloat16)
        if self.xf: self.send(self.r1.at[:, :, 1 - pc.x], self.r2, 1, pc.xn)
        else: self.send(self.r1.at[:, 1 - pc.y], self.r2, 1, pc.yn)
    def p3(self):
        pc = self.pc
        drain(self.r2, self.r.at[1])
        @pl.loop(0, self.F * 2)
        def _(i):
            a, b = i // 2, lax.rem(i, 2)
            mine = self.r1[a, b, pc.x] if self.xf else self.r1[a, pc.y, b]
            self.r2[a, b] = (self.r2[a, b].astype(jnp.float32) + mine.astype(jnp.float32)).astype(jnp.bfloat16)
        if self.xf: self.send(self.r2.at[:, 1 - pc.y], self.r3, 2, pc.yn)
        else: self.send(self.r2.at[:, 1 - pc.x], self.r3, 2, pc.xn)
    def p4(self):
        pc = self.pc
        drain(self.r3, self.r.at[2])
        q = pc.y if self.xf else pc.x
        @pl.loop(0, self.F)
        def _(a):
            self.r3[a] = (self.r3[a].astype(jnp.float32) + self.r2[a, q].astype(jnp.float32)).astype(jnp.bfloat16)
        for o in pc.others: self.send(self.r3.at[o], self.r4.at[pc.f], 3, pc.zdev(o))
    def p5(self):
        pc = self.pc
        drain(self.r4.at[pl.ds(0, self.F - 1)], self.r.at[3])
        tot = self.r3[pc.f].astype(jnp.float32)
        for o in pc.others: tot = tot + self.r4[o].astype(jnp.float32)
        self.res[pc.y, pc.x, :, self.cols] = tot.astype(jnp.bfloat16)
        v = self.res.at[pc.y, pc.x, :, self.cols]
        self.send(v, v, 4, pc.xn); self.send(v, v, 5, pc.yn)
    def p6(self):
        pc = self.pc
        v = self.res.at[0, 0, :, self.cols]
        drain(v, self.r.at[4]); drain(v, self.r.at[5])
        if self.xf:
            v = self.res.at[1 - pc.y, pc.x, :, self.cols]; self.send(v, v, 6, pc.xn)
        else:
            v = self.res.at[pc.y, 1 - pc.x, :, self.cols]; self.send(v, v, 6, pc.yn)
    def p7(self):
        drain(self.res.at[0, 0, :, self.cols], self.r.at[6])
        v = self.res.at[:, :, :, self.cols]
        self.send(v, v, 7, self.pc.core)
    def p8(self):
        drain(self.res.at[:, :, :, self.cols], self.r.at[7])
    def finish(self):
        drain(self.r1, self.s.at[0]); drain(self.r2, self.s.at[1]); drain(self.r3, self.s.at[2])
        drain(self.r4.at[pl.ds(0, self.F - 1)], self.s.at[3])
        v = self.res.at[0, 0, :, self.cols]
        for i in (4, 5, 6): drain(v, self.s.at[i])
        drain(self.res.at[:, :, :, self.cols], self.s.at[7])

Reduce.STAGES = [Reduce.p1, Reduce.p2, Reduce.p3, Reduce.p4, Reduce.p5, Reduce.p6, Reduce.p7, Reduce.p8]

def red_shapes(shape):
    f, _, _, m, c = shape
    return (f, 2, 2, m, c // 2), (f, 2, m, c // 2), (f, m, c // 2), (f, m, c // 2)


HEAD = 64
BLOCK = 128
TRUNK = 512
TREE_LEN = 1024


epsilon = 1e-05
far_below = -1e30


def nt(a, b):
    return lax.dot_general(a, b, (((1,), (1,)), ((), ())), preferred_element_type=jnp.float32)


def tn(a, b):
    return lax.dot_general(a, b, (((0,), (0,)), ((), ())), preferred_element_type=jnp.float32)


def mm(a, b):
    return jnp.dot(a, b, preferred_element_type=jnp.float32)


def bf(a):
    return a.astype(jnp.bfloat16)


def f32(a):
    return a.astype(jnp.float32)


def row_tiles(rows):
    return 256 if rows % 256 == 0 else 128


def normalized(v):
    center = v - jnp.mean(v, axis=1, keepdims=True)
    inv = lax.rsqrt(jnp.mean(center * center, axis=1, keepdims=True) + epsilon)
    return center * inv, inv


class Span:
    def __init__(self, fsdp, rows, reach, f):
        self.rows, self.reach, self.f = rows, reach, f
        self.window = reach * rows
        self.blocks = rows // BLOCK
        self.first = f * self.blocks
        tree = TREE_LEN // BLOCK
        self.tree = tree
        self.start = (self.first // tree) * TREE_LEN - f * rows + self.window

    def kind(self, i):
        return lax.rem(self.first + i, self.tree)

    def base(self, i):
        return pl.multiple_of(((self.first + i) // self.tree) * TREE_LEN - self.f * self.rows + self.window, BLOCK)


def rows_at(start, size):
    return pl.ds(pl.multiple_of(start, BLOCK), size)


def make_bias(span, kseg, qrow, bias):
    @pl.loop(0, span.blocks)
    def _(i):
        b, base = span.kind(i), span.base(i)
        q_pos = b * BLOCK + lax.broadcasted_iota(jnp.int32, (1, BLOCK), 1)
        parent, own = qrow[i, 0:1, :], qrow[i, 1:2, :]

        def put(slot, key, count):
            k_pos = key + lax.broadcasted_iota(jnp.int32, (count, 1), 0)
            seg = kseg[rows_at(base + key, count), :]
            seen = (k_pos <= q_pos) & ((seg == parent) | (seg == own))
            bias[i, pl.ds(slot, count), :] = jnp.where(seen, 0.0, far_below)

        for n in range(TRUNK // BLOCK):

            @pl.when(b == n)
            def _():
                put(0, 0, (n + 1) * BLOCK)

        @pl.when(b >= 4)
        def _():
            put(256, b * BLOCK, BLOCK)

        @pl.when(b >= 6)
        def _():
            put(0, TRUNK, 256)


def by_kind(b, body):
    for n in range(TRUNK // BLOCK):

        @pl.when(b == n)
        def _():
            body([(0, (n + 1) * BLOCK, 0)])

    @pl.when((b >= 4) & (b < 6))
    def _():
        body([(0, 512, None), (None, BLOCK, 256)])

    @pl.when(b >= 6)
    def _():
        body([(0, 512, None), (512, 256, 0), (None, BLOCK, 256)])


def stacked(pair):
    low = lax.broadcasted_iota(jnp.int32, (1, 2 * HEAD), 1) < HEAD
    zero = jnp.zeros_like(pair)
    return jnp.concatenate([jnp.where(low, pair, zero), jnp.where(low, zero, pair)], axis=0)


def unstacked_t(wide):
    both = jnp.concatenate([wide[:HEAD, :BLOCK], wide[HEAD:, BLOCK:]], axis=0)
    return both.T


def part_rows(span, i, b, part):
    key, count, slot = part
    return rows_at(span.base(i) + (b * BLOCK if key is None else key), count)


def part_scores(q2, k, bias, i, part):
    s = nt(k, q2)
    slot = part[2]
    if slot is not None:
        one = bias[i, pl.ds(slot, part[1]), :]
        s = s + jnp.concatenate([one, one], axis=1)
    return s


def pair_cols(p):
    return pl.ds(pl.multiple_of(p * 2 * HEAD, 2 * HEAD), 2 * HEAD)


def transpose_pair(src, p, start, stop, dst):
    @pl.loop(start // BLOCK, stop // BLOCK)
    def _(j):
        dst[:, pl.ds(pl.multiple_of(j * BLOCK, BLOCK), BLOCK)] = src[rows_at(j * BLOCK, BLOCK), pair_cols(p)].T


def attend_pair(span, p, q, k, v, bias, v_t, mixed, lse):
    transpose_pair(v, p, span.start, span.window + span.rows, v_t)
    cols = pair_cols(p)

    @pl.loop(0, span.blocks)
    def _(i):
        b = span.kind(i)
        own = rows_at(i * BLOCK, BLOCK)
        q2 = stacked(q[own, cols])

        def body(parts):
            rows = [part_rows(span, i, b, part) for part in parts]
            scores = [part_scores(q2, k[r, cols], bias, i, part) for r, part in zip(rows, parts)]
            top = functools.reduce(jnp.maximum, [jnp.max(s, axis=0, keepdims=True) for s in scores])
            expo = [jnp.exp(s - top) for s in scores]
            total = sum(jnp.sum(e, axis=0, keepdims=True) for e in expo)
            inv = 1.0 / total
            out = sum(mm(v_t[:, r], bf(e * inv)) for r, e in zip(rows, expo))
            mixed[own, cols] = bf(unstacked_t(out))
            lse[p, pl.ds(i, 1), :] = top + jnp.log(total)

        by_kind(b, body)


def norm_tile(x, gain, shift):
    hat, _ = normalized(f32(x))
    return bf(hat * gain + shift)


def project(span, x, fv, lnp, w1, w2, n1, q, k, v):
    gain, shift = lnp[0:1, :], lnp[1:2, :]
    tile = row_tiles(span.rows)
    third = w1.shape[1] // 4
    half = 2 * third
    scale = HEAD ** (-0.5)

    @pl.loop(span.window // tile, (span.window + span.rows) // tile)
    def _(t):
        rows = rows_at(t * tile, tile)
        n = norm_tile(x[rows, :], gain, shift)
        own = rows_at(t * tile - span.window, tile)
        n1[own, :] = n
        a = mm(n, w1[...])
        q[own, :half] = bf(f32(bf(a[:, :half])) * scale)
        k[rows, :half] = bf(a[:, half:])
        a = mm(n, w2[...])
        q[own, half:] = bf(f32(bf(a[:, :third])) * scale)
        k[rows, half:] = bf(a[:, half:half + third])
        v[rows, :third] = bf(a[:, third:half])
        v[rows, third:third + BLOCK] = bf(a[:, half + third:half + third + BLOCK])
        v[rows, third + BLOCK:] = fv[rows, :]

    @pl.loop(span.start // tile, span.window // tile)
    def _(t):
        rows = rows_at(t * tile, tile)
        n = norm_tile(x[rows, :], gain, shift)
        k[rows, :half] = bf(mm(n, w1[:, half:]))
        a = mm(n, w2[:, third:])
        v[rows, :third] = bf(a[:, :third])
        k[rows, half:] = bf(a[:, third:half])
        v[rows, third:third + BLOCK] = bf(a[:, half:half + BLOCK])
        v[rows, third + BLOCK:] = fv[rows, :]


def branch_out(span, x, lnp, mixed, wo, resid, n2):
    gain, shift = lnp[2:3, :], lnp[3:4, :]
    tile = row_tiles(span.rows)

    @pl.loop(0, span.rows // tile)
    def _(t):
        rows = rows_at(t * tile, tile)
        r = f32(x[rows_at(span.window + t * tile, tile), :]) + mm(mixed[rows, :], wo[...])
        resid[rows, :] = r
        hat, _ = normalized(r)
        n2[rows, :] = bf(hat * gain + shift)


def forward_kernel(fsdp, reach, x, fv, lnp, w1, w2, wo, kseg, qrow, n1, q, k, v, mixed, lse, resid, n2, bias, v_t):
    span = Span(fsdp, q.shape[0], reach, lax.axis_index("fsdp"))
    make_bias(span, kseg, qrow, bias)
    project(span, x, fv, lnp, w1, w2, n1, q, k, v)

    @pl.loop(0, q.shape[1] // (2 * HEAD))
    def _(p):
        attend_pair(span, p, q, k, v, bias, v_t, mixed, lse)

    branch_out(span, x, lnp, mixed, wo, resid, n2)


VM = pl.BlockSpec(memory_space=pltpu.VMEM)


def forward_call(fsdp, reach, x, fv, lnp, w1, w2, wo, kseg, qrow):
    window, width = x.shape
    rows = window // (reach + 1)
    s = jax.ShapeDtypeStruct
    low, full = jnp.bfloat16, jnp.float32
    pairs, blocks = width // (2 * HEAD), rows // BLOCK
    outs = (
        s((rows, width), low), s((rows, width), low), s((window, width), low), s((window, width), low), s((rows, width), low),
        s((pairs, -(-blocks // 8) * 8, 2 * BLOCK), full), s((rows, width), full), s((rows, width), low),
    )
    return pl.pallas_call(
        functools.partial(forward_kernel, fsdp, reach),
        out_shape=outs, in_specs=[VM] * 8, out_specs=[VM] * 8,
        scratch_shapes=[pltpu.VMEM((blocks, TRUNK, BLOCK), full), pltpu.VMEM((2 * HEAD, window), low)],
        compiler_params=pltpu.CompilerParams(vmem_limit_bytes=50 << 20),
    )(x, fv, lnp, w1, w2, wo, kseg, qrow)


GELU_A = 0.7978845608028654
GELU_B = 0.044715


def gelu_both(u):
    sq = u * u
    t = jnp.tanh(GELU_A * u * (1.0 + GELU_B * sq))
    half = 0.5 * (1.0 + t)
    slope = half + 0.5 * u * (1.0 - t * t) * (GELU_A * (1.0 + 3.0 * GELU_B * sq))
    return u * half, slope


def transpose_all(src, dst):
    cols = src.shape[1] // BLOCK

    @pl.loop(0, src.shape[0] // BLOCK)
    def _(j):
        rows = rows_at(j * BLOCK, BLOCK)
        for c in range(cols):
            dst[c * BLOCK:(c + 1) * BLOCK, rows] = src[rows, c * BLOCK:(c + 1) * BLOCK].T


def mlp_chunk(rows, n2, n2_t, cot, win, wdn, out_acc, gn2_acc, hid, gact, gin, gdn):
    tile = row_tiles(rows)

    @pl.loop(0, rows // tile)
    def _(t):
        r = rows_at(t * tile, tile)
        h, slope = gelu_both(mm(n2[r, :], win()))
        h = bf(h)
        hid[r, :] = h
        out_acc[r, :] += mm(h, wdn())
        g = bf(nt(cot[r, :], wdn()) * slope)
        gact[r, :] = g
        gn2_acc[r, :] += nt(g, win())

    gdn(bf(tn(hid[...], cot[...])))
    gin(bf(mm(n2_t[...], gact[...])))


def norm_back(hat, inv, grad, gain):
    e = grad * gain
    return inv * (e - jnp.mean(e, axis=1, keepdims=True) - hat * jnp.mean(e * hat, axis=1, keepdims=True))


def second_norm_back(rows, lnp, resid, cot, gn2, gres, gbranch, sums):
    tile = row_tiles(rows)
    sums[...] = jnp.zeros_like(sums)

    @pl.loop(0, rows // tile)
    def _(t):
        r = rows_at(t * tile, tile)
        hat, inv = normalized(resid[r, :])
        g = gn2[r, :]
        gr = f32(cot[r, :]) + norm_back(hat, inv, g, lnp[2:3, :])
        gres[r, :] = gr
        gbranch[r, :] = bf(gr)
        sums[2:3, :] += jnp.sum(g * hat, axis=0, keepdims=True)
        sums[3:4, :] += jnp.sum(g, axis=0, keepdims=True)


def branch_back(rows, gbranch, wo, gmixed):
    tile = row_tiles(rows)

    @pl.loop(0, rows // tile)
    def _(t):
        r = rows_at(t * tile, tile)
        gmixed[r, :] = bf(nt(gbranch[r, :], wo[...]))


def mlp_kernel(n2, cot, resid, mixed, lnp, win, wdn, wo, outputs, gin, gdn, go, gres, gmixed, sums, n2_t, out_acc, gn2_acc, hid, gact, gbranch):
    rows = n2.shape[0]
    transpose_all(n2, n2_t)
    out_acc[...] = resid[...]
    gn2_acc[...] = jnp.zeros_like(gn2_acc)

    @pl.loop(0, win.shape[0])
    def _(c):
        def put_in(v):
            gin[c] = v

        def put_dn(v):
            gdn[c] = v

        mlp_chunk(rows, n2, n2_t, cot, lambda: win[c], lambda: wdn[c], out_acc, gn2_acc, hid, gact, put_in, put_dn)

    outputs[...] = bf(out_acc[...])
    second_norm_back(rows, lnp, resid, cot, gn2_acc, gres, gbranch, sums)
    branch_back(rows, gbranch, wo, gmixed)
    go[...] = bf(tn(mixed[...], gbranch[...]))


def mlp_call(n2, cot, resid, mixed, lnp, win, wdn, wo):
    rows, width = n2.shape
    n_ff, _, cols = win.shape
    s, low, full = jax.ShapeDtypeStruct, jnp.bfloat16, jnp.float32
    outs = (
        s((rows, width), low), s(win.shape, low), s(wdn.shape, low), s((width, width), low), s((rows, width), full),
        s((rows, width), low), s((8, width), full),
    )
    return pl.pallas_call(
        mlp_kernel, out_shape=outs, in_specs=[VM] * 8, out_specs=[VM] * 7,
        scratch_shapes=[
            pltpu.VMEM((width, rows), low), pltpu.VMEM((rows, width), full), pltpu.VMEM((rows, width), full),
            pltpu.VMEM((rows, cols), low), pltpu.VMEM((rows, cols), low), pltpu.VMEM((rows, width), low),
        ],
        compiler_params=pltpu.CompilerParams(vmem_limit_bytes=58 << 20),
    )(n2, cot, resid, mixed, lnp, win, wdn, wo)


def attend_back_pair(span, p, q, k, v, gmixed, bias, lse, k_t, dk_acc, dv_acc, dq):
    transpose_pair(k, p, span.start, span.window + span.rows, k_t)
    cols = pair_cols(p)

    @pl.loop(span.start // BLOCK, (span.window + span.rows) // BLOCK)
    def _(j):
        r = rows_at(j * BLOCK, BLOCK)
        dk_acc[r, :] = jnp.zeros((BLOCK, 2 * HEAD), jnp.float32)
        dv_acc[r, :] = jnp.zeros((BLOCK, 2 * HEAD), jnp.float32)

    @pl.loop(0, span.blocks)
    def _(i):
        b = span.kind(i)
        own = rows_at(i * BLOCK, BLOCK)
        q2, g2 = stacked(q[own, cols]), stacked(gmixed[own, cols])
        l = lse[p, pl.ds(i, 1), :]

        def body(parts):
            rows = [part_rows(span, i, b, part) for part in parts]
            probs = [jnp.exp(part_scores(q2, k[r, cols], bias, i, part) - l) for r, part in zip(rows, parts)]
            gw = [nt(v[r, cols], g2) for r in rows]
            inner = sum(jnp.sum(a * g, axis=0, keepdims=True) for a, g in zip(probs, gw))
            gs = [bf(a * (g - inner)) for a, g in zip(probs, gw)]
            out = sum(mm(k_t[:, r], g) for r, g in zip(rows, gs))
            dq[own, cols] = bf(unstacked_t(out) * HEAD ** (-0.5))
            for r, a, g in zip(rows, probs, gs):
                dk_acc[r, :] += mm(g, q2)
                dv_acc[r, :] += mm(bf(a), g2)

        by_kind(b, body)


def backward_kernel(fsdp, reach, q, k, v, gmixed, lse, kseg, qrow, dq, dk, dv, wk, wv, bias, k_t, dk_acc, dv_acc):
    span = Span(fsdp, q.shape[0], reach, lax.axis_index("fsdp"))
    make_bias(span, kseg, qrow, bias)
    wk[...] = jnp.zeros_like(wk)
    wv[...] = jnp.zeros_like(wv)

    @pl.loop(0, q.shape[1] // (2 * HEAD))
    def _(p):
        cols = pair_cols(p)
        attend_back_pair(span, p, q, k, v, gmixed, bias, lse, k_t, dk_acc, dv_acc, dq)
        dk[:, cols] = dk_acc[span.window:, :]
        dv[:, cols] = dv_acc[span.window:, :]

        @pl.loop(span.start // BLOCK, span.window // BLOCK)
        def _(j):
            r = rows_at(j * BLOCK, BLOCK)
            wk[r, cols] = bf(dk_acc[r, :])
            wv[r, cols] = bf(dv_acc[r, :])


def backward_call(fsdp, reach, q, k, v, gmixed, lse, kseg, qrow):
    window, width = k.shape
    rows = q.shape[0]
    s, low, full = jax.ShapeDtypeStruct, jnp.bfloat16, jnp.float32
    early = window - rows
    outs = (s((rows, width), low), s((rows, width), full), s((rows, width), full), s((early, width), low), s((early, width), low))
    return pl.pallas_call(
        functools.partial(backward_kernel, fsdp, reach), out_shape=outs, in_specs=[VM] * 7, out_specs=[VM] * 5,
        scratch_shapes=[
            pltpu.VMEM((rows // BLOCK, TRUNK, BLOCK), full), pltpu.VMEM((2 * HEAD, window), low),
            pltpu.VMEM((window, 2 * HEAD), full), pltpu.VMEM((window, 2 * HEAD), full),
        ],
        compiler_params=pltpu.CompilerParams(vmem_limit_bytes=58 << 20),
    )(q, k, v, gmixed, lse, kseg, qrow)


def projection_back(span, x, n1, dq, dk, dv, lnp, w1, w2, gres, gin, gfirst, g1, g2, sums, n1_t, cat1, cat2):
    rows = span.rows
    third = w1.shape[1] // 4
    half = 2 * third
    fresh = third + BLOCK
    tile = row_tiles(rows)
    transpose_all(n1, n1_t)

    @pl.loop(0, rows // tile)
    def _(t):
        r = rows_at(t * tile, tile)
        cat1[r, :half] = dq[r, :half]
        cat1[r, half:] = bf(dk[r, :half])
        cat2[r, :third] = dq[r, half:]
        cat2[r, third:half] = bf(dv[r, :third])
        cat2[r, half:half + third] = bf(dk[r, half:])
        cat2[r, half + third:half + third + BLOCK] = bf(dv[r, third:fresh])
        cat2[r, half + third + BLOCK:] = jnp.zeros((tile, BLOCK), jnp.bfloat16)
        gfirst[r, :] = dv[r, fresh:]

    g1[...] = bf(mm(n1_t[...], cat1[...]))
    g2[...] = bf(mm(n1_t[...], cat2[...]))

    @pl.loop(0, rows // tile)
    def _(t):
        r = rows_at(t * tile, tile)
        g = nt(cat1[r, :], w1[...]) + nt(cat2[r, :], w2[...])
        hat, inv = normalized(f32(x[rows_at(span.window + t * tile, tile), :]))
        gin[r, :] = gres[r, :] + norm_back(hat, inv, g, lnp[0:1, :])
        sums[0:1, :] += jnp.sum(g * hat, axis=0, keepdims=True)
        sums[1:2, :] += jnp.sum(g, axis=0, keepdims=True)


def projection_back_kernel(fsdp, reach, x, n1, dq, dk, dv, lnp, w1, w2, gres, sums_in, gin, gfirst, g1, g2, sums, n1_t, cat1, cat2):
    span = Span(fsdp, dq.shape[0], reach, lax.axis_index("fsdp"))
    sums[...] = sums_in[...]
    projection_back(span, x, n1, dq, dk, dv, lnp, w1, w2, gres, gin, gfirst, g1, g2, sums, n1_t, cat1, cat2)


def projection_back_call(fsdp, reach, x, n1, dq, dk, dv, lnp, w1, w2, gres, sums):
    rows, width = dq.shape
    s, low, full = jax.ShapeDtypeStruct, jnp.bfloat16, jnp.float32
    outs = (s((rows, width), full), s((rows, width // 2), full), s(w1.shape, low), s(w2.shape, low), s((8, width), full))
    return pl.pallas_call(
        functools.partial(projection_back_kernel, fsdp, reach), out_shape=outs, in_specs=[VM] * 10, out_specs=[VM] * 5,
        scratch_shapes=[pltpu.VMEM((width, rows), low), pltpu.VMEM((rows, w1.shape[1]), low), pltpu.VMEM((rows, w1.shape[1]), low)],
        compiler_params=pltpu.CompilerParams(vmem_limit_bytes=58 << 20),
    )(x, n1, dq, dk, dv, lnp, w1, w2, gres, sums)


def gather_steps(items, u):
    for s, stage in enumerate(Gather.STAGES):
        c = u - s

        @pl.when((c >= 0) & (c < items.count))
        def _():
            for g in items(c):
                stage(g)


def reduce_steps(items, u):
    for s, stage in enumerate(Reduce.STAGES):
        c = u - s

        @pl.when((c >= 0) & (c < items.count))
        def _():
            for g in items(c):
                stage(g)


class Chunks:
    def __init__(self, count, make):
        self.count, self.make = count, make

    def __call__(self, c):
        return self.make(c)


class Scratch:
    def __init__(self):
        self.names, self.shapes = [], []

    def add(self, name, shape):
        self.names.append(name)
        self.shapes.append(shape)

    def bind(self, refs):
        for name, ref in zip(self.names, refs):
            setattr(self, name, ref)
        return self


def layer_kernel(fsdp, n_ff, scratch, n_out, *refs):
    (inputs, first, cot_in, vec, a_q, a_k, a_v, a_o, a_in, a_dn, kseg, qrow) = refs[:12]
    (outputs, gin, gfirst, rs_q, rs_k, rs_v, rs_o, rs_in, rs_dn, rs_vec) = refs[12 : 12 + n_out]
    m = scratch.bind(refs[12 + n_out :])
    pc = Place(fsdp)
    f = pc.f
    rows, width = cot_in.shape
    span = Span(fsdp, rows, 1, f)
    tile = row_tiles(rows)
    tiles = rows // tile
    last = fsdp - 1
    flat = lambda ref: ref.reshape(-1, ref.shape[-1])
    w_q, w_k, w_v, w_o = (flat(b) for b in (m.b_q, m.b_k, m.b_v, m.b_o))
    mixed, cot = m.mixed.reshape(rows, width), m.cot.reshape(rows, width)
    x, q, k, v, n1, n2, tr = m.x, m.q, m.k, m.v, m.n1, m.n2, m.tr

    def local(src, dst, sem):
        c = pltpu.make_async_copy(src, dst, sem)
        c.start()
        return c

    lv = local(vec, m.vec.at[f], m.l_sem.at[0])
    lw = [local(a, b.at[f], m.l_sem.at[1 + i]) for i, (a, b) in enumerate(((a_q, m.b_q), (a_k, m.b_k), (a_v, m.b_v), (a_o, m.b_o)))]
    lx = local(inputs, x.at[pl.ds(rows, rows)], m.l_sem.at[5])
    lf = local(first, v.at[pl.ds(rows, rows), pl.ds(width // 2, width // 2)], m.l_sem.at[6])
    lc = local(cot_in, cot, m.l_sem.at[7])
    lk = local(kseg, m.dk_acc, m.l_sem.at[8])
    group = a_in.shape[-1] // fsdp

    def own_chunk(c, act):
        for g in range(fsdp):
            cols = pl.ds(pl.multiple_of(g * group + c * BLOCK, BLOCK), BLOCK)
            act(pltpu.make_async_copy(a_in.at[:, :, :, cols], m.b_in.at[c, f, :, :, :, pl.ds(g * BLOCK, BLOCK)], m.lc_sem.at[c, g]))
        act(pltpu.make_async_copy(a_dn.at[c], m.b_dn.at[c, f], m.lc_sem.at[c, fsdp]))

    @pl.loop(0, n_ff)
    def _(c):
        own_chunk(c, lambda d: d.start())

    pc.barrier()
    lv.wait()
    for o in pc.others:
        pltpu.make_async_remote_copy(
            src_ref=m.vec.at[f], dst_ref=m.vec.at[f], send_sem=m.v_send.at[0], recv_sem=m.v_recv.at[0], device_id=pc.zdev(o), device_id_type=MESH
        ).start()
    gat = [Gather(pc, b, m.g_send.at[i], m.g_recv.at[i], xf) for i, (b, xf) in enumerate(((m.b_q, True), (m.b_k, False), (m.b_v, True), (m.b_o, False)))]
    for l, g in zip(lw[:3], gat):
        l.wait()
        g.z_start()

    next_start = Span(fsdp, rows, 1, f + 1).start

    def window(t):
        r = pl.ds(t * tile, tile)
        nxt = (pc.r, f + 1)
        return [
            pltpu.make_async_remote_copy(src_ref=inputs.at[r], dst_ref=x.at[r], send_sem=m.w_send.at[0, t], recv_sem=m.w_recv.at[0, t], device_id=nxt, device_id_type=MESH),
            pltpu.make_async_remote_copy(
                src_ref=first.at[r], dst_ref=v.at[r, pl.ds(width // 2, width // 2)], send_sem=m.w_send.at[1, t], recv_sem=m.w_recv.at[1, t], device_id=nxt, device_id_type=MESH
            ),
        ]

    for t in range(tiles):

        @pl.when((f < last) & (t * tile >= next_start))
        def _():
            for c in window(t):
                c.start()

    lw[3].wait()
    gat[3].z_start()
    ff = Chunks(
        n_ff,
        lambda c: [Gather(pc, m.b_in.at[c], m.gi_send.at[c], m.gi_recv.at[c], True), Gather(pc, m.b_dn.at[c], m.gd_send.at[c], m.gd_recv.at[c], False)],
    )

    @pl.loop(0, n_ff)
    def _(c):
        own_chunk(c, lambda d: d.wait())
        for g in ff(c):
            g.z_start()

    for g in gat[:3]:
        g.z_wait()
        g.a_start()
    lk.wait()
    make_bias(span, m.dk_acc, qrow, m.bias)
    for g in gat[:3]:
        g.a_wait()
        g.b_start()
    gat[3].z_wait()
    gat[3].a_start()
    v3 = m.vec.at[pl.ds(0, last)]
    drain(v3, m.v_recv.at[0])
    drain(v3, m.v_send.at[0])
    m.lnp[...] = functools.reduce(lambda a, b: a + b, [m.vec[j] for j in range(fsdp)])
    gain, shift = m.lnp[0:1, :], m.lnp[1:2, :]
    lx.wait()

    @pl.loop(0, tiles)
    def _(t):
        n1[rows_at(t * tile, tile), :] = norm_tile(x[rows_at(rows + t * tile, tile), :], gain, shift)

    for g in gat[:3]:
        g.b_wait()
        g.c_start()
    gat[3].a_wait()
    gat[3].b_start()
    lf.wait()
    for g in gat[:3]:
        g.c_wait()
    half = width // 2

    @pl.loop(0, tiles)
    def _(t):
        r, own = rows_at(rows + t * tile, tile), rows_at(t * tile, tile)
        n = n1[own, :]
        q[own, :] = bf(f32(bf(mm(n, w_q[...]))) * HEAD ** (-0.5))
        k[r, :] = bf(mm(n, w_k[...]))
        v[r, :half] = bf(mm(n, w_v[:, :half]))

    for t in range(tiles):

        @pl.when(t * tile >= span.start)
        def _():
            drain(x.at[pl.ds(t * tile, tile)], m.w_recv.at[0, t])
            drain(v.at[pl.ds(t * tile, tile), pl.ds(half, half)], m.w_recv.at[1, t])

    @pl.loop(span.start // tile, tiles)
    def _(t):
        r = rows_at(t * tile, tile)
        n = norm_tile(x[r, :], gain, shift)
        k[r, :] = bf(mm(n, w_k[...]))
        v[r, :half] = bf(mm(n, w_v[:, :half]))

    gat[3].b_wait()
    gat[3].c_start()

    pairs = width // (2 * HEAD)

    @pl.loop(0, pairs)
    def _(p):
        attend_pair(span, p, q, k, v, m.bias, m.turned, mixed, m.lse)
        gather_steps(ff, p)

    gat[3].c_wait()
    branch_out(span, x, m.lnp, mixed, w_o, m.resid, n2)
    for g in gat:
        g.finish()

    lc.wait()
    transpose_all(n2, tr)
    m.acc1[...] = m.resid[...]
    m.acc2[...] = jnp.zeros_like(m.acc2)
    red = Chunks(
        n_ff,
        lambda c: [
            Reduce(pc, m.b_in.at[c], *(a.at[c] for a in m.r_in), rs_in.at[c], m.ri_send.at[c], m.ri_recv.at[c], True),
            Reduce(pc, m.b_dn.at[c], *(a.at[c] for a in m.r_dn), rs_dn.at[c], m.rd_send.at[c], m.rd_recv.at[c], False),
        ],
    )
    hid, gact = m.back.at[0, :, pl.ds(0, fsdp * BLOCK)], m.back.at[1, :, pl.ds(0, fsdp * BLOCK)]

    @pl.loop(0, n_ff)
    def _(c):
        gather_steps(ff, c + pairs)
        b_in, b_dn = flat(m.b_in.at[c]), flat(m.b_dn.at[c])

        def put_in(val):
            b_in[...] = val

        def put_dn(val):
            b_dn[...] = val

        mlp_chunk(rows, n2, tr, cot, lambda: b_in[...], lambda: b_dn[...], m.acc1, m.acc2, hid, gact, put_in, put_dn)
        reduce_steps(red, c)

    @pl.loop(0, tiles)
    def _(t):
        r = rows_at(t * tile, tile)
        m.back[0, r, :] = bf(m.acc1[r, :])

    lo = local(m.back.at[0], outputs, m.l_sem.at[0])
    m.sums[...] = jnp.zeros_like(m.sums)
    second_norm_back(rows, m.lnp, m.resid, cot, m.acc2, m.resid, n2, m.sums)
    branch_back(rows, n2, w_o, m.gmixed)

    @pl.loop(0, width // tile)
    def _(t):
        r = rows_at(t * tile, tile)
        w_o[r, :] = bf(tn(mixed[:, pl.ds(pl.multiple_of(t * tile, tile), tile)], n2[...]))

    lo.wait()

    @pl.when(f < last)
    def _():
        pl.semaphore_signal(m.ready, inc=1, device_id=(pc.r, f + 1), device_id_type=MESH)

    @pl.when(f > 0)
    def _():
        pl.semaphore_wait(m.ready, 1)

    transpose_all(n1, tr)
    stat = [
        Reduce(pc, b, *scr, res, m.rs_send.at[i], m.rs_recv.at[i], xf)
        for i, (b, scr, res, xf) in enumerate(
            ((m.b_o, m.r_o, rs_o, True), (m.mixed, m.r_q, rs_q, False), (m.cot, m.r_k, rs_k, True), (m.g_v, m.r_v, rs_v, False))
        )
    ]
    red_o, red_q, red_k, red_v = stat

    def early(t, p):
        r, cols = pl.ds(t * tile, tile), pair_cols(p)
        prev = (pc.r, f - 1)
        return [
            pltpu.make_async_remote_copy(
                src_ref=x.at[pl.ds(j * rows + t * tile, tile), cols], dst_ref=m.back.at[j, r, cols], send_sem=m.e_send.at[j, p, t], recv_sem=m.e_recv.at[j, p, t],
                device_id=prev, device_id_type=MESH,
            )
            for j in range(2)
        ]

    dk, dv = m.acc1, m.acc2

    @pl.loop(0, pairs)
    def _(p):
        cols = pair_cols(p)
        attend_back_pair(span, p, q, k, v, m.gmixed, m.bias, m.lse, m.turned, m.dk_acc, m.dv_acc, q)
        dk[:, cols] = m.dk_acc[rows:, :]
        dv[:, cols] = m.dv_acc[rows:, :]
        for t in range(tiles):

            @pl.when((f > 0) & (t * tile >= span.start))
            def _():
                r = pl.ds(t * tile, tile)
                x[r, cols] = bf(m.dk_acc[r, :])
                x[pl.ds(rows + t * tile, tile), cols] = bf(m.dv_acc[r, :])
                for c in early(t, p):
                    c.start()

        reduce_steps(red, n_ff + p)
        for s in range(6):

            @pl.when(p == s)
            def _():
                Reduce.STAGES[s](red_o)

    d_q = flat(m.mixed)
    wide = width // tile

    def weight_grad(dst, grad, cols):
        @pl.loop(0, wide)
        def _(t):
            r = rows_at(t * tile, tile)
            dst[r, :cols] = bf(mm(tr[r, :], grad[:, :cols]))

    weight_grad(d_q, q, width)
    red_q.p1()
    for u in range(n_ff + pairs, n_ff + 7):
        reduce_steps(red, u)
    red_o.p7()

    @pl.loop(0, pairs)
    def _(p):
        for t in range(tiles):

            @pl.when((f < last) & (t * tile >= next_start))
            def _():
                r, cols = pl.ds(t * tile, tile), pair_cols(p)
                for j, own in enumerate((dk, dv)):
                    drain(m.back.at[j, r, cols], m.e_recv.at[j, p, t])
                    own[r, cols] += f32(m.back[j, r, cols])

    red_q.p2()

    @pl.loop(0, tiles)
    def _(t):
        r = rows_at(t * tile, tile)
        k[r, :] = bf(dk[r, :])
        v[r, :half] = bf(dv[r, :half])

    gf = local(dv.at[:, pl.ds(half, half)], gfirst, m.l_sem.at[1])
    d_k, d_v = flat(m.cot), flat(m.g_v)
    weight_grad(d_k, k.at[pl.ds(0, rows)], width)
    red_k.p1()
    d_v[:, half:] = jnp.zeros((width, d_v.shape[1] - half), jnp.bfloat16)
    weight_grad(d_v, v.at[pl.ds(0, rows)], half)
    red_v.p1()
    red_q.p3()
    red_o.p8()

    @pl.loop(0, tiles)
    def _(t):
        r = rows_at(t * tile, tile)
        g = nt(q[r, :], w_q[...]) + nt(k[r, :], w_k[...]) + nt(v[r, :half], w_v[:, :half])
        dk[r, :] = g

    red_q.p4()
    red_k.p2()
    red_v.p2()
    lx = local(inputs, n1, m.l_sem.at[2])
    lx.wait()

    @pl.loop(0, tiles)
    def _(t):
        r = rows_at(t * tile, tile)
        g = dk[r, :]
        hat, inv = normalized(f32(n1[r, :]))
        m.resid[r, :] += norm_back(hat, inv, g, m.lnp[0:1, :])
        m.sums[0:1, :] += jnp.sum(g * hat, axis=0, keepdims=True)
        m.sums[1:2, :] += jnp.sum(g, axis=0, keepdims=True)

    gi = local(m.resid, gin, m.l_sem.at[3])
    red_q.p5()
    red_k.p3()
    red_v.p3()

    def exchange(src, dst, i, dev):
        c = pltpu.make_async_remote_copy(src_ref=src, dst_ref=dst, send_sem=m.v_send.at[i], recv_sem=m.v_recv.at[i], device_id=dev, device_id_type=MESH)
        c.start()
        return c

    cur = m.sums
    work = [(red_q.p6, red_k.p4, red_v.p4), (red_q.p7, red_k.p5, red_v.p5), (red_q.p8, red_k.p6, red_v.p6)]
    for i, dev in enumerate((pc.core, pc.xn, pc.yn)):
        c = exchange(cur, m.s_pair.at[i], 1 + i, dev)
        for step in work[i]:
            step()
        c.wait()
        m.s_pair[i] = m.s_pair[i] + cur[...]
        cur = m.s_pair.at[i]
    for o in pc.others:
        exchange(cur, m.s_z.at[f], 4, pc.zdev(o))
    red_k.p7()
    red_v.p7()
    z3 = m.s_z.at[pl.ds(0, last)]
    drain(z3, m.v_recv.at[4])
    drain(z3, m.v_send.at[4])
    m.s_z[f] = cur[...]
    rs_vec[...] = functools.reduce(lambda a, b: a + b, [m.s_z[j] for j in range(fsdp)])
    red_k.p8()
    red_v.p8()
    for g in stat:
        g.finish()

    @pl.loop(0, n_ff)
    def _(c):
        for g in red(c):
            g.finish()

    for t in range(tiles):

        @pl.when((f < last) & (t * tile >= next_start))
        def _():
            for c in window(t):
                c.wait_send()

    @pl.loop(0, pairs)
    def _(p):
        for t in range(tiles):

            @pl.when((f > 0) & (t * tile >= span.start))
            def _():
                for c in early(t, p):
                    c.wait_send()

    gf.wait()
    gi.wait()


def layer_call(fsdp, inputs, first, cot, vec, w_query, w_key, w_value, w_out, w_in, w_down, kseg, qrow):
    rows, width = inputs.shape
    shard = w_query.shape[0]
    n_ff = w_down.shape[0] // BLOCK
    low, full = jnp.bfloat16, jnp.float32
    mq, md = shard // 4, BLOCK // 4
    pairs, blocks = width // (2 * HEAD), rows // BLOCK
    value = jnp.pad(w_value, ((0, 0), (0, BLOCK)))
    split = lambda a: a.reshape(2, 2, mq, a.shape[1])
    buf = lambda m, c, lead=(): (*lead, fsdp, 2, 2, m, c)
    chunk = fsdp * BLOCK
    sc = Scratch()
    V, D = pltpu.VMEM, pltpu.SemaphoreType.DMA
    for name, shape in (
        ("b_q", buf(mq, width)), ("b_k", buf(mq, width)), ("b_v", buf(mq, value.shape[1])), ("b_o", buf(mq, width)),
        ("b_in", buf(mq, chunk, (n_ff,))), ("b_dn", buf(md, width, (n_ff,))), ("g_v", buf(mq, value.shape[1])),
        ("mixed", buf(mq, width)), ("cot", buf(mq, width)), ("x", (2 * rows, width)), ("k", (2 * rows, width)), ("v", (2 * rows, width)),
        ("q", (rows, width)), ("n1", (rows, width)), ("n2", (rows, width)), ("tr", (width, rows)), ("gmixed", (rows, width)), ("back", (2, rows, width)),
        ("turned", (2 * HEAD, 2 * rows)),
    ):
        sc.add(name, V(shape, low))
    for name, shape in (
        ("vec", (fsdp, 8, width)), ("lnp", (8, width)), ("sums", (8, width)), ("s_pair", (3, 8, width)), ("s_z", (fsdp, 8, width)),
        ("resid", (rows, width)), ("acc1", (rows, width)), ("acc2", (rows, width)), ("bias", (blocks, TRUNK, BLOCK)),
        ("dk_acc", (2 * rows, 2 * HEAD)), ("dv_acc", (2 * rows, 2 * HEAD)), ("lse", (pairs, -(-blocks // 8) * 8, 2 * BLOCK)),
    ):
        sc.add(name, V(shape, full))
    for name, shape in (
        ("l_sem", (9,)), ("lc_sem", (n_ff, fsdp + 1)), ("v_send", (5,)), ("v_recv", (5,)), ("g_send", (4, 5)), ("g_recv", (4, 5)),
        ("w_send", (2, rows // row_tiles(rows))), ("w_recv", (2, rows // row_tiles(rows))),
        ("gi_send", (n_ff, 5)), ("gi_recv", (n_ff, 5)), ("gd_send", (n_ff, 5)), ("gd_recv", (n_ff, 5)),
        ("ri_send", (n_ff, 8)), ("ri_recv", (n_ff, 8)), ("rd_send", (n_ff, 8)), ("rd_recv", (n_ff, 8)), ("rs_send", (4, 8)), ("rs_recv", (4, 8)),
        ("e_send", (2, pairs, rows // row_tiles(rows))), ("e_recv", (2, pairs, rows // row_tiles(rows))),
    ):
        sc.add(name, D(shape))
    sc.add("ready", pltpu.SemaphoreType.REGULAR)
    groups = (("r_in", buf(mq, chunk), n_ff), ("r_dn", buf(md, width), n_ff), ("r_o", buf(mq, width), 0), ("r_q", buf(mq, width), 0), ("r_k", buf(mq, width), 0), ("r_v", buf(mq, value.shape[1]), 0))
    for name, shape, lead in groups:
        for i, sub in enumerate(red_shapes(shape)):
            sc.add(f"{name}{i}", V((lead, *sub) if lead else sub, low))

    n_out = 10
    s = jax.ShapeDtypeStruct
    outs = (
        s((rows, width), low), s((rows, width), full), s((rows, width // 2), full),
        s((2, 2, mq, width), low), s((2, 2, mq, width), low), s((2, 2, mq, value.shape[1]), low), s((2, 2, mq, width), low),
        s((n_ff, 2, 2, mq, chunk), low), s((n_ff, 2, 2, md, width), low), s((8, width), full),
    )

    def body(*refs):
        names = Scratch()
        names.names, names.shapes = sc.names, sc.shapes
        bound = names.bind(refs[12 + n_out :])
        for name, _, _ in groups:
            setattr(bound, name, [getattr(bound, f"{name}{i}") for i in range(4)])
        layer_kernel(fsdp, n_ff, bound, n_out, *refs)

    any_ = pl.BlockSpec(memory_space=pl.ANY)
    return pl.pallas_call(
        body, out_shape=outs, in_specs=[any_] * 11 + [VM], out_specs=[any_] * 3 + [VM] * 7, scratch_shapes=sc.shapes,
        compiler_params=pltpu.CompilerParams(collective_id=3, has_side_effects=True, vmem_limit_bytes=61 << 20),
    )(inputs, first, cot, vec, split(w_query), split(w_key), split(value), split(w_out), split(w_in), w_down.reshape(n_ff, 2, 2, md, width), kseg, qrow)


def shifted(block, axis, distance):
    devices = range(lax.axis_size(axis))
    route = [(i - distance, i) for i in devices if i - distance in devices]
    return lax.ppermute(block, axis, route)


def path_rows(tree_ids, segment_ids, path_table):
    seg_count = path_table.shape[1]
    flat_table = path_table.reshape(-1, 3)
    lookup = tree_ids * seg_count + segment_ids
    onehot = (lookup[:, None] == jnp.arange(flat_table.shape[0], dtype=jnp.int32)[None, :]).astype(
        jnp.int32
    )
    return jnp.sum(onehot[:, :, None] * flat_table[None, :, :], axis=1)


def reorder_rows(grad_block, fsdp_count, rep_count):
    return grad_block.reshape(fsdp_count, rep_count, -1).transpose(1, 0, 2).reshape(-1)


def packed_qkv(query, key, value):
    h, pad = query.shape[1] * 2 // 3, jnp.zeros_like(value[:, : value.shape[1] // 3])
    n = value.shape[1] * 2 // 3
    return jnp.concatenate([query[:, :h], key[:, :h], query[:, h:], value[:, :n], key[:, h:], value[:, n:], pad], axis=1)


def unpacked_qkv(first, second):
    h = first.shape[-1] // 2
    q = h // 2
    return (
        jnp.concatenate([first[..., :h], second[..., :q]], axis=-1),
        jnp.concatenate([first[..., h:], second[..., h : h + q]], axis=-1),
        jnp.concatenate([second[..., q:h], second[..., h + q : h + q + q // 2]], axis=-1),
    )


def segment_info(tree_ids, segment_ids, path_table, row_start, row_count, reach):
    seg_win = lax.dynamic_slice_in_dim(jnp.pad(segment_ids, (reach * row_count, 0)), row_start, (reach + 1) * row_count, 0)
    tree_own = lax.dynamic_slice_in_dim(tree_ids, row_start, row_count, 0)
    seg_own = seg_win[reach * row_count:]
    parent = path_rows(tree_own, seg_own, path_table)[:, 1]
    blocks = row_count // BLOCK
    rows = jnp.stack([parent.reshape(blocks, BLOCK), seg_own.reshape(blocks, BLOCK)], axis=1)
    return seg_win[:, None].astype(jnp.float32), jnp.pad(rows, ((0, 0), (0, 6), (0, 0))).astype(jnp.float32)


def gathered(fsdp, gain1, shift1, gain2, shift2, w_query, w_key, w_value, w_out, w_in, w_down):
    width = w_query.shape[1]
    n_ff = w_down.shape[0] // BLOCK
    packed = packed_qkv(w_query, w_key, w_value)
    full = [lax.all_gather(v, "fsdp", axis=0, tiled=True) for v in (packed, w_out, w_in, w_down)]
    vec = lax.all_gather(jnp.stack([gain1, shift1, gain2, shift2]), "fsdp", axis=1, tiled=True).astype(jnp.float32)
    half = packed.shape[1] // 2
    inner = full[2].reshape(width, fsdp, n_ff, BLOCK).transpose(2, 0, 1, 3).reshape(n_ff, width, -1)
    down = full[3].reshape(fsdp, n_ff, BLOCK, width).transpose(1, 0, 2, 3).reshape(n_ff, -1, width)
    return jnp.pad(vec, ((0, 4), (0, 0))), full[0][:, :half], full[0][:, half:], full[1], inner, down


def reduced(fsdp, sums, g1, g2, go, gin, gdn):
    width = go.shape[0]
    rows = width // fsdp
    n_ff = gin.shape[0]
    both = ("rep", "fsdp")
    rep = lax.axis_size("rep")

    def total(a):
        piece = lax.psum_scatter(reorder_rows(a.astype(jnp.float32), fsdp, rep), both, scatter_dimension=0, tiled=True)
        return lax.all_gather(piece.astype(jnp.bfloat16), "rep", axis=0, tiled=True)

    first, second, ro = (total(a).reshape(rows, -1) for a in (g1, g2, go))
    ri = total(gin.transpose(1, 0, 2)).reshape(rows, n_ff, -1).transpose(1, 0, 2)
    rd = total(gdn.reshape(n_ff, fsdp, BLOCK, width).transpose(1, 0, 2, 3)).reshape(n_ff, BLOCK, width)
    return lax.psum(sums, both), *unpacked_qkv(first, second), ro, ri, rd


def one_kernel(inputs, first_values, cotangent, kseg, qrow, gain1, shift1, gain2, shift2, w_query, w_key, w_value, w_out, w_in, w_down):
    fsdp = lax.axis_size("fsdp")
    rows, width = w_query.shape
    vec = jnp.pad(jnp.stack([gain1, shift1, gain2, shift2]).astype(jnp.float32), ((0, 4), (0, width - rows)))
    vec = jnp.roll(vec, lax.axis_index("fsdp") * rows, axis=1)
    kseg = jnp.broadcast_to(kseg, (kseg.shape[0], BLOCK))
    outputs, input_grad, first_grad, rq, rk, rv, ro, ri, rd, sums = layer_call(
        fsdp, inputs, first_values, cotangent, vec, w_query, w_key, w_value, w_out, w_in, w_down, kseg, qrow
    )
    rq, rk, rv, ro, ri, rd = (a.reshape(*a.shape[:-4], -1, a.shape[-1]) for a in (rq, rk, rv, ro, ri, rd))
    return outputs, input_grad, first_grad, sums, rq, rk, rv[:, : width // 2], ro, ri, rd


def several_kernels(reach, inputs, first_values, cotangent, kseg, qrow, gain1, shift1, gain2, shift2, w_query, w_key, w_value, w_out, w_in, w_down):
    row_count, width = inputs.shape
    fsdp = lax.axis_size("fsdp")
    lnp, w1, w2, wo, win, wdn = gathered(fsdp, gain1, shift1, gain2, shift2, w_query, w_key, w_value, w_out, w_in, w_down)
    x = jnp.concatenate([shifted(inputs, "fsdp", d) for d in range(reach, 0, -1)] + [inputs], axis=0)
    fv = jnp.concatenate([shifted(first_values, "fsdp", d) for d in range(reach, 0, -1)] + [first_values], axis=0)
    n1, q, k, v, mixed, lse, resid, n2 = forward_call(fsdp, reach, x, fv, lnp, w1, w2, wo, kseg, qrow)
    outputs, gin, gdn, go, gres, gmixed, sums = mlp_call(n2, cotangent, resid, mixed, lnp, win, wdn, wo)
    dq, dk, dv, wk, wv = backward_call(fsdp, reach, q, k, v, gmixed, lse, kseg, qrow)
    for d in range(1, reach + 1):
        early = slice((reach - d) * row_count, (reach - d + 1) * row_count)
        both = shifted(jnp.concatenate([wk[early], wv[early]], axis=1), "fsdp", -d).astype(jnp.float32)
        dk, dv = dk + both[:, :width], dv + both[:, width:]
    input_grad, first_grad, g1, g2, sums = projection_back_call(fsdp, reach, x, n1, dq, dk, dv, lnp, w1, w2, gres, sums)
    return outputs, input_grad, first_grad, *reduced(fsdp, sums, g1, g2, go, gin, gdn)


def on_device(
    inputs,
    first_values,
    cotangent,
    tree_ids,
    segment_ids,
    path_table,
    attn_gain,
    attn_shift,
    w_query,
    w_key,
    w_value,
    w_out,
    mlp_gain,
    mlp_shift,
    w_in,
    w_down,
):
    row_count, width = inputs.shape
    fsdp = lax.axis_size("fsdp")
    reach = 0
    for device_pos in range(fsdp):
        offset = device_pos * row_count % TREE_LEN
        reach = max(reach, (offset + row_count - 1) // row_count)
    row_start = lax.axis_index("fsdp") * row_count
    kseg, qrow = segment_info(tree_ids, segment_ids, path_table, row_start, row_count, reach)
    weights = (attn_gain, attn_shift, mlp_gain, mlp_shift, w_query, w_key, w_value, w_out, w_in, w_down)
    if lax.axis_size("rep") == 8 and reach == 1 and row_count == width:
        results = one_kernel(inputs, first_values, cotangent, kseg, qrow, *weights)
    else:
        results = several_kernels(reach, inputs, first_values, cotangent, kseg, qrow, *weights)
    outputs, input_grad, first_grad, sums, d_q, d_k, d_v, d_o, d_in, d_dn = results
    rows = w_query.shape[0]
    sums = lax.dynamic_slice_in_dim(sums, lax.axis_index("fsdp") * rows, rows, 1)
    d_in = d_in.reshape(-1, rows, fsdp, BLOCK).transpose(1, 2, 0, 3).reshape(rows, -1)
    d_q, d_k, d_v, d_o, d_in, d_dn = (a.astype(jnp.float32) for a in (d_q, d_k, d_v, d_o, d_in, d_dn.reshape(-1, width)))
    return (outputs, input_grad, first_grad, sums[0], sums[1], d_q, d_k, d_v, d_o, sums[2], sums[3], d_in, d_dn)


def solution(mesh):
    placed = (
        P(("rep", "fsdp"), None),
        P(("rep", "fsdp"), None),
        P(("rep", "fsdp"), None),
        P("rep"),
        P("rep"),
        P("rep", None, None),
        P("fsdp"),
        P("fsdp"),
        P("fsdp", None),
        P("fsdp", None),
        P("fsdp", None),
        P("fsdp", None),
        P("fsdp"),
        P("fsdp"),
        P("fsdp", None),
        P("fsdp", None),
    )
    return jax.shard_map(
        on_device,
        mesh=mesh,
        in_specs=placed,
        out_specs=(
            P(("rep", "fsdp"), None),
            P(("rep", "fsdp"), None),
            P(("rep", "fsdp"), None),
            P("fsdp"),
            P("fsdp"),
            P("fsdp", None),
            P("fsdp", None),
            P("fsdp", None),
            P("fsdp", None),
            P("fsdp"),
            P("fsdp"),
            P("fsdp", None),
            P("fsdp", None),
        ),
        check_vma=False,
    )
```

```python
import functools

import jax
import jax.numpy as jnp
from jax import lax
from jax.experimental import pallas as pl
from jax.experimental.pallas import tpu as pltpu
from jax.sharding import PartitionSpec as P

MESH = pl.DeviceIdType.MESH

class Place:
    def __init__(self, fsdp):
        self.fsdp = fsdp
        r = lax.axis_index("rep")
        self.f = lax.axis_index("fsdp")
        self.k = lax.rem(r, 2)
        self.x = lax.rem(r // 2, 2)
        self.y = r // 4
        def rid(y, x, k): return (y * 2 + x) * 2 + k
        self.core = (rid(self.y, self.x, 1 - self.k), self.f)
        self.xn = (rid(self.y, 1 - self.x, self.k), self.f)
        self.yn = (rid(1 - self.y, self.x, self.k), self.f)
        self.r = r
        self.others = [lax.rem(self.f + j, fsdp) for j in range(1, fsdp)]
    def zdev(self, fo): return (self.r, fo)
    def barrier(self):
        bar = pltpu.get_barrier_semaphore()
        devs = [self.core, self.xn, self.yn] + [self.zdev(o) for o in self.others]
        for d in devs:
            pl.semaphore_signal(bar, inc=1, device_id=d, device_id_type=MESH)
        pl.semaphore_wait(bar, len(devs))

def drain(view, sem):
    pltpu.make_async_copy(view, view, sem).wait()

class Gather:
    def __init__(self, pc, buf, send, recv, xfirst):
        self.pc, self.buf, self.s, self.r, self.xf = pc, buf, send, recv, xfirst
        self.H = buf.shape[-1] // 2
        self.cols = pl.ds(pl.multiple_of(pc.k * self.H, 128), self.H)
    def push(self, view, stage, dev):
        pltpu.make_async_remote_copy(src_ref=view, dst_ref=view, send_sem=self.s.at[stage], recv_sem=self.r.at[stage], device_id=dev, device_id_type=MESH).start()
    def z_start(self):
        pc = self.pc
        v = self.buf.at[pc.f, pc.y, pc.x, :, self.cols]
        for o in pc.others: self.push(v, 0, pc.zdev(o))
    def three(self): return self.buf.at[pl.ds(0, self.pc.fsdp - 1), 0, 0, :, self.cols]
    def z_wait(self): drain(self.three(), self.r.at[0])
    def a_start(self):
        pc = self.pc
        for o in pc.others:
            v = self.buf.at[o, pc.y, pc.x, :, self.cols]
            self.push(v, 1, pc.xn); self.push(v, 2, pc.yn)
    def a_wait(self):
        drain(self.three(), self.r.at[1]); drain(self.three(), self.r.at[2])
    def b_start(self):
        pc = self.pc
        for o in pc.others:
            if self.xf: self.push(self.buf.at[o, 1 - pc.y, pc.x, :, self.cols], 3, pc.xn)
            else: self.push(self.buf.at[o, pc.y, 1 - pc.x, :, self.cols], 3, pc.yn)
    def b_wait(self): drain(self.three(), self.r.at[3])
    def c_start(self):
        pc = self.pc
        for o in pc.others: self.push(self.buf.at[o, :, :, :, self.cols], 4, pc.core)
    def big(self): return self.buf.at[pl.ds(0, self.pc.fsdp - 1), :, :, :, self.cols]
    def c_wait(self): drain(self.big(), self.r.at[4])
    def finish(self):
        for st in range(4): drain(self.three(), self.s.at[st])
        drain(self.big(), self.s.at[4])

Gather.STAGES = [
    lambda g: (g.z_wait(), g.a_start()),
    lambda g: (g.a_wait(), g.b_start()),
    lambda g: (g.b_wait(), g.c_start()),
    lambda g: (g.c_wait(), g.finish()),
]


class Reduce:
    def __init__(self, pc, buf, r1, r2, r3, r4, res, send, recv, xfirst):
        self.pc, self.buf, self.r1, self.r2, self.r3, self.r4, self.res = pc, buf, r1, r2, r3, r4, res
        self.s, self.r, self.xf = send, recv, xfirst
        self.H = H = buf.shape[-1] // 2
        self.cols = pl.ds(pl.multiple_of(pc.k * H, 128), H)
        self.ocols = pl.ds(pl.multiple_of((1 - pc.k) * H, 128), H)
        self.F = buf.shape[0]
    def send(self, src, dst, stage, dev):
        pltpu.make_async_remote_copy(src_ref=src, dst_ref=dst, send_sem=self.s.at[stage], recv_sem=self.r.at[stage], device_id=dev, device_id_type=MESH).start()
    def p1(self):
        self.send(self.buf.at[:, :, :, :, self.ocols], self.r1, 0, self.pc.core)
    def p2(self):
        pc = self.pc
        drain(self.r1, self.r.at[0])
        @pl.loop(0, self.F * 4)
        def _(i):
            a, b, c = i // 4, lax.rem(i // 2, 2), lax.rem(i, 2)
            self.r1[a, b, c] = self.r1[a, b, c] + self.buf[a, b, c, :, self.cols]
        if self.xf: self.send(self.r1.at[:, :, 1 - pc.x], self.r2, 1, pc.xn)
        else: self.send(self.r1.at[:, 1 - pc.y], self.r2, 1, pc.yn)
    def p3(self):
        pc = self.pc
        drain(self.r2, self.r.at[1])
        @pl.loop(0, self.F * 2)
        def _(i):
            a, b = i // 2, lax.rem(i, 2)
            mine = self.r1[a, b, pc.x] if self.xf else self.r1[a, pc.y, b]
            self.r2[a, b] = self.r2[a, b] + mine
        if self.xf: self.send(self.r2.at[:, 1 - pc.y], self.r3, 2, pc.yn)
        else: self.send(self.r2.at[:, 1 - pc.x], self.r3, 2, pc.xn)
    def p4(self):
        pc = self.pc
        drain(self.r3, self.r.at[2])
        q = pc.y if self.xf else pc.x
        @pl.loop(0, self.F)
        def _(a):
            self.r3[a] = self.r3[a] + self.r2[a, q]
        for o in pc.others: self.send(self.r3.at[o], self.r4.at[pc.f], 3, pc.zdev(o))
    def p5(self):
        pc = self.pc
        drain(self.r4.at[pl.ds(0, self.F - 1)], self.r.at[3])
        tot = self.r3[pc.f].astype(jnp.float32)
        for o in pc.others: tot = tot + self.r4[o].astype(jnp.float32)
        self.res[pc.y, pc.x, :, self.cols] = tot.astype(jnp.bfloat16)
        v = self.res.at[pc.y, pc.x, :, self.cols]
        self.send(v, v, 4, pc.xn); self.send(v, v, 5, pc.yn)
    def p6(self):
        pc = self.pc
        v = self.res.at[0, 0, :, self.cols]
        drain(v, self.r.at[4]); drain(v, self.r.at[5])
        if self.xf:
            v = self.res.at[1 - pc.y, pc.x, :, self.cols]; self.send(v, v, 6, pc.xn)
        else:
            v = self.res.at[pc.y, 1 - pc.x, :, self.cols]; self.send(v, v, 6, pc.yn)
    def p7(self):
        drain(self.res.at[0, 0, :, self.cols], self.r.at[6])
        v = self.res.at[:, :, :, self.cols]
        self.send(v, v, 7, self.pc.core)
    def p8(self):
        drain(self.res.at[:, :, :, self.cols], self.r.at[7])
    def finish(self):
        drain(self.r1, self.s.at[0]); drain(self.r2, self.s.at[1]); drain(self.r3, self.s.at[2])
        drain(self.r4.at[pl.ds(0, self.F - 1)], self.s.at[3])
        v = self.res.at[0, 0, :, self.cols]
        for i in (4, 5, 6): drain(v, self.s.at[i])
        drain(self.res.at[:, :, :, self.cols], self.s.at[7])

Reduce.STAGES = [Reduce.p1, Reduce.p2, Reduce.p3, Reduce.p4, Reduce.p5, Reduce.p6, Reduce.p7, Reduce.p8]

def red_shapes(shape):
    f, _, _, m, c = shape
    return (f, 2, 2, m, c // 2), (f, 2, m, c // 2), (f, m, c // 2), (f, m, c // 2)


HEAD = 64
BLOCK = 128
TRUNK = 512
TREE_LEN = 1024


epsilon = 1e-05
far_below = -1e30


def nt(a, b):
    return lax.dot_general(a, b, (((1,), (1,)), ((), ())), preferred_element_type=jnp.float32)


def tn(a, b):
    return lax.dot_general(a, b, (((0,), (0,)), ((), ())), preferred_element_type=jnp.float32)


def mm(a, b):
    return jnp.dot(a, b, preferred_element_type=jnp.float32)


def bf(a):
    return a.astype(jnp.bfloat16)


def f32(a):
    return a.astype(jnp.float32)


def row_tiles(rows):
    return 256 if rows % 256 == 0 else 128


def normalized(v):
    center = v - jnp.mean(v, axis=1, keepdims=True)
    inv = lax.rsqrt(jnp.mean(center * center, axis=1, keepdims=True) + epsilon)
    return center * inv, inv


class Span:
    def __init__(self, fsdp, rows, reach, f):
        self.rows, self.reach, self.f = rows, reach, f
        self.window = reach * rows
        self.blocks = rows // BLOCK
        self.first = f * self.blocks
        tree = TREE_LEN // BLOCK
        self.tree = tree
        self.start = (self.first // tree) * TREE_LEN - f * rows + self.window

    def kind(self, i):
        return lax.rem(self.first + i, self.tree)

    def base(self, i):
        return pl.multiple_of(((self.first + i) // self.tree) * TREE_LEN - self.f * self.rows + self.window, BLOCK)


def rows_at(start, size):
    return pl.ds(pl.multiple_of(start, BLOCK), size)


def make_bias(span, segs, trees, table, bias, extra=0):
    @pl.loop(0, span.blocks + extra)
    def _(i):
        b = span.kind(i)
        first = ((span.first + i) // span.tree) * span.tree
        q_pos = b * BLOCK + lax.broadcasted_iota(jnp.int32, (1, BLOCK), 1)
        own = segs[pl.ds(span.first + i, 1), :]

        def put(slot, key, related):
            k_pos = key * BLOCK + lax.broadcasted_iota(jnp.int32, (BLOCK, 1), 0)
            column = jnp.broadcast_to(f32(segs[pl.ds(first + key, 1), :]), (BLOCK, BLOCK)).T
            seen = (k_pos <= q_pos) & (column == f32(related))
            bias[i, pl.ds(slot, BLOCK), :] = jnp.where(seen, 0.0, far_below)

        put(256, b, own)

        @pl.when(b >= 6)
        def _():
            tree = trees[first * BLOCK]
            parent = jnp.zeros_like(own)
            for leaf in range(table.shape[1]):
                parent = jnp.where(own == leaf, table[tree, leaf, 1], parent)
            put(0, 4, parent)
            put(BLOCK, 5, parent)


def by_kind(b, body, lent=None):
    for n in range(TRUNK // BLOCK):

        @pl.when(b == n)
        def _():
            body([(0, n * BLOCK, None)][: n] + [(None, BLOCK, 256)])

    @pl.when((b >= 4) & (b < 6))
    def _():
        body([(0, 512, None), (None, BLOCK, 256)])

    leaf_parts = [(0, 512, None), (512, 256, 0), (None, BLOCK, 256)]
    if lent is None:

        @pl.when(b >= 6)
        def _():
            body(leaf_parts)

    else:

        @pl.when((b >= 6) & jnp.logical_not(lent))
        def _():
            body(leaf_parts)

        @pl.when((b >= 6) & lent)
        def _():
            body(leaf_parts, only_own=True)


def stacked(pair):
    low = lax.broadcasted_iota(jnp.int32, (1, 2 * HEAD), 1) < HEAD
    zero = jnp.zeros_like(pair)
    return jnp.concatenate([jnp.where(low, pair, zero), jnp.where(low, zero, pair)], axis=0)


def unstacked_t(wide):
    both = jnp.concatenate([wide[:HEAD, :BLOCK], wide[HEAD:, BLOCK:]], axis=0)
    return both.T


def part_rows(span, i, b, part):
    key, count, slot = part
    return rows_at(span.base(i) + (b * BLOCK if key is None else key), count)


def part_scores(q2, k, bias, i, part):
    s = nt(k, q2)
    slot = part[2]
    if slot is not None:
        one = bias[i, pl.ds(slot, part[1]), :]
        s = s + jnp.concatenate([one, one], axis=1)
    return s


def pair_cols(p):
    return pl.ds(pl.multiple_of(p * 2 * HEAD, 2 * HEAD), 2 * HEAD)


def transpose_pair(src, p, start, stop, dst):
    @pl.loop(start // BLOCK, stop // BLOCK)
    def _(j):
        dst[:, pl.ds(pl.multiple_of(j * BLOCK, BLOCK), BLOCK)] = src[rows_at(j * BLOCK, BLOCK), pair_cols(p)].T


def attend_pair(span, p, lo, hi, start, stop, q, k, v, bias, v_t, mixed, lse):
    transpose_pair(v, p, start, stop, v_t)
    cols = pair_cols(p)

    @pl.loop(lo, hi)
    def _(i):
        b = span.kind(i)
        own = rows_at(i * BLOCK, BLOCK)
        q2 = stacked(q[own, cols])

        def body(parts):
            rows = [part_rows(span, i, b, part) for part in parts]
            scores = [part_scores(q2, k[r, cols], bias, i, part) for r, part in zip(rows, parts)]
            top = functools.reduce(jnp.maximum, [jnp.max(s, axis=0, keepdims=True) for s in scores])
            expo = [jnp.exp(s - top) for s in scores]
            total = sum(jnp.sum(e, axis=0, keepdims=True) for e in expo)
            inv = 1.0 / total
            out = sum(mm(v_t[:, r], bf(e * inv)) for r, e in zip(rows, expo))
            mixed[own, cols] = bf(unstacked_t(out))
            lse[p, pl.ds(i, 1), :] = top + jnp.log(total)

        by_kind(b, body)


def norm_tile(x, gain, shift):
    hat, _ = normalized(f32(x))
    return bf(hat * gain + shift)


def project(span, x, fv, lnp, w1, w2, n1, q, k, v):
    gain, shift = lnp[0:1, :], lnp[1:2, :]
    tile = row_tiles(span.rows)
    third = w1.shape[1] // 4
    half = 2 * third
    scale = HEAD ** (-0.5)

    @pl.loop(span.window // tile, (span.window + span.rows) // tile)
    def _(t):
        rows = rows_at(t * tile, tile)
        n = norm_tile(x[rows, :], gain, shift)
        own = rows_at(t * tile - span.window, tile)
        n1[own, :] = n
        a = mm(n, w1[...])
        q[own, :half] = bf(f32(bf(a[:, :half])) * scale)
        k[rows, :half] = bf(a[:, half:])
        a = mm(n, w2[...])
        q[own, half:] = bf(f32(bf(a[:, :third])) * scale)
        k[rows, half:] = bf(a[:, half:half + third])
        v[rows, :third] = bf(a[:, third:half])
        v[rows, third:third + BLOCK] = bf(a[:, half + third:half + third + BLOCK])
        v[rows, third + BLOCK:] = fv[rows, :]

    @pl.loop(span.start // tile, span.window // tile)
    def _(t):
        rows = rows_at(t * tile, tile)
        n = norm_tile(x[rows, :], gain, shift)
        k[rows, :half] = bf(mm(n, w1[:, half:]))
        a = mm(n, w2[:, third:])
        v[rows, :third] = bf(a[:, :third])
        k[rows, half:] = bf(a[:, third:half])
        v[rows, third:third + BLOCK] = bf(a[:, half:half + BLOCK])
        v[rows, third + BLOCK:] = fv[rows, :]


def branch_out(span, x, lnp, mixed, wo, resid, n2):
    gain, shift = lnp[2:3, :], lnp[3:4, :]
    tile = row_tiles(span.rows)

    @pl.loop(0, span.rows // tile)
    def _(t):
        rows = rows_at(t * tile, tile)
        r = f32(x[rows_at(span.window + t * tile, tile), :]) + mm(mixed[rows, :], wo[...])
        resid[rows, :] = r
        hat, _ = normalized(r)
        n2[rows, :] = bf(hat * gain + shift)


def forward_kernel(fsdp, reach, x, fv, lnp, w1, w2, wo, segs, trees, table, n1, q, k, v, mixed, lse, resid, n2, bias, v_t):
    span = Span(fsdp, q.shape[0], reach, lax.axis_index("fsdp"))
    rows = q.shape[0]
    make_bias(span, segs, trees, table, bias)
    project(span, x, fv, lnp, w1, w2, n1, q, k, v)

    @pl.loop(0, q.shape[1] // (2 * HEAD))
    def _(p):
        attend_pair(span, p, 0, span.blocks, span.start, span.window + rows, q, k, v, bias, v_t, mixed, lse)

    branch_out(span, x, lnp, mixed, wo, resid, n2)


VM = pl.BlockSpec(memory_space=pltpu.VMEM)
SM = pl.BlockSpec(memory_space=pltpu.SMEM)


def forward_call(fsdp, reach, x, fv, lnp, w1, w2, wo, segs, trees, table):
    window, width = x.shape
    rows = window // (reach + 1)
    s = jax.ShapeDtypeStruct
    low, full = jnp.bfloat16, jnp.float32
    pairs, blocks = width // (2 * HEAD), rows // BLOCK
    outs = (
        s((rows, width), low), s((rows, width), low), s((window, width), low), s((window, width), low), s((rows, width), low),
        s((pairs, -(-blocks // 8) * 8, 2 * BLOCK), full), s((rows, width), full), s((rows, width), low),
    )
    return pl.pallas_call(
        functools.partial(forward_kernel, fsdp, reach),
        out_shape=outs, in_specs=[VM] * 7 + [SM] * 2, out_specs=[VM] * 8,
        scratch_shapes=[pltpu.VMEM((blocks, 3 * BLOCK, BLOCK), full), pltpu.VMEM((2 * HEAD, window), low)],
        compiler_params=pltpu.CompilerParams(vmem_limit_bytes=50 << 20),
    )(x, fv, lnp, w1, w2, wo, segs, trees, table)


GELU_A = 0.7978845608028654
GELU_B = 0.044715


def gelu_both(u):
    sq = u * u
    t = jnp.tanh(GELU_A * u * (1.0 + GELU_B * sq))
    half = 0.5 * (1.0 + t)
    slope = half + 0.5 * u * (1.0 - t * t) * (GELU_A * (1.0 + 3.0 * GELU_B * sq))
    return u * half, slope


def transpose_all(src, dst):
    cols = src.shape[1] // BLOCK

    @pl.loop(0, src.shape[0] // BLOCK)
    def _(j):
        rows = rows_at(j * BLOCK, BLOCK)
        for c in range(cols):
            dst[c * BLOCK:(c + 1) * BLOCK, rows] = src[rows, c * BLOCK:(c + 1) * BLOCK].T


def mlp_chunk(rows, n2, n2_t, cot, win, wdn, out_acc, gn2_acc, hid, gact, gin, gdn):
    tile = row_tiles(rows)

    @pl.loop(0, rows // tile)
    def _(t):
        r = rows_at(t * tile, tile)
        h, slope = gelu_both(mm(n2[r, :], win()))
        h = bf(h)
        hid[r, :] = h
        out_acc[r, :] += mm(h, wdn())
        g = bf(nt(cot[r, :], wdn()) * slope)
        gact[r, :] = g
        gn2_acc[r, :] += nt(g, win())

    gdn(bf(tn(hid[...], cot[...])))
    gin(bf(mm(n2_t[...], gact[...])))


def norm_back(hat, inv, grad, gain):
    e = grad * gain
    return inv * (e - jnp.mean(e, axis=1, keepdims=True) - hat * jnp.mean(e * hat, axis=1, keepdims=True))


def second_norm_back(rows, lnp, resid, cot, gn2, gres, gbranch, sums):
    tile = row_tiles(rows)
    sums[...] = jnp.zeros_like(sums)

    @pl.loop(0, rows // tile)
    def _(t):
        r = rows_at(t * tile, tile)
        hat, inv = normalized(resid[r, :])
        g = gn2[r, :]
        gr = f32(cot[r, :]) + norm_back(hat, inv, g, lnp[2:3, :])
        gres[r, :] = gr
        gbranch[r, :] = bf(gr)
        sums[2:3, :] += jnp.sum(g * hat, axis=0, keepdims=True)
        sums[3:4, :] += jnp.sum(g, axis=0, keepdims=True)


def branch_back(rows, gbranch, wo, gmixed):
    tile = row_tiles(rows)

    @pl.loop(0, rows // tile)
    def _(t):
        r = rows_at(t * tile, tile)
        gmixed[r, :] = bf(nt(gbranch[r, :], wo[...]))


def mlp_kernel(n2, cot, resid, mixed, lnp, win, wdn, wo, outputs, gin, gdn, go, gres, gmixed, sums, n2_t, out_acc, gn2_acc, hid, gact, gbranch):
    rows = n2.shape[0]
    transpose_all(n2, n2_t)
    out_acc[...] = resid[...]
    gn2_acc[...] = jnp.zeros_like(gn2_acc)

    @pl.loop(0, win.shape[0])
    def _(c):
        def put_in(v):
            gin[c] = v

        def put_dn(v):
            gdn[c] = v

        mlp_chunk(rows, n2, n2_t, cot, lambda: win[c], lambda: wdn[c], out_acc, gn2_acc, hid, gact, put_in, put_dn)

    outputs[...] = bf(out_acc[...])
    second_norm_back(rows, lnp, resid, cot, gn2_acc, gres, gbranch, sums)
    branch_back(rows, gbranch, wo, gmixed)
    go[...] = bf(tn(mixed[...], gbranch[...]))


def mlp_call(n2, cot, resid, mixed, lnp, win, wdn, wo):
    rows, width = n2.shape
    n_ff, _, cols = win.shape
    s, low, full = jax.ShapeDtypeStruct, jnp.bfloat16, jnp.float32
    outs = (
        s((rows, width), low), s(win.shape, low), s(wdn.shape, low), s((width, width), low), s((rows, width), full),
        s((rows, width), low), s((8, width), full),
    )
    return pl.pallas_call(
        mlp_kernel, out_shape=outs, in_specs=[VM] * 8, out_specs=[VM] * 7,
        scratch_shapes=[
            pltpu.VMEM((width, rows), low), pltpu.VMEM((rows, width), full), pltpu.VMEM((rows, width), full),
            pltpu.VMEM((rows, cols), low), pltpu.VMEM((rows, cols), low), pltpu.VMEM((rows, width), low),
        ],
        compiler_params=pltpu.CompilerParams(vmem_limit_bytes=58 << 20),
    )(n2, cot, resid, mixed, lnp, win, wdn, wo)


def attend_back_pair(span, p, q, k, v, gmixed, bias, lse, k_t, dk_acc, dv_acc, dq, lent=None):
    transpose_pair(k, p, span.start, span.window + span.rows, k_t)
    cols = pair_cols(p)

    @pl.loop(span.start // BLOCK, (span.window + span.rows) // BLOCK)
    def _(j):
        r = rows_at(j * BLOCK, BLOCK)
        dk_acc[r, :] = jnp.zeros((BLOCK, 2 * HEAD), jnp.float32)
        dv_acc[r, :] = jnp.zeros((BLOCK, 2 * HEAD), jnp.float32)

    @pl.loop(0, span.blocks)
    def _(i):
        b = span.kind(i)
        own = rows_at(i * BLOCK, BLOCK)
        q2, g2 = stacked(q[own, cols]), stacked(gmixed[own, cols])
        l = lse[p, pl.ds(i, 1), :]

        def body(parts, only_own=False):
            rows = [part_rows(span, i, b, part) for part in parts]
            probs = [jnp.exp(part_scores(q2, k[r, cols], bias, i, part) - l) for r, part in zip(rows, parts)]
            gw = [nt(v[r, cols], g2) for r in rows]
            inner = sum(jnp.sum(a * g, axis=0, keepdims=True) for a, g in zip(probs, gw))
            gs = [bf(a * (g - inner)) for a, g in zip(probs, gw)]
            out = sum(mm(k_t[:, r], g) for r, g in zip(rows, gs))
            dq[own, cols] = bf(unstacked_t(out) * HEAD ** (-0.5))
            for r, a, g, part in zip(rows, probs, gs, parts):
                if only_own and part[0] is not None:
                    continue
                dk_acc[r, :] += mm(g, q2)
                dv_acc[r, :] += mm(bf(a), g2)

        by_kind(b, body, None if lent is None else lent & (i < span.tree - 6))


def lent_sums(gmixed, mixed):
    heads = lax.broadcasted_iota(jnp.int32, (16, mixed.shape[1]), 0)
    cols = lax.broadcasted_iota(jnp.int32, (16, mixed.shape[1]), 1)
    pick = ((cols >= heads * HEAD) & (cols < heads * HEAD + HEAD)).astype(jnp.float32)
    return lax.dot_general(pick, f32(gmixed) * f32(mixed), (((1,), (1,)), ((), ())), precision=lax.Precision.HIGHEST, preferred_element_type=jnp.float32)


def borrowed_back(span, p, q, g, k, v, bias, lse, inner, dk, dv):
    cols = pair_cols(p)

    @pl.loop(0, 2)
    def _(j):
        r = rows_at(j * BLOCK, BLOCK)
        q2, g2 = stacked(q[r, cols]), stacked(g[r, cols])
        l = lse[p, pl.ds(j, 1), :]
        mean = inner[p, pl.ds(j, 1), :]
        for part in ((0, 512, None), (512, 256, 0)):
            rows = rows_at(span.window + part[0], part[1])
            own = rows_at(part[0], part[1])
            probs = jnp.exp(part_scores(q2, k[rows, cols], bias, span.blocks + j, part) - l)
            gs = bf(probs * (nt(v[rows, cols], g2) - mean))
            dk[own, cols] += mm(gs, q2)
            dv[own, cols] += mm(bf(probs), g2)


def backward_kernel(fsdp, reach, q, k, v, gmixed, lse, segs, trees, table, dq, dk, dv, wk, wv, bias, k_t, dk_acc, dv_acc):
    span = Span(fsdp, q.shape[0], reach, lax.axis_index("fsdp"))
    make_bias(span, segs, trees, table, bias)
    wk[...] = jnp.zeros_like(wk)
    wv[...] = jnp.zeros_like(wv)

    @pl.loop(0, q.shape[1] // (2 * HEAD))
    def _(p):
        cols = pair_cols(p)
        attend_back_pair(span, p, q, k, v, gmixed, bias, lse, k_t, dk_acc, dv_acc, dq)
        dk[:, cols] = dk_acc[span.window:, :]
        dv[:, cols] = dv_acc[span.window:, :]

        @pl.loop(span.start // BLOCK, span.window // BLOCK)
        def _(j):
            r = rows_at(j * BLOCK, BLOCK)
            wk[r, cols] = bf(dk_acc[r, :])
            wv[r, cols] = bf(dv_acc[r, :])


def backward_call(fsdp, reach, q, k, v, gmixed, lse, segs, trees, table):
    window, width = k.shape
    rows = q.shape[0]
    s, low, full = jax.ShapeDtypeStruct, jnp.bfloat16, jnp.float32
    early = window - rows
    outs = (s((rows, width), low), s((rows, width), full), s((rows, width), full), s((early, width), low), s((early, width), low))
    return pl.pallas_call(
        functools.partial(backward_kernel, fsdp, reach), out_shape=outs, in_specs=[VM] * 6 + [SM] * 2, out_specs=[VM] * 5,
        scratch_shapes=[
            pltpu.VMEM((rows // BLOCK, 3 * BLOCK, BLOCK), full), pltpu.VMEM((2 * HEAD, window), low),
            pltpu.VMEM((window, 2 * HEAD), full), pltpu.VMEM((window, 2 * HEAD), full),
        ],
        compiler_params=pltpu.CompilerParams(vmem_limit_bytes=58 << 20),
    )(q, k, v, gmixed, lse, segs, trees, table)


def projection_back(span, x, n1, dq, dk, dv, lnp, w1, w2, gres, gin, gfirst, g1, g2, sums, n1_t, cat1, cat2):
    rows = span.rows
    third = w1.shape[1] // 4
    half = 2 * third
    fresh = third + BLOCK
    tile = row_tiles(rows)
    transpose_all(n1, n1_t)

    @pl.loop(0, rows // tile)
    def _(t):
        r = rows_at(t * tile, tile)
        cat1[r, :half] = dq[r, :half]
        cat1[r, half:] = bf(dk[r, :half])
        cat2[r, :third] = dq[r, half:]
        cat2[r, third:half] = bf(dv[r, :third])
        cat2[r, half:half + third] = bf(dk[r, half:])
        cat2[r, half + third:half + third + BLOCK] = bf(dv[r, third:fresh])
        cat2[r, half + third + BLOCK:] = jnp.zeros((tile, BLOCK), jnp.bfloat16)
        gfirst[r, :] = dv[r, fresh:]

    g1[...] = bf(mm(n1_t[...], cat1[...]))
    g2[...] = bf(mm(n1_t[...], cat2[...]))

    @pl.loop(0, rows // tile)
    def _(t):
        r = rows_at(t * tile, tile)
        g = nt(cat1[r, :], w1[...]) + nt(cat2[r, :], w2[...])
        hat, inv = normalized(f32(x[rows_at(span.window + t * tile, tile), :]))
        gin[r, :] = gres[r, :] + norm_back(hat, inv, g, lnp[0:1, :])
        sums[0:1, :] += jnp.sum(g * hat, axis=0, keepdims=True)
        sums[1:2, :] += jnp.sum(g, axis=0, keepdims=True)


def projection_back_kernel(fsdp, reach, x, n1, dq, dk, dv, lnp, w1, w2, gres, sums_in, gin, gfirst, g1, g2, sums, n1_t, cat1, cat2):
    span = Span(fsdp, dq.shape[0], reach, lax.axis_index("fsdp"))
    sums[...] = sums_in[...]
    projection_back(span, x, n1, dq, dk, dv, lnp, w1, w2, gres, gin, gfirst, g1, g2, sums, n1_t, cat1, cat2)


def projection_back_call(fsdp, reach, x, n1, dq, dk, dv, lnp, w1, w2, gres, sums):
    rows, width = dq.shape
    s, low, full = jax.ShapeDtypeStruct, jnp.bfloat16, jnp.float32
    outs = (s((rows, width), full), s((rows, width // 2), full), s(w1.shape, low), s(w2.shape, low), s((8, width), full))
    return pl.pallas_call(
        functools.partial(projection_back_kernel, fsdp, reach), out_shape=outs, in_specs=[VM] * 10, out_specs=[VM] * 5,
        scratch_shapes=[pltpu.VMEM((width, rows), low), pltpu.VMEM((rows, w1.shape[1]), low), pltpu.VMEM((rows, w1.shape[1]), low)],
        compiler_params=pltpu.CompilerParams(vmem_limit_bytes=58 << 20),
    )(x, n1, dq, dk, dv, lnp, w1, w2, gres, sums)


def gather_steps(items, u):
    for s, stage in enumerate(Gather.STAGES):
        c = u - s

        @pl.when((c >= 0) & (c < items.count))
        def _():
            for g in items(c):
                stage(g)


def reduce_steps(items, u):
    for s, stage in enumerate(Reduce.STAGES):
        c = u - s

        @pl.when((c >= 0) & (c < items.count))
        def _():
            for g in items(c):
                stage(g)


class Chunks:
    def __init__(self, count, make):
        self.count, self.make = count, make

    def __call__(self, c):
        return self.make(c)


N_IN = 13


class Scratch:
    def __init__(self):
        self.names, self.shapes = [], []

    def add(self, name, shape):
        self.names.append(name)
        self.shapes.append(shape)

    def bind(self, refs):
        for name, ref in zip(self.names, refs):
            setattr(self, name, ref)
        return self


def layer_kernel(fsdp, n_ff, scratch, n_out, *refs):
    (inputs, first, cot_in, a_q, a_k, a_v, a_o, a_in, a_dn, norms, segs, trees, table) = refs[:N_IN]
    (outputs, gin, gfirst, rs_q, rs_k, rs_v, rs_o, rs_in, rs_dn, rs_vec) = refs[N_IN : N_IN + n_out]
    m = scratch.bind(refs[N_IN + n_out :])
    pc = Place(fsdp)
    f = pc.f
    rows, width = cot_in.shape
    span = Span(fsdp, rows, 1, f)
    tile = row_tiles(rows)
    tiles = rows // tile
    last = fsdp - 1
    flat = lambda ref: ref.reshape(-1, ref.shape[-1])
    w_q, w_k, w_v, w_o = (flat(b) for b in (m.b_q, m.b_k, m.b_v, m.b_o))
    mixed, cot = m.mixed.reshape(rows, width), m.cot.reshape(rows, width)
    x, q, k, v, n1, n2, tr = m.x, m.q, m.k, m.v, m.n1, m.n2, m.tr

    guest = span.kind(0) == 6
    host = (f < last) & (lax.rem(span.first + span.blocks, span.tree) == 6)
    gq, gg = x.at[pl.ds(0, 2 * BLOCK)], x.at[pl.ds(2 * BLOCK, 2 * BLOCK)]

    def lend(i, src, dst):
        return pltpu.make_async_remote_copy(src_ref=src, dst_ref=dst, send_sem=m.b_send.at[i], recv_sem=m.b_recv.at[i], device_id=(pc.r, f - 1), device_id_type=MESH)

    two = pl.ds(0, 2 * BLOCK)
    lent = [lambda: lend(0, q.at[two], gq), lambda: lend(1, m.lse, m.g_lse), lambda: lend(2, m.inner, m.g_inner)]

    def lent_pair(p):
        return lend(3 + p, m.gmixed.at[two, pair_cols(p)], gg.at[:, pair_cols(p)])

    def local(src, dst, sem):
        c = pltpu.make_async_copy(src, dst, sem)
        c.start()
        return c

    half = width // 2
    lw = [
        local(a, b.at[f, :, :, :, pl.ds(0, a.shape[-1])], m.l_sem.at[1 + i])
        for i, (a, b) in enumerate(((a_q, m.b_q), (a_k, m.b_k), (a_v, m.b_v), (a_o, m.b_o)))
    ]
    lx = local(inputs, x.at[pl.ds(rows, rows)], m.l_sem.at[5])
    lf = local(first, v.at[pl.ds(rows, rows), pl.ds(width // 2, width // 2)], m.l_sem.at[6])
    lc = local(cot_in, cot, m.l_sem.at[7])
    group = a_in.shape[-1] // fsdp

    def own_chunk(c, act):
        for g in range(fsdp):
            cols = pl.ds(pl.multiple_of(g * group + c * BLOCK, BLOCK), BLOCK)
            act(pltpu.make_async_copy(a_in.at[:, :, :, cols], m.b_in.at[c, f, :, :, :, pl.ds(g * BLOCK, BLOCK)], m.lc_sem.at[c, g]))
        act(pltpu.make_async_copy(a_dn.at[c], m.b_dn.at[c, f], m.lc_sem.at[c, fsdp]))

    @pl.loop(0, n_ff)
    def _(c):
        own_chunk(c, lambda d: d.start())

    pad = m.b_v.shape[-1] - half
    m.b_v[f, :, :, :, half:] = jnp.zeros((2, 2, m.b_v.shape[3], pad), jnp.bfloat16)
    own_norms = jnp.concatenate([f32(norms[...]), jnp.zeros((4, norms.shape[1]), jnp.float32)], axis=0)
    own_norms = jnp.concatenate([own_norms, jnp.zeros((8, width - norms.shape[1]), jnp.float32)], axis=1)
    m.vec[f] = pltpu.roll(own_norms, f * norms.shape[1], 1)
    pc.barrier()
    for o in pc.others:
        pltpu.make_async_remote_copy(
            src_ref=m.vec.at[f], dst_ref=m.vec.at[f], send_sem=m.v_send.at[0], recv_sem=m.v_recv.at[0], device_id=pc.zdev(o), device_id_type=MESH
        ).start()
    gat = [Gather(pc, b, m.g_send.at[i], m.g_recv.at[i], xf) for i, (b, xf) in enumerate(((m.b_q, True), (m.b_k, False), (m.b_v, True), (m.b_o, False)))]
    for l, g in zip(lw, gat):
        l.wait()
        g.z_start()

    next_start = Span(fsdp, rows, 1, f + 1).start

    def window(t):
        r, own = pl.ds(t * tile, tile), pl.ds(rows + t * tile, tile)
        nxt = (pc.r, f + 1)
        return [
            pltpu.make_async_remote_copy(src_ref=x.at[own], dst_ref=x.at[r], send_sem=m.w_send.at[0, t], recv_sem=m.w_recv.at[0, t], device_id=nxt, device_id_type=MESH),
            pltpu.make_async_remote_copy(
                src_ref=v.at[own, pl.ds(half, half)], dst_ref=v.at[r, pl.ds(half, half)], send_sem=m.w_send.at[1, t], recv_sem=m.w_recv.at[1, t], device_id=nxt, device_id_type=MESH
            ),
        ]

    ff = Chunks(
        n_ff,
        lambda c: [Gather(pc, m.b_in.at[c], m.gi_send.at[c], m.gi_recv.at[c], True), Gather(pc, m.b_dn.at[c], m.gd_send.at[c], m.gd_recv.at[c], False)],
    )

    make_bias(span, segs, trees, table, m.bias, jnp.where(host, 2, 0))
    for g in gat[:3]:
        g.z_wait()
        g.a_start()
    lx.wait()
    lf.wait()
    for t in range(tiles):

        @pl.when((f < last) & (t * tile >= next_start))
        def _():
            for c in window(t):
                c.start()

    v3 = m.vec.at[pl.ds(0, last)]
    drain(v3, m.v_recv.at[0])
    drain(v3, m.v_send.at[0])
    m.lnp[...] = functools.reduce(lambda a, b: a + b, [m.vec[j] for j in range(fsdp)])
    gain, shift = m.lnp[0:1, :], m.lnp[1:2, :]

    @pl.loop(0, tiles)
    def _(t):
        n1[rows_at(t * tile, tile), :] = norm_tile(x[rows_at(rows + t * tile, tile), :], gain, shift)

    for g in gat[:3]:
        g.a_wait()
        g.b_start()
    for g in gat[:3]:
        g.b_wait()
        g.c_start()
    for g in gat[:3]:
        g.c_wait()

    @pl.loop(0, tiles)
    def _(t):
        r, own = rows_at(rows + t * tile, tile), rows_at(t * tile, tile)
        n = n1[own, :]
        q[own, :] = bf(f32(bf(mm(n, w_q[...]))) * HEAD ** (-0.5))
        k[r, :] = bf(mm(n, w_k[...]))
        v[r, :half] = bf(mm(n, w_v[:, :half]))

    pairs = width // (2 * HEAD)
    here = lax.rem(span.tree - lax.rem(span.first, span.tree), span.tree)
    here = jnp.minimum(here, span.blocks)
    border = span.base(here)

    @pl.loop(0, pairs)
    def _(p):
        attend_pair(span, p, here, span.blocks, border, 2 * rows, q, k, v, m.bias, m.turned, mixed, m.lse)
        for when, step in ((0, lambda: (gat[3].z_wait(), gat[3].a_start())), (2, lambda: (gat[3].a_wait(), gat[3].b_start())), (4, lambda: (gat[3].b_wait(), gat[3].c_start()))):

            @pl.when(p == when)
            def _():
                step()

        @pl.when(p >= pairs // 2)
        def _():
            for j in range(2):
                c = 2 * (p - pairs // 2) + j
                own_chunk(c, lambda d: d.wait())
                for g in ff(c):
                    g.z_start()

    for t in range(tiles):

        @pl.when(t * tile >= span.start)
        def _():
            drain(x.at[pl.ds(t * tile, tile)], m.w_recv.at[0, t])
            drain(v.at[pl.ds(t * tile, tile), pl.ds(half, half)], m.w_recv.at[1, t])

    @pl.loop(span.start // tile, tiles)
    def _(t):
        r = rows_at(t * tile, tile)
        n = norm_tile(x[r, :], gain, shift)
        k[r, :] = bf(mm(n, w_k[...]))
        v[r, :half] = bf(mm(n, w_v[:, :half]))


    @pl.loop(0, pairs)
    def _(p):
        attend_pair(span, p, 0, here, span.start, border, q, k, v, m.bias, m.turned, mixed, m.lse)

        @pl.when(p >= pairs // 2)
        def _():
            gather_steps(ff, p - pairs // 2)

    @pl.when(guest)
    def _():
        lent[0]().start()
        lent[1]().start()

    gat[3].c_wait()
    branch_out(span, x, m.lnp, mixed, w_o, m.resid, n2)
    for g in gat:
        g.finish()

    lc.wait()
    transpose_all(n2, tr)
    m.acc1[...] = m.resid[...]
    m.acc2[...] = jnp.zeros_like(m.acc2)
    red = Chunks(
        n_ff,
        lambda c: [
            Reduce(pc, m.b_in.at[c], *(a.at[c] for a in m.r_in), rs_in.at[c], m.ri_send.at[c], m.ri_recv.at[c], True),
            Reduce(pc, m.b_dn.at[c], *(a.at[c] for a in m.r_dn), rs_dn.at[c], m.rd_send.at[c], m.rd_recv.at[c], False),
        ],
    )
    hid, gact = m.back.at[0, :, pl.ds(0, fsdp * BLOCK)], m.back.at[1, :, pl.ds(0, fsdp * BLOCK)]

    @pl.loop(0, n_ff)
    def _(c):
        gather_steps(ff, c + 3)
        b_in, b_dn = flat(m.b_in.at[c]), flat(m.b_dn.at[c])

        def put_in(val):
            b_in[...] = val

        def put_dn(val):
            b_dn[...] = val

        mlp_chunk(rows, n2, tr, cot, lambda: b_in[...], lambda: b_dn[...], m.acc1, m.acc2, hid, gact, put_in, put_dn)
        reduce_steps(red, c)

    @pl.loop(0, tiles)
    def _(t):
        r = rows_at(t * tile, tile)
        m.back[0, r, :] = bf(m.acc1[r, :])

    lo = local(m.back.at[0], outputs, m.l_sem.at[0])
    m.sums[...] = jnp.zeros_like(m.sums)
    second_norm_back(rows, m.lnp, m.resid, cot, m.acc2, m.resid, n2, m.sums)
    branch_back(rows, n2, w_o, m.gmixed)

    @pl.when(guest)
    def _():
        sums = lent_sums(m.gmixed[two, :], mixed[two, :])
        for p in range(pairs):
            for j in range(2):
                at = slice(j * BLOCK, (j + 1) * BLOCK)
                m.inner[p, j:j + 1, :] = jnp.concatenate([sums[2 * p:2 * p + 1, at], sums[2 * p + 1:2 * p + 2, at]], axis=1)
        lent[2]().start()
        for p in range(pairs):
            lent_pair(p).start()


    @pl.loop(0, width // tile)
    def _(t):
        r = rows_at(t * tile, tile)
        w_o[r, :] = bf(tn(mixed[:, pl.ds(pl.multiple_of(t * tile, tile), tile)], n2[...]))

    lo.wait()

    @pl.when((f < last) & jnp.logical_not(host))
    def _():
        pl.semaphore_signal(m.ready, inc=1, device_id=(pc.r, f + 1), device_id_type=MESH)

    for t in range(tiles):

        @pl.when((f < last) & (t * tile >= next_start))
        def _():
            for c in window(t):
                c.wait_send()

    @pl.when(guest)
    def _():
        lent[0]().wait_send()

    transpose_all(n1, tr)
    mid, end = half + (pairs // 2 - 1) * BLOCK, width
    wide = 2 * (mid - half)
    rest = lambda ref: (ref.at[..., pl.ds(0, wide)], ref.at[..., pl.ds(wide, 2 * BLOCK)])
    narrow = lambda refs, i: [ref.at[..., pl.ds(0, wide // 2) if i == 0 else pl.ds(wide // 2, BLOCK)] for ref in refs]
    buf1, buf2 = rest(m.cot)
    res1, res2 = rest(rs_k)
    stat = [
        Reduce(pc, b, *scr, res, m.rs_send.at[i], m.rs_recv.at[i], xf)
        for i, (b, scr, res, xf) in enumerate(
            (
                (m.b_o, m.r_o, rs_o, True), (m.mixed, m.r_q, rs_q, False), (m.g_v, m.r_v, rs_v, True),
                (buf1, narrow(m.r_k, 0), res1, True), (buf2, narrow(m.r_k, 1), res2, False),
            )
        )
    ]
    red_o, red_0, red_v, red_1, red_2 = stat

    def early(t, p):
        r, cols = pl.ds(t * tile, tile), pair_cols(p)
        prev = (pc.r, f - 1)
        return [
            pltpu.make_async_remote_copy(
                src_ref=x.at[pl.ds(j * rows + t * tile, tile), cols], dst_ref=m.back.at[j, r, cols], send_sem=m.e_send.at[j, p, t], recv_sem=m.e_recv.at[j, p, t],
                device_id=prev, device_id_type=MESH,
            )
            for j in range(2)
        ]

    dk, dv = m.acc1, m.acc2

    def complete(p):
        cols = pl.ds(p * BLOCK, BLOCK)
        for t in range(tiles):
            r = pl.ds(t * tile, tile)

            @pl.when((f < last) & jnp.logical_not(host) & (t * tile >= next_start))
            def _():
                for j, own in enumerate((dk, dv)):
                    drain(m.back.at[j, r, cols], m.e_recv.at[j, p, t])
                    own[r, cols] += f32(m.back[j, r, cols])

            k[r, cols] = bf(dk[r, cols])
            if p < pairs // 2:
                v[r, cols] = bf(dv[r, cols])

    def weight_grad(dst, at, grad, lo, hi):
        @pl.loop(0, width // tile)
        def _(t):
            r = rows_at(t * tile, tile)
            dst[r, at:at + hi - lo] = bf(mm(tr[r, :], grad[pl.ds(0, rows), lo:hi]))

    d_0, d_v, d_1 = flat(m.mixed), flat(m.g_v), flat(m.cot)

    def run_0():
        for p in range(pairs // 2):
            complete(p)
        weight_grad(d_0, 0, q, 0, half)
        weight_grad(d_0, half, k, 0, half)
        red_0.p1()
        d_v[:, half:] = jnp.zeros((width, d_v.shape[1] - half), jnp.bfloat16)
        weight_grad(d_v, 0, v, 0, half)
        red_v.p1()

    @pl.loop(0, pairs)
    def _(p):
        cols = pair_cols(p)
        attend_back_pair(span, p, q, k, v, m.gmixed, m.bias, m.lse, m.turned, m.dk_acc, m.dv_acc, q, guest)
        dk[:, cols] = m.dk_acc[rows:, :]
        dv[:, cols] = m.dv_acc[rows:, :]

        @pl.when((p == 0) & (f > 0) & jnp.logical_not(guest))
        def _():
            pl.semaphore_wait(m.ready, 1)

        for t in range(tiles):

            @pl.when((f > 0) & jnp.logical_not(guest) & (t * tile >= span.start))
            def _():
                r = pl.ds(t * tile, tile)
                x[r, cols] = bf(m.dk_acc[r, :])
                x[pl.ds(rows + t * tile, tile), cols] = bf(m.dv_acc[r, :])
                for c in early(t, p):
                    c.start()

        reduce_steps(red, n_ff + p)

        @pl.when(host)
        def _():
            @pl.when(p == 0)
            def _():
                for c in lent:
                    c().wait_recv()

            lent_pair(p).wait_recv()
            borrowed_back(span, p, gq, gg, k, v, m.bias, m.g_lse, m.g_inner, dk, dv)

        for s in range(6):

            @pl.when(p == s)
            def _():
                Reduce.STAGES[s](red_o)

        @pl.when(p == pairs - 2)
        def _():
            run_0()

        @pl.when(p == pairs - 1)
        def _():
            red_0.p2()
            red_v.p2()

    red_o.p7()
    for p in range(pairs // 2, pairs - 1):
        complete(p)
    weight_grad(d_1, 0, q, half, mid)
    weight_grad(d_1, mid - half, k, half, mid)
    red_1.p1()
    red_0.p3()
    red_v.p3()
    weight_grad(d_1, wide, q, mid, end)
    complete(pairs - 1)
    weight_grad(d_1, wide + BLOCK, k, mid, end)
    red_2.p1()
    gf = local(dv.at[:, pl.ds(half, half)], gfirst, m.l_sem.at[1])
    red_1.p2()
    for u in range(n_ff + pairs, n_ff + 7):
        reduce_steps(red, u)
    lx = local(inputs, n1, m.l_sem.at[2])
    red_2.p2()
    red_0.p4()
    red_v.p4()
    red_o.p8()

    @pl.loop(0, tiles)
    def _(t):
        r = rows_at(t * tile, tile)
        dk[r, :] = nt(q[r, :], w_q[...]) + nt(k[r, :], w_k[...]) + nt(v[r, :half], w_v[:, :half])

    red_1.p3()
    red_2.p3()
    lx.wait()

    @pl.loop(0, tiles)
    def _(t):
        r = rows_at(t * tile, tile)
        g = dk[r, :]
        hat, inv = normalized(f32(n1[r, :]))
        m.resid[r, :] += norm_back(hat, inv, g, m.lnp[0:1, :])
        m.sums[0:1, :] += jnp.sum(g * hat, axis=0, keepdims=True)
        m.sums[1:2, :] += jnp.sum(g, axis=0, keepdims=True)

    gi = local(m.resid, gin, m.l_sem.at[3])
    red_0.p5()
    red_v.p5()
    red_1.p4()
    red_2.p4()

    def exchange(src, dst, i, dev):
        c = pltpu.make_async_remote_copy(src_ref=src, dst_ref=dst, send_sem=m.v_send.at[i], recv_sem=m.v_recv.at[i], device_id=dev, device_id_type=MESH)
        c.start()
        return c

    cur = m.sums
    work = [
        (red_0.p6, red_v.p6, red_1.p5, red_2.p5), (red_0.p7, red_v.p7, red_1.p6, red_2.p6), (red_0.p8, red_v.p8, red_1.p7, red_2.p7),
    ]
    for i, dev in enumerate((pc.core, pc.xn, pc.yn)):
        c = exchange(cur, m.s_pair.at[i], 1 + i, dev)
        for step in work[i]:
            step()
        c.wait()
        m.s_pair[i] = m.s_pair[i] + cur[...]
        cur = m.s_pair.at[i]
    for o in pc.others:
        exchange(cur, m.s_z.at[f], 4, pc.zdev(o))
    red_1.p8()
    red_2.p8()
    z3 = m.s_z.at[pl.ds(0, last)]
    drain(z3, m.v_recv.at[4])
    drain(z3, m.v_send.at[4])
    m.s_z[f] = cur[...]
    rs_vec[...] = functools.reduce(lambda a, b: a + b, [m.s_z[j] for j in range(fsdp)])
    for g in stat:
        g.finish()

    @pl.loop(0, n_ff)
    def _(c):
        for g in red(c):
            g.finish()

    @pl.loop(0, pairs)
    def _(p):
        for t in range(tiles):

            @pl.when((f > 0) & jnp.logical_not(guest) & (t * tile >= span.start))
            def _():
                for c in early(t, p):
                    c.wait_send()

    @pl.when(guest)
    def _():
        for c in lent[1:]:
            c().wait_send()
        for p in range(pairs):
            lent_pair(p).wait_send()

    gf.wait()
    gi.wait()


def layer_call(fsdp, inputs, first, cot, norms, w_query, w_key, w_value, w_out, w_in, w_down, segs, trees, table):
    rows, width = inputs.shape
    shard = w_query.shape[0]
    n_ff = w_down.shape[0] // BLOCK
    low, full = jnp.bfloat16, jnp.float32
    mq, md = shard // 4, BLOCK // 4
    pairs, blocks = width // (2 * HEAD), rows // BLOCK
    wide_v = width // 2 + BLOCK
    split = lambda a: a.reshape(2, 2, mq, a.shape[1])
    buf = lambda m, c, lead=(): (*lead, fsdp, 2, 2, m, c)
    chunk = fsdp * BLOCK
    sc = Scratch()
    V, D = pltpu.VMEM, pltpu.SemaphoreType.DMA
    for name, shape in (
        ("b_q", buf(mq, width)), ("b_k", buf(mq, width)), ("b_v", buf(mq, wide_v)), ("b_o", buf(mq, width)),
        ("b_in", buf(mq, chunk, (n_ff,))), ("b_dn", buf(md, width, (n_ff,))), ("g_v", buf(mq, wide_v)),
        ("mixed", buf(mq, width)), ("cot", buf(mq, width)), ("x", (2 * rows, width)), ("k", (2 * rows, width)), ("v", (2 * rows, width)),
        ("q", (rows, width)), ("n1", (rows, width)), ("n2", (rows, width)), ("tr", (width, rows)), ("gmixed", (rows, width)), ("back", (2, rows, width)),
        ("turned", (2 * HEAD, 2 * rows)),
    ):
        sc.add(name, V(shape, low))
    for name, shape in (
        ("vec", (fsdp, 8, width)), ("lnp", (8, width)), ("sums", (8, width)), ("s_pair", (3, 8, width)), ("s_z", (fsdp, 8, width)),
        ("resid", (rows, width)), ("acc1", (rows, width)), ("acc2", (rows, width)), ("bias", (blocks + 2, 3 * BLOCK, BLOCK)), ("inner", (pairs, 8, 2 * BLOCK)), ("g_inner", (pairs, 8, 2 * BLOCK)), ("g_lse", (pairs, -(-blocks // 8) * 8, 2 * BLOCK)),
        ("dk_acc", (2 * rows, 2 * HEAD)), ("dv_acc", (2 * rows, 2 * HEAD)), ("lse", (pairs, -(-blocks // 8) * 8, 2 * BLOCK)),
    ):
        sc.add(name, V(shape, full))
    for name, shape in (
        ("l_sem", (9,)), ("lc_sem", (n_ff, fsdp + 1)), ("v_send", (5,)), ("v_recv", (5,)), ("g_send", (4, 5)), ("g_recv", (4, 5)),
        ("w_send", (2, rows // row_tiles(rows))), ("w_recv", (2, rows // row_tiles(rows))),
        ("gi_send", (n_ff, 5)), ("gi_recv", (n_ff, 5)), ("gd_send", (n_ff, 5)), ("gd_recv", (n_ff, 5)),
        ("ri_send", (n_ff, 8)), ("ri_recv", (n_ff, 8)), ("rd_send", (n_ff, 8)), ("rd_recv", (n_ff, 8)), ("rs_send", (5, 8)), ("rs_recv", (5, 8)),
        ("b_send", (3 + pairs,)), ("b_recv", (3 + pairs,)), ("e_send", (2, pairs, rows // row_tiles(rows))), ("e_recv", (2, pairs, rows // row_tiles(rows))),
    ):
        sc.add(name, D(shape))
    sc.add("ready", pltpu.SemaphoreType.REGULAR)
    groups = (("r_in", buf(mq, chunk), n_ff), ("r_dn", buf(md, width), n_ff), ("r_o", buf(mq, width), 0), ("r_q", buf(mq, width), 0), ("r_k", buf(mq, width), 0), ("r_v", buf(mq, wide_v), 0))
    for name, shape, lead in groups:
        for i, sub in enumerate(red_shapes(shape)):
            sc.add(f"{name}{i}", V((lead, *sub) if lead else sub, low))

    n_out = 10
    s = jax.ShapeDtypeStruct
    outs = (
        s((rows, width), low), s((rows, width), full), s((rows, width // 2), full),
        s((2, 2, mq, width), low), s((2, 2, mq, width), low), s((2, 2, mq, wide_v), low), s((2, 2, mq, width), low),
        s((n_ff, 2, 2, mq, chunk), low), s((n_ff, 2, 2, md, width), low), s((8, width), full),
    )

    def body(*refs):
        names = Scratch()
        names.names, names.shapes = sc.names, sc.shapes
        bound = names.bind(refs[N_IN + n_out :])
        for name, _, _ in groups:
            setattr(bound, name, [getattr(bound, f"{name}{i}") for i in range(4)])
        layer_kernel(fsdp, n_ff, bound, n_out, *refs)

    any_ = pl.BlockSpec(memory_space=pl.ANY)
    return pl.pallas_call(
        body, out_shape=outs, in_specs=[any_] * 9 + [VM] * 2 + [SM] * 2, out_specs=[any_] * 3 + [VM] * 7, scratch_shapes=sc.shapes,
        compiler_params=pltpu.CompilerParams(collective_id=3, has_side_effects=True, vmem_limit_bytes=61 << 20),
    )(inputs, first, cot, split(w_query), split(w_key), split(w_value), split(w_out), split(w_in), w_down.reshape(n_ff, 2, 2, md, width), norms, segs, trees, table)


def finish_kernel(o_in, g_in, f_in, vec, *refs):
    src, (o_out, g_out, f_out, *dst), rows_out = refs[:6], refs[6:15], refs[15]
    low, full, passed, sem, load = refs[16:22], refs[22:28], refs[28:31], refs[31], refs[32]
    copies = []

    def go(src, dst):
        c = pltpu.make_async_copy(src, dst, sem.at[len(copies)])
        c.start()
        copies.append(c)

    loads = [pltpu.make_async_copy(a, b, load.at[i]) for i, (a, b) in enumerate(zip((*src, g_in, o_in, f_in), (*low, *passed)))]
    for c in loads:
        c.start()
    (l_in, l_dn, l_0, l_1, l_o, l_v), (d_in, d_dn, d_q, d_k, d_o, d_v) = low, full

    def done(i, mid):
        go(mid, dst[i])

    n_ff, width = l_in.shape[0], l_0.shape[1]
    half = width // 2
    loads[0].wait()
    for j in range(n_ff):
        for g in range(l_in.shape[2] // BLOCK):
            at = (g * n_ff + j) * BLOCK
            d_in[:, at:at + BLOCK] = f32(l_in[j, :, g * BLOCK:(g + 1) * BLOCK])
    done(0, d_in)
    for c, a, b in zip(loads[6:], passed, (g_out, o_out, f_out)):
        c.wait()
        go(a, b)
    loads[1].wait()
    for j in range(n_ff):
        d_dn[j * BLOCK:(j + 1) * BLOCK, :] = f32(l_dn[j])
    done(1, d_dn)
    loads[2].wait()
    loads[3].wait()
    rest = half - BLOCK
    for i, mid in ((2, d_q), (3, d_k)):
        s = i - 2
        mid[:, :half] = f32(l_0[:, s * half:(s + 1) * half])
        mid[:, half:half + rest] = f32(l_1[:, s * rest:(s + 1) * rest])
        mid[:, half + rest:] = f32(l_1[:, 2 * rest + s * BLOCK:2 * rest + (s + 1) * BLOCK])
        done(i, mid)
    loads[4].wait()
    d_o[...] = f32(l_o[...])
    done(4, d_o)
    loads[5].wait()
    d_v[...] = f32(l_v[:, :half])
    done(5, d_v)
    rows, width = rows_out.shape[1], vec.shape[1]
    turned = pltpu.roll(vec[...], lax.rem(width - lax.axis_index("fsdp") * rows, width), 1)
    rows_out[...] = turned[:, :rows]
    for c in copies:
        c.wait()


def finish_call(outputs, gin, gfirst, rq, rk, rv, ro, ri, rd, vec):
    rows, width = rq.shape
    full = jnp.float32
    s = jax.ShapeDtypeStruct
    grads = (ri, rd, rq, rk, ro, rv)
    shapes = [(rows, ri.shape[0] * ri.shape[2]), (rd.shape[0] * BLOCK, width), (rows, width), (rows, width), (rows, width), (rows, width // 2)]
    hbm = pl.BlockSpec(memory_space=pltpu.HBM)
    out = pl.pallas_call(
        finish_kernel,
        out_shape=(s(outputs.shape, outputs.dtype), s(gin.shape, full), s(gfirst.shape, full), *(s(a, full) for a in shapes), s((8, rows), full)),
        in_specs=[hbm] * 3 + [VM] + [hbm] * 6, out_specs=[hbm] * 9 + [VM],
        scratch_shapes=[*(pltpu.VMEM(a.shape, a.dtype) for a in grads), *(pltpu.VMEM(a, full) for a in shapes), *(pltpu.VMEM(a.shape, a.dtype) for a in (gin, outputs, gfirst)), pltpu.SemaphoreType.DMA((9,)), pltpu.SemaphoreType.DMA((9,))],
        compiler_params=pltpu.CompilerParams(vmem_limit_bytes=61 << 20),
    )(outputs, gin, gfirst, vec, *grads)
    din, ddn, dq, dk, do, dv = out[3:9]
    return out[0], out[1], out[2], dq, dk, dv, do, din, ddn, out[9]


def shifted(block, axis, distance):
    devices = range(lax.axis_size(axis))
    route = [(i - distance, i) for i in devices if i - distance in devices]
    return lax.ppermute(block, axis, route)


def reorder_rows(grad_block, fsdp_count, rep_count):
    return grad_block.reshape(fsdp_count, rep_count, -1).transpose(1, 0, 2).reshape(-1)


def packed_qkv(query, key, value):
    h, pad = query.shape[1] * 2 // 3, jnp.zeros_like(value[:, : value.shape[1] // 3])
    n = value.shape[1] * 2 // 3
    return jnp.concatenate([query[:, :h], key[:, :h], query[:, h:], value[:, :n], key[:, h:], value[:, n:], pad], axis=1)


def unpacked_qkv(first, second):
    h = first.shape[-1] // 2
    q = h // 2
    return (
        jnp.concatenate([first[..., :h], second[..., :q]], axis=-1),
        jnp.concatenate([first[..., h:], second[..., h : h + q]], axis=-1),
        jnp.concatenate([second[..., q:h], second[..., h + q : h + q + q // 2]], axis=-1),
    )


def gathered(fsdp, gain1, shift1, gain2, shift2, w_query, w_key, w_value, w_out, w_in, w_down):
    width = w_query.shape[1]
    n_ff = w_down.shape[0] // BLOCK
    packed = packed_qkv(w_query, w_key, w_value)
    full = [lax.all_gather(v, "fsdp", axis=0, tiled=True) for v in (packed, w_out, w_in, w_down)]
    vec = lax.all_gather(jnp.stack([gain1, shift1, gain2, shift2]), "fsdp", axis=1, tiled=True).astype(jnp.float32)
    half = packed.shape[1] // 2
    inner = full[2].reshape(width, fsdp, n_ff, BLOCK).transpose(2, 0, 1, 3).reshape(n_ff, width, -1)
    down = full[3].reshape(fsdp, n_ff, BLOCK, width).transpose(1, 0, 2, 3).reshape(n_ff, -1, width)
    return jnp.pad(vec, ((0, 4), (0, 0))), full[0][:, :half], full[0][:, half:], full[1], inner, down


def reduced(fsdp, sums, g1, g2, go, gin, gdn):
    width = go.shape[0]
    rows = width // fsdp
    n_ff = gin.shape[0]
    both = ("rep", "fsdp")
    rep = lax.axis_size("rep")

    def total(a):
        piece = lax.psum_scatter(reorder_rows(a.astype(jnp.float32), fsdp, rep), both, scatter_dimension=0, tiled=True)
        return lax.all_gather(piece.astype(jnp.bfloat16), "rep", axis=0, tiled=True)

    first, second, ro = (total(a).reshape(rows, -1) for a in (g1, g2, go))
    ri = total(gin.transpose(1, 0, 2)).reshape(rows, n_ff, -1).transpose(1, 0, 2)
    rd = total(gdn.reshape(n_ff, fsdp, BLOCK, width).transpose(1, 0, 2, 3)).reshape(n_ff, BLOCK, width)
    return lax.psum(sums, both), *unpacked_qkv(first, second), ro, ri, rd


def one_kernel(inputs, first_values, cotangent, segs, trees, table, gain1, shift1, gain2, shift2, w_query, w_key, w_value, w_out, w_in, w_down):
    fsdp = lax.axis_size("fsdp")
    rows, width = w_query.shape
    norms = jnp.concatenate([gain1, shift1, gain2, shift2]).reshape(4, rows)
    outputs, input_grad, first_grad, rq, rk, rv, ro, ri, rd, sums = layer_call(
        fsdp, inputs, first_values, cotangent, norms, w_query, w_key, w_value, w_out, w_in, w_down, segs, trees, table
    )
    rq, rk, rv, ro, ri, rd = (a.reshape(*a.shape[:-4], -1, a.shape[-1]) for a in (rq, rk, rv, ro, ri, rd))
    outputs, input_grad, first_grad, rq, rk, rv, ro, ri, rd, sums = finish_call(outputs, input_grad, first_grad, rq, rk, rv, ro, ri, rd, sums)
    return outputs, input_grad, first_grad, sums[0], sums[1], rq, rk, rv, ro, sums[2], sums[3], ri, rd


def several_kernels(reach, inputs, first_values, cotangent, segs, trees, table, gain1, shift1, gain2, shift2, w_query, w_key, w_value, w_out, w_in, w_down):
    row_count, width = inputs.shape
    fsdp = lax.axis_size("fsdp")
    lnp, w1, w2, wo, win, wdn = gathered(fsdp, gain1, shift1, gain2, shift2, w_query, w_key, w_value, w_out, w_in, w_down)
    x = jnp.concatenate([shifted(inputs, "fsdp", d) for d in range(reach, 0, -1)] + [inputs], axis=0)
    fv = jnp.concatenate([shifted(first_values, "fsdp", d) for d in range(reach, 0, -1)] + [first_values], axis=0)
    n1, q, k, v, mixed, lse, resid, n2 = forward_call(fsdp, reach, x, fv, lnp, w1, w2, wo, segs, trees, table)
    outputs, gin, gdn, go, gres, gmixed, sums = mlp_call(n2, cotangent, resid, mixed, lnp, win, wdn, wo)
    dq, dk, dv, wk, wv = backward_call(fsdp, reach, q, k, v, gmixed, lse, segs, trees, table)
    for d in range(1, reach + 1):
        early = slice((reach - d) * row_count, (reach - d + 1) * row_count)
        both = shifted(jnp.concatenate([wk[early], wv[early]], axis=1), "fsdp", -d).astype(jnp.float32)
        dk, dv = dk + both[:, :width], dv + both[:, width:]
    input_grad, first_grad, g1, g2, sums = projection_back_call(fsdp, reach, x, n1, dq, dk, dv, lnp, w1, w2, gres, sums)
    return outputs, input_grad, first_grad, *reduced(fsdp, sums, g1, g2, go, gin, gdn)


def on_device(
    inputs,
    first_values,
    cotangent,
    tree_ids,
    segment_ids,
    path_table,
    attn_gain,
    attn_shift,
    w_query,
    w_key,
    w_value,
    w_out,
    mlp_gain,
    mlp_shift,
    w_in,
    w_down,
):
    row_count, width = inputs.shape
    fsdp = lax.axis_size("fsdp")
    reach = 0
    for device_pos in range(fsdp):
        offset = device_pos * row_count % TREE_LEN
        reach = max(reach, (offset + row_count - 1) // row_count)
    marks = (segment_ids.reshape(-1, BLOCK), tree_ids, path_table)
    weights = (attn_gain, attn_shift, mlp_gain, mlp_shift, w_query, w_key, w_value, w_out, w_in, w_down)
    if lax.axis_size("rep") == 8 and reach == 1 and row_count == width:
        return one_kernel(inputs, first_values, cotangent, *marks, *weights)
    results = several_kernels(reach, inputs, first_values, cotangent, *marks, *weights)
    outputs, input_grad, first_grad, sums, d_q, d_k, d_v, d_o, d_in, d_dn = results
    rows = w_query.shape[0]
    sums = lax.dynamic_slice_in_dim(sums, lax.axis_index("fsdp") * rows, rows, 1)
    d_in = d_in.reshape(-1, rows, fsdp, BLOCK).transpose(1, 2, 0, 3).reshape(rows, -1)
    d_q, d_k, d_v, d_o, d_in, d_dn = (a.astype(jnp.float32) for a in (d_q, d_k, d_v, d_o, d_in, d_dn.reshape(-1, width)))
    return (outputs, input_grad, first_grad, sums[0], sums[1], d_q, d_k, d_v, d_o, sums[2], sums[3], d_in, d_dn)


def solution(mesh):
    placed = (
        P(("rep", "fsdp"), None),
        P(("rep", "fsdp"), None),
        P(("rep", "fsdp"), None),
        P("rep"),
        P("rep"),
        P("rep", None, None),
        P("fsdp"),
        P("fsdp"),
        P("fsdp", None),
        P("fsdp", None),
        P("fsdp", None),
        P("fsdp", None),
        P("fsdp"),
        P("fsdp"),
        P("fsdp", None),
        P("fsdp", None),
    )
    return jax.shard_map(
        on_device,
        mesh=mesh,
        in_specs=placed,
        out_specs=(
            P(("rep", "fsdp"), None),
            P(("rep", "fsdp"), None),
            P(("rep", "fsdp"), None),
            P("fsdp"),
            P("fsdp"),
            P("fsdp", None),
            P("fsdp", None),
            P("fsdp", None),
            P("fsdp", None),
            P("fsdp"),
            P("fsdp"),
            P("fsdp", None),
            P("fsdp", None),
        ),
        check_vma=False,
    )
```

```python
import functools

import jax
import jax.numpy as jnp
from jax import lax
from jax.experimental import pallas as pl
from jax.experimental.pallas import tpu as pltpu
from jax.sharding import PartitionSpec as P

MESH = pl.DeviceIdType.MESH

class Place:
    def __init__(self, fsdp):
        self.fsdp = fsdp
        r = lax.axis_index("rep")
        self.f = lax.axis_index("fsdp")
        self.k = lax.rem(r, 2)
        self.x = lax.rem(r // 2, 2)
        self.y = r // 4
        def rid(y, x, k): return (y * 2 + x) * 2 + k
        self.core = (rid(self.y, self.x, 1 - self.k), self.f)
        self.xn = (rid(self.y, 1 - self.x, self.k), self.f)
        self.yn = (rid(1 - self.y, self.x, self.k), self.f)
        self.r = r
        self.others = [lax.rem(self.f + j, fsdp) for j in range(1, fsdp)]
    def zdev(self, fo): return (self.r, fo)
    def barrier(self):
        bar = pltpu.get_barrier_semaphore()
        devs = [self.core, self.xn, self.yn] + [self.zdev(o) for o in self.others]
        for d in devs:
            pl.semaphore_signal(bar, inc=1, device_id=d, device_id_type=MESH)
        pl.semaphore_wait(bar, len(devs))

def drain(view, sem):
    pltpu.make_async_copy(view, view, sem).wait()

class Gather:
    def __init__(self, pc, buf, send, recv, xfirst):
        self.pc, self.buf, self.s, self.r, self.xf = pc, buf, send, recv, xfirst
        self.H = buf.shape[-1] // 2
        self.cols = pl.ds(pl.multiple_of(pc.k * self.H, 128), self.H)
    def push(self, view, stage, dev):
        pltpu.make_async_remote_copy(src_ref=view, dst_ref=view, send_sem=self.s.at[stage], recv_sem=self.r.at[stage], device_id=dev, device_id_type=MESH).start()
    def z_start(self):
        pc = self.pc
        v = self.buf.at[pc.f, pc.y, pc.x, :, self.cols]
        for o in pc.others: self.push(v, 0, pc.zdev(o))
    def three(self): return self.buf.at[pl.ds(0, self.pc.fsdp - 1), 0, 0, :, self.cols]
    def z_wait(self): drain(self.three(), self.r.at[0])
    def a_start(self):
        pc = self.pc
        for o in pc.others:
            v = self.buf.at[o, pc.y, pc.x, :, self.cols]
            self.push(v, 1, pc.xn); self.push(v, 2, pc.yn)
    def a_wait(self):
        drain(self.three(), self.r.at[1]); drain(self.three(), self.r.at[2])
    def b_start(self):
        pc = self.pc
        for o in pc.others:
            if self.xf: self.push(self.buf.at[o, 1 - pc.y, pc.x, :, self.cols], 3, pc.xn)
            else: self.push(self.buf.at[o, pc.y, 1 - pc.x, :, self.cols], 3, pc.yn)
    def b_wait(self): drain(self.three(), self.r.at[3])
    def c_start(self):
        pc = self.pc
        for o in pc.others: self.push(self.buf.at[o, :, :, :, self.cols], 4, pc.core)
    def big(self): return self.buf.at[pl.ds(0, self.pc.fsdp - 1), :, :, :, self.cols]
    def c_wait(self): drain(self.big(), self.r.at[4])
    def finish(self):
        for st in range(4): drain(self.three(), self.s.at[st])
        drain(self.big(), self.s.at[4])

Gather.STAGES = [
    lambda g: (g.z_wait(), g.a_start()),
    lambda g: (g.a_wait(), g.b_start()),
    lambda g: (g.b_wait(), g.c_start()),
    lambda g: (g.c_wait(), g.finish()),
]


class Reduce:
    def __init__(self, pc, buf, r1, r2, r3, r4, res, send, recv, xfirst):
        self.pc, self.buf, self.r1, self.r2, self.r3, self.r4, self.res = pc, buf, r1, r2, r3, r4, res
        self.s, self.r, self.xf = send, recv, xfirst
        self.H = H = buf.shape[-1] // 2
        self.cols = pl.ds(pl.multiple_of(pc.k * H, 128), H)
        self.ocols = pl.ds(pl.multiple_of((1 - pc.k) * H, 128), H)
        self.F = buf.shape[0]
    def send(self, src, dst, stage, dev):
        pltpu.make_async_remote_copy(src_ref=src, dst_ref=dst, send_sem=self.s.at[stage], recv_sem=self.r.at[stage], device_id=dev, device_id_type=MESH).start()
    def p1(self):
        self.send(self.buf.at[:, :, :, :, self.ocols], self.r1, 0, self.pc.core)
    def p2(self):
        pc = self.pc
        drain(self.r1, self.r.at[0])
        @pl.loop(0, self.F * 4)
        def _(i):
            a, b, c = i // 4, lax.rem(i // 2, 2), lax.rem(i, 2)
            self.r1[a, b, c] = self.r1[a, b, c] + self.buf[a, b, c, :, self.cols]
        if self.xf: self.send(self.r1.at[:, :, 1 - pc.x], self.r2, 1, pc.xn)
        else: self.send(self.r1.at[:, 1 - pc.y], self.r2, 1, pc.yn)
    def p3(self):
        pc = self.pc
        drain(self.r2, self.r.at[1])
        @pl.loop(0, self.F * 2)
        def _(i):
            a, b = i // 2, lax.rem(i, 2)
            mine = self.r1[a, b, pc.x] if self.xf else self.r1[a, pc.y, b]
            self.r2[a, b] = self.r2[a, b] + mine
        if self.xf: self.send(self.r2.at[:, 1 - pc.y], self.r3, 2, pc.yn)
        else: self.send(self.r2.at[:, 1 - pc.x], self.r3, 2, pc.xn)
    def p4(self):
        pc = self.pc
        drain(self.r3, self.r.at[2])
        q = pc.y if self.xf else pc.x
        @pl.loop(0, self.F)
        def _(a):
            self.r3[a] = self.r3[a] + self.r2[a, q]
        for o in pc.others: self.send(self.r3.at[o], self.r4.at[pc.f], 3, pc.zdev(o))
    def p5(self):
        pc = self.pc
        drain(self.r4.at[pl.ds(0, self.F - 1)], self.r.at[3])
        tot = self.r3[pc.f].astype(jnp.float32)
        for o in pc.others: tot = tot + self.r4[o].astype(jnp.float32)
        self.res[pc.y, pc.x, :, self.cols] = tot.astype(jnp.bfloat16)
        v = self.res.at[pc.y, pc.x, :, self.cols]
        self.send(v, v, 4, pc.xn); self.send(v, v, 5, pc.yn)
    def p6(self):
        pc = self.pc
        v = self.res.at[0, 0, :, self.cols]
        drain(v, self.r.at[4]); drain(v, self.r.at[5])
        if self.xf:
            v = self.res.at[1 - pc.y, pc.x, :, self.cols]; self.send(v, v, 6, pc.xn)
        else:
            v = self.res.at[pc.y, 1 - pc.x, :, self.cols]; self.send(v, v, 6, pc.yn)
    def p7(self):
        drain(self.res.at[0, 0, :, self.cols], self.r.at[6])
        v = self.res.at[:, :, :, self.cols]
        self.send(v, v, 7, self.pc.core)
    def p8(self):
        drain(self.res.at[:, :, :, self.cols], self.r.at[7])
    def finish(self):
        drain(self.r1, self.s.at[0]); drain(self.r2, self.s.at[1]); drain(self.r3, self.s.at[2])
        drain(self.r4.at[pl.ds(0, self.F - 1)], self.s.at[3])
        v = self.res.at[0, 0, :, self.cols]
        for i in (4, 5, 6): drain(v, self.s.at[i])
        drain(self.res.at[:, :, :, self.cols], self.s.at[7])

Reduce.STAGES = [Reduce.p1, Reduce.p2, Reduce.p3, Reduce.p4, Reduce.p5, Reduce.p6, Reduce.p7, Reduce.p8]

def red_shapes(shape):
    f, _, _, m, c = shape
    return (f, 2, 2, m, c // 2), (f, 2, m, c // 2), (f, m, c // 2), (f, m, c // 2)


HEAD = 64
BLOCK = 128
TRUNK = 512
TREE_LEN = 1024


epsilon = 1e-05
far_below = -1e30


def nt(a, b):
    return lax.dot_general(a, b, (((1,), (1,)), ((), ())), preferred_element_type=jnp.float32)


def tn(a, b):
    return lax.dot_general(a, b, (((0,), (0,)), ((), ())), preferred_element_type=jnp.float32)


def mm(a, b):
    return jnp.dot(a, b, preferred_element_type=jnp.float32)


def bf(a):
    return a.astype(jnp.bfloat16)


def f32(a):
    return a.astype(jnp.float32)


def row_tiles(rows):
    return 256 if rows % 256 == 0 else 128


def normalized(v):
    center = v - jnp.mean(v, axis=1, keepdims=True)
    inv = lax.rsqrt(jnp.mean(center * center, axis=1, keepdims=True) + epsilon)
    return center * inv, inv


class Span:
    def __init__(self, fsdp, rows, reach, f):
        self.rows, self.reach, self.f = rows, reach, f
        self.window = reach * rows
        self.blocks = rows // BLOCK
        self.first = f * self.blocks
        tree = TREE_LEN // BLOCK
        self.tree = tree
        self.start = (self.first // tree) * TREE_LEN - f * rows + self.window

    def kind(self, i):
        return lax.rem(self.first + i, self.tree)

    def base(self, i):
        return pl.multiple_of(((self.first + i) // self.tree) * TREE_LEN - self.f * self.rows + self.window, BLOCK)


def rows_at(start, size):
    return pl.ds(pl.multiple_of(start, BLOCK), size)


def make_bias(span, segs, trees, table, bias, extra=0):
    @pl.loop(0, span.blocks + extra)
    def _(i):
        b = span.kind(i)
        first = ((span.first + i) // span.tree) * span.tree
        q_pos = b * BLOCK + lax.broadcasted_iota(jnp.int32, (1, BLOCK), 1)
        own = segs[pl.ds(span.first + i, 1), :]

        def put(slot, key, related):
            k_pos = key * BLOCK + lax.broadcasted_iota(jnp.int32, (BLOCK, 1), 0)
            column = jnp.broadcast_to(f32(segs[pl.ds(first + key, 1), :]), (BLOCK, BLOCK)).T
            seen = (k_pos <= q_pos) & (column == f32(related))
            bias[i, pl.ds(slot, BLOCK), :] = jnp.where(seen, 0.0, far_below)

        put(256, b, own)

        @pl.when(b >= 6)
        def _():
            tree = trees[first * BLOCK]
            parent = jnp.zeros_like(own)
            for leaf in range(table.shape[1]):
                parent = jnp.where(own == leaf, table[tree, leaf, 1], parent)
            put(0, 4, parent)
            put(BLOCK, 5, parent)


def by_kind(b, body, lent=None):
    for n in range(TRUNK // BLOCK):

        @pl.when(b == n)
        def _():
            body([(0, n * BLOCK, None)][: n] + [(None, BLOCK, 256)])

    @pl.when((b >= 4) & (b < 6))
    def _():
        body([(0, 512, None), (None, BLOCK, 256)])

    leaf_parts = [(0, 512, None), (512, 256, 0), (None, BLOCK, 256)]
    if lent is None:

        @pl.when(b >= 6)
        def _():
            body(leaf_parts)

    else:

        @pl.when((b >= 6) & jnp.logical_not(lent))
        def _():
            body(leaf_parts)

        @pl.when((b >= 6) & lent)
        def _():
            body(leaf_parts, only_own=True)


def stacked(pair):
    low = lax.broadcasted_iota(jnp.int32, (1, 2 * HEAD), 1) < HEAD
    zero = jnp.zeros_like(pair)
    return jnp.concatenate([jnp.where(low, pair, zero), jnp.where(low, zero, pair)], axis=0)


def unstacked_t(wide):
    both = jnp.concatenate([wide[:HEAD, :BLOCK], wide[HEAD:, BLOCK:]], axis=0)
    return both.T


def part_rows(span, i, b, part):
    key, count, slot = part
    return rows_at(span.base(i) + (b * BLOCK if key is None else key), count)


def part_scores(q2, k, bias, i, part):
    s = nt(k, q2)
    slot = part[2]
    if slot is not None:
        one = bias[i, pl.ds(slot, part[1]), :]
        s = s + jnp.concatenate([one, one], axis=1)
    return s


def pair_cols(p):
    return pl.ds(pl.multiple_of(p * 2 * HEAD, 2 * HEAD), 2 * HEAD)


def transpose_pair(src, p, start, stop, dst):
    step = row_tiles(src.shape[0])

    @pl.loop(start // step, stop // step)
    def _(j):
        dst[:, pl.ds(pl.multiple_of(j * step, step), step)] = src[rows_at(j * step, step), pair_cols(p)].T


def attend_pair(span, p, lo, hi, start, stop, q, k, v, bias, v_t, mixed, lse):
    transpose_pair(v, p, start, stop, v_t)
    cols = pair_cols(p)

    @pl.loop(lo, hi)
    def _(i):
        b = span.kind(i)
        own = rows_at(i * BLOCK, BLOCK)
        q2 = stacked(q[own, cols])

        def body(parts):
            rows = [part_rows(span, i, b, part) for part in parts]
            scores = [part_scores(q2, k[r, cols], bias, i, part) for r, part in zip(rows, parts)]
            top = functools.reduce(jnp.maximum, [jnp.max(s, axis=0, keepdims=True) for s in scores])
            expo = [jnp.exp(s - top) for s in scores]
            total = sum(jnp.sum(e, axis=0, keepdims=True) for e in expo)
            out = sum(mm(v_t[:, r], bf(e)) for r, e in zip(rows, expo))
            mixed[own, cols] = bf(unstacked_t(out * (1.0 / total)))
            lse[p, pl.ds(i, 1), :] = top + jnp.log(total)

        by_kind(b, body)


def norm_tile(x, gain, shift):
    hat, _ = normalized(f32(x))
    return bf(hat * gain + shift)


def project(span, x, fv, lnp, w1, w2, n1, q, k, v):
    gain, shift = lnp[0:1, :], lnp[1:2, :]
    tile = row_tiles(span.rows)
    third = w1.shape[1] // 4
    half = 2 * third
    scale = HEAD ** (-0.5)

    @pl.loop(span.window // tile, (span.window + span.rows) // tile)
    def _(t):
        rows = rows_at(t * tile, tile)
        n = norm_tile(x[rows, :], gain, shift)
        own = rows_at(t * tile - span.window, tile)
        n1[own, :] = n
        a = mm(n, w1[...])
        q[own, :half] = bf(f32(bf(a[:, :half])) * scale)
        k[rows, :half] = bf(a[:, half:])
        a = mm(n, w2[...])
        q[own, half:] = bf(f32(bf(a[:, :third])) * scale)
        k[rows, half:] = bf(a[:, half:half + third])
        v[rows, :third] = bf(a[:, third:half])
        v[rows, third:third + BLOCK] = bf(a[:, half + third:half + third + BLOCK])
        v[rows, third + BLOCK:] = fv[rows, :]

    @pl.loop(span.start // tile, span.window // tile)
    def _(t):
        rows = rows_at(t * tile, tile)
        n = norm_tile(x[rows, :], gain, shift)
        k[rows, :half] = bf(mm(n, w1[:, half:]))
        a = mm(n, w2[:, third:])
        v[rows, :third] = bf(a[:, :third])
        k[rows, half:] = bf(a[:, third:half])
        v[rows, third:third + BLOCK] = bf(a[:, half:half + BLOCK])
        v[rows, third + BLOCK:] = fv[rows, :]


def branch_out(span, x, lnp, mixed, wo, resid, n2):
    gain, shift = lnp[2:3, :], lnp[3:4, :]
    tile = row_tiles(span.rows)

    @pl.loop(0, span.rows // tile)
    def _(t):
        rows = rows_at(t * tile, tile)
        r = f32(x[rows_at(span.window + t * tile, tile), :]) + mm(mixed[rows, :], wo[...])
        resid[rows, :] = r
        hat, _ = normalized(r)
        n2[rows, :] = bf(hat * gain + shift)


def forward_kernel(fsdp, reach, x, fv, lnp, w1, w2, wo, segs, trees, table, n1, q, k, v, mixed, lse, resid, n2, bias, v_t):
    span = Span(fsdp, q.shape[0], reach, lax.axis_index("fsdp"))
    rows = q.shape[0]
    make_bias(span, segs, trees, table, bias)
    project(span, x, fv, lnp, w1, w2, n1, q, k, v)

    @pl.loop(0, q.shape[1] // (2 * HEAD))
    def _(p):
        attend_pair(span, p, 0, span.blocks, span.start, span.window + rows, q, k, v, bias, v_t, mixed, lse)

    branch_out(span, x, lnp, mixed, wo, resid, n2)


VM = pl.BlockSpec(memory_space=pltpu.VMEM)
SM = pl.BlockSpec(memory_space=pltpu.SMEM)


def forward_call(fsdp, reach, x, fv, lnp, w1, w2, wo, segs, trees, table):
    window, width = x.shape
    rows = window // (reach + 1)
    s = jax.ShapeDtypeStruct
    low, full = jnp.bfloat16, jnp.float32
    pairs, blocks = width // (2 * HEAD), rows // BLOCK
    outs = (
        s((rows, width), low), s((rows, width), low), s((window, width), low), s((window, width), low), s((rows, width), low),
        s((pairs, -(-blocks // 8) * 8, 2 * BLOCK), full), s((rows, width), full), s((rows, width), low),
    )
    return pl.pallas_call(
        functools.partial(forward_kernel, fsdp, reach),
        out_shape=outs, in_specs=[VM] * 7 + [SM] * 2, out_specs=[VM] * 8,
        scratch_shapes=[pltpu.VMEM((blocks, 3 * BLOCK, BLOCK), full), pltpu.VMEM((2 * HEAD, window), low)],
        compiler_params=pltpu.CompilerParams(vmem_limit_bytes=50 << 20),
    )(x, fv, lnp, w1, w2, wo, segs, trees, table)


GELU_A = 0.7978845608028654
GELU_B = 0.044715


def gelu_both(u):
    sq = u * u
    t = jnp.tanh(GELU_A * u * (1.0 + GELU_B * sq))
    half = 0.5 * (1.0 + t)
    slope = half + 0.5 * u * (1.0 - t * t) * (GELU_A * (1.0 + 3.0 * GELU_B * sq))
    return u * half, slope


def transpose_all(src, dst):
    cols = src.shape[1] // BLOCK

    @pl.loop(0, src.shape[0] // BLOCK)
    def _(j):
        rows = rows_at(j * BLOCK, BLOCK)
        for c in range(cols):
            dst[c * BLOCK:(c + 1) * BLOCK, rows] = src[rows, c * BLOCK:(c + 1) * BLOCK].T


def mlp_chunk(rows, n2, n2_t, cot, win, wdn, out_acc, gn2_acc, hid, gact, gin, gdn):
    tile = row_tiles(rows)

    @pl.loop(0, rows // tile)
    def _(t):
        r = rows_at(t * tile, tile)
        h, slope = gelu_both(mm(n2[r, :], win()))
        h = bf(h)
        hid[r, :] = h
        out_acc[r, :] += mm(h, wdn())
        g = bf(nt(cot[r, :], wdn()) * slope)
        gact[r, :] = g
        gn2_acc[r, :] += nt(g, win())

    gdn(bf(tn(hid[...], cot[...])))
    gin(bf(mm(n2_t[...], gact[...])))


def norm_back(hat, inv, grad, gain):
    e = grad * gain
    return inv * (e - jnp.mean(e, axis=1, keepdims=True) - hat * jnp.mean(e * hat, axis=1, keepdims=True))


def second_norm_back(rows, lnp, resid, cot, gn2, gres, gbranch, sums):
    tile = row_tiles(rows)
    sums[...] = jnp.zeros_like(sums)

    @pl.loop(0, rows // tile)
    def _(t):
        r = rows_at(t * tile, tile)
        hat, inv = normalized(resid[r, :])
        g = gn2[r, :]
        gr = f32(cot[r, :]) + norm_back(hat, inv, g, lnp[2:3, :])
        gres[r, :] = gr
        gbranch[r, :] = bf(gr)
        sums[2:3, :] += jnp.sum(g * hat, axis=0, keepdims=True)
        sums[3:4, :] += jnp.sum(g, axis=0, keepdims=True)


def branch_back(rows, gbranch, wo, gmixed):
    tile = row_tiles(rows)

    @pl.loop(0, rows // tile)
    def _(t):
        r = rows_at(t * tile, tile)
        gmixed[r, :] = bf(nt(gbranch[r, :], wo[...]))


def mlp_kernel(n2, cot, resid, mixed, lnp, win, wdn, wo, outputs, gin, gdn, go, gres, gmixed, sums, n2_t, out_acc, gn2_acc, hid, gact, gbranch):
    rows = n2.shape[0]
    transpose_all(n2, n2_t)
    out_acc[...] = resid[...]
    gn2_acc[...] = jnp.zeros_like(gn2_acc)

    @pl.loop(0, win.shape[0])
    def _(c):
        def put_in(v):
            gin[c] = v

        def put_dn(v):
            gdn[c] = v

        mlp_chunk(rows, n2, n2_t, cot, lambda: win[c], lambda: wdn[c], out_acc, gn2_acc, hid, gact, put_in, put_dn)

    outputs[...] = bf(out_acc[...])
    second_norm_back(rows, lnp, resid, cot, gn2_acc, gres, gbranch, sums)
    branch_back(rows, gbranch, wo, gmixed)
    go[...] = bf(tn(mixed[...], gbranch[...]))


def mlp_call(n2, cot, resid, mixed, lnp, win, wdn, wo):
    rows, width = n2.shape
    n_ff, _, cols = win.shape
    s, low, full = jax.ShapeDtypeStruct, jnp.bfloat16, jnp.float32
    outs = (
        s((rows, width), low), s(win.shape, low), s(wdn.shape, low), s((width, width), low), s((rows, width), full),
        s((rows, width), low), s((8, width), full),
    )
    return pl.pallas_call(
        mlp_kernel, out_shape=outs, in_specs=[VM] * 8, out_specs=[VM] * 7,
        scratch_shapes=[
            pltpu.VMEM((width, rows), low), pltpu.VMEM((rows, width), full), pltpu.VMEM((rows, width), full),
            pltpu.VMEM((rows, cols), low), pltpu.VMEM((rows, cols), low), pltpu.VMEM((rows, width), low),
        ],
        compiler_params=pltpu.CompilerParams(vmem_limit_bytes=58 << 20),
    )(n2, cot, resid, mixed, lnp, win, wdn, wo)


def attend_back_pair(span, p, q, k, v, gmixed, bias, lse, inner, k_t, dk_acc, dv_acc, dq, lent=None):
    transpose_pair(k, p, span.start, span.window + span.rows, k_t)
    cols = pair_cols(p)

    @pl.loop(span.start // BLOCK, (span.window + span.rows) // BLOCK)
    def _(j):
        r = rows_at(j * BLOCK, BLOCK)
        dk_acc[r, :] = jnp.zeros((BLOCK, 2 * HEAD), jnp.float32)
        dv_acc[r, :] = jnp.zeros((BLOCK, 2 * HEAD), jnp.float32)

    @pl.loop(0, span.blocks)
    def _(i):
        b = span.kind(i)
        own = rows_at(i * BLOCK, BLOCK)
        q2, g2 = stacked(q[own, cols]), stacked(gmixed[own, cols])
        l, mean = lse[p, pl.ds(i, 1), :], inner[p, pl.ds(i, 1), :]

        def body(parts, only_own=False):
            rows = [part_rows(span, i, b, part) for part in parts]
            probs = [jnp.exp(part_scores(q2, k[r, cols], bias, i, part) - l) for r, part in zip(rows, parts)]
            gs = [bf(a * (nt(v[r, cols], g2) - mean)) for a, r in zip(probs, rows)]
            out = sum(mm(k_t[:, r], g) for r, g in zip(rows, gs))
            dq[own, cols] = bf(unstacked_t(out) * HEAD ** (-0.5))
            for r, a, g, part in zip(rows, probs, gs, parts):
                if only_own and part[0] is not None:
                    continue
                dk_acc[r, :] += mm(g, q2)
                dv_acc[r, :] += mm(bf(a), g2)

        by_kind(b, body, None if lent is None else lent & (i < span.tree - 6))


def head_sums(gmixed, mixed, inner):
    width = mixed.shape[1]
    heads = lax.broadcasted_iota(jnp.int32, (16, width), 0)
    cols = lax.broadcasted_iota(jnp.int32, (16, width), 1)
    pick = bf(((cols >= heads * HEAD) & (cols < heads * HEAD + HEAD)).astype(jnp.float32))
    tile = row_tiles(mixed.shape[0])
    for t in range(mixed.shape[0] // tile):
        r = slice(t * tile, (t + 1) * tile)
        each = f32(gmixed[r, :]) * f32(mixed[r, :])
        high = bf(each)
        sums = nt(pick, high) + nt(pick, bf(each - f32(high)))
        for j in range(tile // BLOCK):
            at, i = slice(j * BLOCK, (j + 1) * BLOCK), t * (tile // BLOCK) + j
            for p in range(width // (2 * HEAD)):
                inner[p, i:i + 1, :] = jnp.concatenate([sums[2 * p:2 * p + 1, at], sums[2 * p + 1:2 * p + 2, at]], axis=1)


def borrowed_back(span, p, q, g, k, v, bias, lse, inner, dk, dv):
    cols = pair_cols(p)

    @pl.loop(0, 2)
    def _(j):
        r = rows_at(j * BLOCK, BLOCK)
        q2, g2 = stacked(q[r, cols]), stacked(g[r, cols])
        l = lse[p, pl.ds(j, 1), :]
        mean = inner[p, pl.ds(j, 1), :]
        for part in ((0, 512, None), (512, 256, 0)):
            rows = rows_at(span.window + part[0], part[1])
            own = rows_at(part[0], part[1])
            probs = jnp.exp(part_scores(q2, k[rows, cols], bias, span.blocks + j, part) - l)
            gs = bf(probs * (nt(v[rows, cols], g2) - mean))
            dk[own, cols] += mm(gs, q2)
            dv[own, cols] += mm(bf(probs), g2)


def backward_kernel(fsdp, reach, q, k, v, gmixed, mixed, lse, segs, trees, table, dq, dk, dv, wk, wv, bias, inner, k_t, dk_acc, dv_acc):
    span = Span(fsdp, q.shape[0], reach, lax.axis_index("fsdp"))
    make_bias(span, segs, trees, table, bias)
    head_sums(gmixed, mixed, inner)
    wk[...] = jnp.zeros_like(wk)
    wv[...] = jnp.zeros_like(wv)

    @pl.loop(0, q.shape[1] // (2 * HEAD))
    def _(p):
        cols = pair_cols(p)
        attend_back_pair(span, p, q, k, v, gmixed, bias, lse, inner, k_t, dk_acc, dv_acc, dq)
        dk[:, cols] = dk_acc[span.window:, :]
        dv[:, cols] = dv_acc[span.window:, :]

        @pl.loop(span.start // BLOCK, span.window // BLOCK)
        def _(j):
            r = rows_at(j * BLOCK, BLOCK)
            wk[r, cols] = bf(dk_acc[r, :])
            wv[r, cols] = bf(dv_acc[r, :])


def backward_call(fsdp, reach, q, k, v, gmixed, mixed, lse, segs, trees, table):
    window, width = k.shape
    rows = q.shape[0]
    s, low, full = jax.ShapeDtypeStruct, jnp.bfloat16, jnp.float32
    early = window - rows
    outs = (s((rows, width), low), s((rows, width), full), s((rows, width), full), s((early, width), low), s((early, width), low))
    return pl.pallas_call(
        functools.partial(backward_kernel, fsdp, reach), out_shape=outs, in_specs=[VM] * 7 + [SM] * 2, out_specs=[VM] * 5,
        scratch_shapes=[
            pltpu.VMEM((rows // BLOCK, 3 * BLOCK, BLOCK), full), pltpu.VMEM(lse.shape, full), pltpu.VMEM((2 * HEAD, window), low),
            pltpu.VMEM((window, 2 * HEAD), full), pltpu.VMEM((window, 2 * HEAD), full),
        ],
        compiler_params=pltpu.CompilerParams(vmem_limit_bytes=58 << 20),
    )(q, k, v, gmixed, mixed, lse, segs, trees, table)


def projection_back(span, x, n1, dq, dk, dv, lnp, w1, w2, gres, gin, gfirst, g1, g2, sums, n1_t, cat1, cat2):
    rows = span.rows
    third = w1.shape[1] // 4
    half = 2 * third
    fresh = third + BLOCK
    tile = row_tiles(rows)
    transpose_all(n1, n1_t)

    @pl.loop(0, rows // tile)
    def _(t):
        r = rows_at(t * tile, tile)
        cat1[r, :half] = dq[r, :half]
        cat1[r, half:] = bf(dk[r, :half])
        cat2[r, :third] = dq[r, half:]
        cat2[r, third:half] = bf(dv[r, :third])
        cat2[r, half:half + third] = bf(dk[r, half:])
        cat2[r, half + third:half + third + BLOCK] = bf(dv[r, third:fresh])
        cat2[r, half + third + BLOCK:] = jnp.zeros((tile, BLOCK), jnp.bfloat16)
        gfirst[r, :] = dv[r, fresh:]

    g1[...] = bf(mm(n1_t[...], cat1[...]))
    g2[...] = bf(mm(n1_t[...], cat2[...]))

    @pl.loop(0, rows // tile)
    def _(t):
        r = rows_at(t * tile, tile)
        g = nt(cat1[r, :], w1[...]) + nt(cat2[r, :], w2[...])
        hat, inv = normalized(f32(x[rows_at(span.window + t * tile, tile), :]))
        gin[r, :] = gres[r, :] + norm_back(hat, inv, g, lnp[0:1, :])
        sums[0:1, :] += jnp.sum(g * hat, axis=0, keepdims=True)
        sums[1:2, :] += jnp.sum(g, axis=0, keepdims=True)


def projection_back_kernel(fsdp, reach, x, n1, dq, dk, dv, lnp, w1, w2, gres, sums_in, gin, gfirst, g1, g2, sums, n1_t, cat1, cat2):
    span = Span(fsdp, dq.shape[0], reach, lax.axis_index("fsdp"))
    sums[...] = sums_in[...]
    projection_back(span, x, n1, dq, dk, dv, lnp, w1, w2, gres, gin, gfirst, g1, g2, sums, n1_t, cat1, cat2)


def projection_back_call(fsdp, reach, x, n1, dq, dk, dv, lnp, w1, w2, gres, sums):
    rows, width = dq.shape
    s, low, full = jax.ShapeDtypeStruct, jnp.bfloat16, jnp.float32
    outs = (s((rows, width), full), s((rows, width // 2), full), s(w1.shape, low), s(w2.shape, low), s((8, width), full))
    return pl.pallas_call(
        functools.partial(projection_back_kernel, fsdp, reach), out_shape=outs, in_specs=[VM] * 10, out_specs=[VM] * 5,
        scratch_shapes=[pltpu.VMEM((width, rows), low), pltpu.VMEM((rows, w1.shape[1]), low), pltpu.VMEM((rows, w1.shape[1]), low)],
        compiler_params=pltpu.CompilerParams(vmem_limit_bytes=58 << 20),
    )(x, n1, dq, dk, dv, lnp, w1, w2, gres, sums)


def gather_steps(items, u):
    for s, stage in enumerate(Gather.STAGES[:3]):
        c = u - s

        @pl.when((c >= 0) & (c < items.count))
        def _():
            for g in items(c):
                stage(g)


REDUCE_AT = (0, 1, 2, 3, 5, 6, 7)


def reduce_steps(items, u):
    for s, stage in enumerate(Reduce.STAGES[:7]):
        c = u - REDUCE_AT[s]

        @pl.when((c >= 0) & (c < items.count))
        def _():
            for g in items(c):
                stage(g)


class Chunks:
    def __init__(self, count, make):
        self.count, self.make = count, make

    def __call__(self, c):
        return self.make(c)


N_IN = 13


class Scratch:
    def __init__(self):
        self.names, self.shapes = [], []

    def add(self, name, shape):
        self.names.append(name)
        self.shapes.append(shape)

    def bind(self, refs):
        for name, ref in zip(self.names, refs):
            setattr(self, name, ref)
        return self


def layer_kernel(fsdp, n_ff, scratch, n_out, *refs):
    (inputs, first, cot_in, a_q, a_k, a_v, a_o, a_in, a_dn, norms, segs, trees, table) = refs[:N_IN]
    (outputs, gin, gfirst, rs_q, rs_k, rs_v, rs_o, rs_in, rs_dn, rs_vec) = refs[N_IN : N_IN + n_out]
    m = scratch.bind(refs[N_IN + n_out :])
    pc = Place(fsdp)
    f = pc.f
    rows, width = cot_in.shape
    span = Span(fsdp, rows, 1, f)
    tile = row_tiles(rows)
    tiles = rows // tile
    last = fsdp - 1
    flat = lambda ref: ref.reshape(-1, ref.shape[-1])
    w_q, w_k, w_v, w_o = (flat(b) for b in (m.b_q, m.b_k, m.b_v, m.b_o))
    mixed, cot = m.mixed.reshape(rows, width), m.cot.reshape(rows, width)
    x, q, k, v, n1, n2, tr = m.x, m.q, m.k, m.v, m.n1, m.n2, m.tr

    guest = span.kind(0) == 6
    host = (f < last) & (lax.rem(span.first + span.blocks, span.tree) == 6)
    gq, gg = x.at[pl.ds(0, 2 * BLOCK)], x.at[pl.ds(2 * BLOCK, 2 * BLOCK)]

    def lend(i, src, dst):
        return pltpu.make_async_remote_copy(src_ref=src, dst_ref=dst, send_sem=m.b_send.at[i], recv_sem=m.b_recv.at[i], device_id=(pc.r, f - 1), device_id_type=MESH)

    two = pl.ds(0, 2 * BLOCK)
    lent = [lambda: lend(0, q.at[two], gq), lambda: lend(1, m.lse, m.g_lse), lambda: lend(2, m.inner, m.g_inner)]

    def lent_pair(p):
        return lend(3 + p, m.gmixed.at[two, pair_cols(p)], gg.at[:, pair_cols(p)])

    def local(src, dst, sem):
        c = pltpu.make_async_copy(src, dst, sem)
        c.start()
        return c

    half = width // 2
    lw = [
        local(a, b.at[f, :, :, :, pl.ds(0, a.shape[-1])], m.l_sem.at[1 + i])
        for i, (a, b) in enumerate(((a_q, m.b_q), (a_k, m.b_k), (a_v, m.b_v), (a_o, m.b_o)))
    ]
    lx = local(inputs, x.at[pl.ds(rows, rows)], m.l_sem.at[5])
    lf = local(first, v.at[pl.ds(rows, rows), pl.ds(width // 2, width // 2)], m.l_sem.at[6])
    lc = local(cot_in, cot, m.l_sem.at[7])
    group = a_in.shape[-1] // fsdp

    def own_chunk(c, act):
        for g in range(fsdp):
            cols = pl.ds(pl.multiple_of(g * group + c * BLOCK, BLOCK), BLOCK)
            act(pltpu.make_async_copy(a_in.at[:, :, :, cols], m.b_in.at[c, f, :, :, :, pl.ds(g * BLOCK, BLOCK)], m.lc_sem.at[c, g]))
        act(pltpu.make_async_copy(a_dn.at[c], m.b_dn.at[c, f], m.lc_sem.at[c, fsdp]))

    @pl.loop(0, n_ff)
    def _(c):
        own_chunk(c, lambda d: d.start())

    pad = m.b_v.shape[-1] - half
    m.b_v[f, :, :, :, half:] = jnp.zeros((2, 2, m.b_v.shape[3], pad), jnp.bfloat16)
    own_norms = jnp.concatenate([f32(norms[...]), jnp.zeros((4, norms.shape[1]), jnp.float32)], axis=0)
    own_norms = jnp.concatenate([own_norms, jnp.zeros((8, width - norms.shape[1]), jnp.float32)], axis=1)
    m.vec[f] = pltpu.roll(own_norms, f * norms.shape[1], 1)
    pc.barrier()
    for o in pc.others:
        pltpu.make_async_remote_copy(
            src_ref=m.vec.at[f], dst_ref=m.vec.at[f], send_sem=m.v_send.at[0], recv_sem=m.v_recv.at[0], device_id=pc.zdev(o), device_id_type=MESH
        ).start()
    gat = [Gather(pc, b, m.g_send.at[i], m.g_recv.at[i], xf) for i, (b, xf) in enumerate(((m.b_q, True), (m.b_k, False), (m.b_v, True), (m.b_o, False)))]
    for l, g in zip(lw, gat):
        l.wait()
        g.z_start()

    next_start = Span(fsdp, rows, 1, f + 1).start

    def window(t):
        r, own = pl.ds(t * tile, tile), pl.ds(rows + t * tile, tile)
        nxt = (pc.r, f + 1)
        return [
            pltpu.make_async_remote_copy(src_ref=x.at[own], dst_ref=x.at[r], send_sem=m.w_send.at[0, t], recv_sem=m.w_recv.at[0, t], device_id=nxt, device_id_type=MESH),
            pltpu.make_async_remote_copy(
                src_ref=v.at[own, pl.ds(half, half)], dst_ref=v.at[r, pl.ds(half, half)], send_sem=m.w_send.at[1, t], recv_sem=m.w_recv.at[1, t], device_id=nxt, device_id_type=MESH
            ),
        ]

    ff = Chunks(
        n_ff,
        lambda c: [Gather(pc, m.b_in.at[c], m.gi_send.at[c], m.gi_recv.at[c], True), Gather(pc, m.b_dn.at[c], m.gd_send.at[c], m.gd_recv.at[c], False)],
    )

    make_bias(span, segs, trees, table, m.bias, jnp.where(host, 2, 0))
    for g in gat[:3]:
        g.z_wait()
        g.a_start()
    lx.wait()
    lf.wait()
    for t in range(tiles):

        @pl.when((f < last) & (t * tile >= next_start))
        def _():
            for c in window(t):
                c.start()

    v3 = m.vec.at[pl.ds(0, last)]
    drain(v3, m.v_recv.at[0])
    drain(v3, m.v_send.at[0])
    m.lnp[...] = functools.reduce(lambda a, b: a + b, [m.vec[j] for j in range(fsdp)])
    gain, shift = m.lnp[0:1, :], m.lnp[1:2, :]

    @pl.loop(0, tiles)
    def _(t):
        n1[rows_at(t * tile, tile), :] = norm_tile(x[rows_at(rows + t * tile, tile), :], gain, shift)

    for g in gat[:3]:
        g.a_wait()
        g.b_start()
    for g in gat[:3]:
        g.b_wait()
        g.c_start()
    for g in gat[:3]:
        g.c_wait()

    @pl.loop(0, tiles)
    def _(t):
        r, own = rows_at(rows + t * tile, tile), rows_at(t * tile, tile)
        n = n1[own, :]
        q[own, :] = bf(f32(bf(mm(n, w_q[...]))) * HEAD ** (-0.5))
        k[r, :] = bf(mm(n, w_k[...]))
        v[r, :half] = bf(mm(n, w_v[:, :half]))

    pairs = width // (2 * HEAD)
    here = lax.rem(span.tree - lax.rem(span.first, span.tree), span.tree)
    here = jnp.minimum(here, span.blocks)
    border = span.base(here)

    @pl.loop(0, pairs)
    def _(p):
        attend_pair(span, p, here, span.blocks, border, 2 * rows, q, k, v, m.bias, m.turned, mixed, m.lse)
        @pl.when(p >= pairs // 2)
        def _():
            for j in range(2):
                c = 2 * (p - pairs // 2) + j
                own_chunk(c, lambda d: d.wait())
                for g in ff(c):
                    g.z_start()

    for t in range(tiles):

        @pl.when(t * tile >= span.start)
        def _():
            drain(x.at[pl.ds(t * tile, tile)], m.w_recv.at[0, t])
            drain(v.at[pl.ds(t * tile, tile), pl.ds(half, half)], m.w_recv.at[1, t])

    @pl.loop(span.start // tile, tiles)
    def _(t):
        r = rows_at(t * tile, tile)
        n = norm_tile(x[r, :], gain, shift)
        k[r, :] = bf(mm(n, w_k[...]))
        v[r, :half] = bf(mm(n, w_v[:, :half]))


    @pl.loop(0, pairs)
    def _(p):
        attend_pair(span, p, 0, here, span.start, border, q, k, v, m.bias, m.turned, mixed, m.lse)

        for s, stage in enumerate(Gather.STAGES[:3]):

            @pl.when(p == s)
            def _():
                stage(gat[3])

        gather_steps(ff, p - 2)

    @pl.when(guest)
    def _():
        lent[0]().start()
        lent[1]().start()

    gat[3].c_wait()
    branch_out(span, x, m.lnp, mixed, w_o, m.resid, n2)
    for g in gat:
        g.finish()

    lc.wait()
    transpose_all(n2, tr)
    m.acc1[...] = m.resid[...]
    m.acc2[...] = jnp.zeros_like(m.acc2)
    red = Chunks(
        n_ff,
        lambda c: [
            Reduce(pc, m.b_in.at[c], *(a.at[c] for a in m.r_in), rs_in.at[c], m.ri_send.at[c], m.ri_recv.at[c], True),
            Reduce(pc, m.b_dn.at[c], *(a.at[c] for a in m.r_dn), rs_dn.at[c], m.rd_send.at[c], m.rd_recv.at[c], False),
        ],
    )
    hid, gact = m.back.at[0, :, pl.ds(0, fsdp * BLOCK)], m.back.at[1, :, pl.ds(0, fsdp * BLOCK)]

    @pl.loop(0, n_ff)
    def _(c):
        gather_steps(ff, c + pairs - 2)
        for g in ff(c):
            Gather.STAGES[3](g)

        b_in, b_dn = flat(m.b_in.at[c]), flat(m.b_dn.at[c])

        def put_in(val):
            b_in[...] = val

        def put_dn(val):
            b_dn[...] = val

        mlp_chunk(rows, n2, tr, cot, lambda: b_in[...], lambda: b_dn[...], m.acc1, m.acc2, hid, gact, put_in, put_dn)
        reduce_steps(red, c)

    @pl.loop(0, tiles)
    def _(t):
        r = rows_at(t * tile, tile)
        m.back[0, r, :] = bf(m.acc1[r, :])

    lo = local(m.back.at[0], outputs, m.l_sem.at[0])
    m.sums[...] = jnp.zeros_like(m.sums)
    second_norm_back(rows, m.lnp, m.resid, cot, m.acc2, m.resid, n2, m.sums)
    branch_back(rows, n2, w_o, m.gmixed)
    head_sums(m.gmixed, mixed, m.inner)

    @pl.when(guest)
    def _():
        lent[2]().start()
        for p in range(pairs):
            lent_pair(p).start()


    @pl.loop(0, width // tile)
    def _(t):
        r = rows_at(t * tile, tile)
        w_o[r, :] = bf(tn(mixed[:, pl.ds(pl.multiple_of(t * tile, tile), tile)], n2[...]))

    lo.wait()

    @pl.when((f < last) & jnp.logical_not(host))
    def _():
        pl.semaphore_signal(m.ready, inc=1, device_id=(pc.r, f + 1), device_id_type=MESH)

    for t in range(tiles):

        @pl.when((f < last) & (t * tile >= next_start))
        def _():
            for c in window(t):
                c.wait_send()

    @pl.when(guest)
    def _():
        lent[0]().wait_send()

    transpose_all(n1, tr)
    mid, end = half + (pairs // 2 - 1) * BLOCK, width
    wide = 2 * (mid - half)
    rest = lambda ref: (ref.at[..., pl.ds(0, wide)], ref.at[..., pl.ds(wide, 2 * BLOCK)])
    narrow = lambda refs, i: [ref.at[..., pl.ds(0, wide // 2) if i == 0 else pl.ds(wide // 2, BLOCK)] for ref in refs]
    buf1, buf2 = rest(m.cot)
    res1, res2 = rest(rs_k)
    stat = [
        Reduce(pc, b, *scr, res, m.rs_send.at[i], m.rs_recv.at[i], xf)
        for i, (b, scr, res, xf) in enumerate(
            (
                (m.b_o, m.r_o, rs_o, True), (m.mixed, m.r_q, rs_q, False), (m.g_v, m.r_v, rs_v, True),
                (buf1, narrow(m.r_k, 0), res1, True), (buf2, narrow(m.r_k, 1), res2, False),
            )
        )
    ]
    red_o, red_0, red_v, red_1, red_2 = stat

    def early(t, p):
        r, cols = pl.ds(t * tile, tile), pair_cols(p)
        prev = (pc.r, f - 1)
        return [
            pltpu.make_async_remote_copy(
                src_ref=x.at[pl.ds(j * rows + t * tile, tile), cols], dst_ref=m.back.at[j, r, cols], send_sem=m.e_send.at[j, p, t], recv_sem=m.e_recv.at[j, p, t],
                device_id=prev, device_id_type=MESH,
            )
            for j in range(2)
        ]

    dk, dv = m.acc1, m.acc2

    def complete(p):
        cols = pl.ds(p * BLOCK, BLOCK)
        for t in range(tiles):
            r = pl.ds(t * tile, tile)

            @pl.when((f < last) & jnp.logical_not(host) & (t * tile >= next_start))
            def _():
                for j, own in enumerate((dk, dv)):
                    drain(m.back.at[j, r, cols], m.e_recv.at[j, p, t])
                    own[r, cols] += f32(m.back[j, r, cols])

            k[r, cols] = bf(dk[r, cols])
            if p < pairs // 2:
                v[r, cols] = bf(dv[r, cols])

    def weight_grad(dst, at, grad, lo, hi):
        @pl.loop(0, width // tile)
        def _(t):
            r = rows_at(t * tile, tile)
            dst[r, at:at + hi - lo] = bf(mm(tr[r, :], grad[pl.ds(0, rows), lo:hi]))

    d_0, d_v, d_1 = flat(m.mixed), flat(m.g_v), flat(m.cot)

    def run_0():
        for p in range(pairs // 2):
            complete(p)
        weight_grad(d_0, 0, q, 0, half)
        weight_grad(d_0, half, k, 0, half)
        red_0.p1()
        d_v[:, half:] = jnp.zeros((width, d_v.shape[1] - half), jnp.bfloat16)
        weight_grad(d_v, 0, v, 0, half)
        red_v.p1()

    @pl.loop(0, pairs)
    def _(p):
        cols = pair_cols(p)
        attend_back_pair(span, p, q, k, v, m.gmixed, m.bias, m.lse, m.inner, m.turned, m.dk_acc, m.dv_acc, q, guest)
        dk[:, cols] = m.dk_acc[rows:, :]
        dv[:, cols] = m.dv_acc[rows:, :]

        @pl.when((p == 0) & (f > 0) & jnp.logical_not(guest))
        def _():
            pl.semaphore_wait(m.ready, 1)

        for t in range(tiles):

            @pl.when((f > 0) & jnp.logical_not(guest) & (t * tile >= span.start))
            def _():
                r = pl.ds(t * tile, tile)
                x[r, cols] = bf(m.dk_acc[r, :])
                x[pl.ds(rows + t * tile, tile), cols] = bf(m.dv_acc[r, :])
                for c in early(t, p):
                    c.start()

        reduce_steps(red, n_ff + p)

        @pl.when(host)
        def _():
            @pl.when(p == 0)
            def _():
                for c in lent:
                    c().wait_recv()

            lent_pair(p).wait_recv()
            borrowed_back(span, p, gq, gg, k, v, m.bias, m.g_lse, m.g_inner, dk, dv)

        for s in range(5):

            @pl.when(p == REDUCE_AT[s])
            def _():
                Reduce.STAGES[s](red_o)

        @pl.when(p == pairs - 2)
        def _():
            run_0()

        @pl.when(p == pairs - 1)
        def _():
            red_0.p2()
            red_v.p2()

    for p in range(pairs // 2, pairs - 1):
        complete(p)
    weight_grad(d_1, 0, q, half, mid)
    weight_grad(d_1, mid - half, k, half, mid)
    red_1.p1()
    weight_grad(d_1, wide, q, mid, end)
    red_0.p3()
    red_v.p3()
    red_o.p6()
    complete(pairs - 1)
    weight_grad(d_1, wide + BLOCK, k, mid, end)
    red_2.p1()
    gf = local(dv.at[:, pl.ds(half, half)], gfirst, m.l_sem.at[1])
    lx = local(inputs, n1, m.l_sem.at[2])
    red_1.p2()
    red_2.p2()
    red_0.p4()
    red_v.p4()

    @pl.loop(0, tiles)
    def _(t):
        r = rows_at(t * tile, tile)
        dk[r, :] = nt(q[r, :], w_q[...]) + nt(k[r, :], w_k[...]) + nt(v[r, :half], w_v[:, :half])

    red_2.p3()
    red_1.p3()
    reduce_steps(red, n_ff + pairs)
    red_o.p7()
    lx.wait()

    @pl.loop(0, tiles)
    def _(t):
        r = rows_at(t * tile, tile)
        g = dk[r, :]
        hat, inv = normalized(f32(n1[r, :]))
        m.resid[r, :] += norm_back(hat, inv, g, m.lnp[0:1, :])
        m.sums[0:1, :] += jnp.sum(g * hat, axis=0, keepdims=True)
        m.sums[1:2, :] += jnp.sum(g, axis=0, keepdims=True)

    gi = local(m.resid, gin, m.l_sem.at[3])

    def exchange(src, dst, i, dev):
        c = pltpu.make_async_remote_copy(src_ref=src, dst_ref=dst, send_sem=m.v_send.at[i], recv_sem=m.v_recv.at[i], device_id=dev, device_id_type=MESH)
        c.start()
        return c

    cur = m.sums
    work = [
        (red_2.p4, red_1.p4, red_0.p5, red_v.p5), (red_0.p6, red_v.p6), (red_2.p5, red_1.p5, red_0.p7, red_v.p7),
    ]
    for i, dev in enumerate((pc.core, pc.xn, pc.yn)):
        c = exchange(cur, m.s_pair.at[i], 1 + i, dev)
        for step in work[i]:
            step()
        c.wait()
        m.s_pair[i] = m.s_pair[i] + cur[...]
        cur = m.s_pair.at[i]
    for o in pc.others:
        exchange(cur, m.s_z.at[f], 4, pc.zdev(o))
    red_2.p6()
    red_1.p6()
    for u in range(n_ff + pairs + 1, n_ff + REDUCE_AT[-1]):
        reduce_steps(red, u)
    red_2.p7()
    red_1.p7()
    z3 = m.s_z.at[pl.ds(0, last)]
    drain(z3, m.v_recv.at[4])
    drain(z3, m.v_send.at[4])
    m.s_z[f] = cur[...]
    rs_vec[...] = functools.reduce(lambda a, b: a + b, [m.s_z[j] for j in range(fsdp)])
    for g in stat:
        g.p8()
        g.finish()

    @pl.loop(0, n_ff)
    def _(c):
        for g in red(c):
            g.p8()
            g.finish()

    @pl.loop(0, pairs)
    def _(p):
        for t in range(tiles):

            @pl.when((f > 0) & jnp.logical_not(guest) & (t * tile >= span.start))
            def _():
                for c in early(t, p):
                    c.wait_send()

    @pl.when(guest)
    def _():
        for c in lent[1:]:
            c().wait_send()
        for p in range(pairs):
            lent_pair(p).wait_send()

    gf.wait()
    gi.wait()


def layer_call(fsdp, inputs, first, cot, norms, w_query, w_key, w_value, w_out, w_in, w_down, segs, trees, table):
    rows, width = inputs.shape
    shard = w_query.shape[0]
    n_ff = w_down.shape[0] // BLOCK
    low, full = jnp.bfloat16, jnp.float32
    mq, md = shard // 4, BLOCK // 4
    pairs, blocks = width // (2 * HEAD), rows // BLOCK
    wide_v = width // 2 + BLOCK
    split = lambda a: a.reshape(2, 2, mq, a.shape[1])
    buf = lambda m, c, lead=(): (*lead, fsdp, 2, 2, m, c)
    chunk = fsdp * BLOCK
    sc = Scratch()
    V, D = pltpu.VMEM, pltpu.SemaphoreType.DMA
    for name, shape in (
        ("b_q", buf(mq, width)), ("b_k", buf(mq, width)), ("b_v", buf(mq, wide_v)), ("b_o", buf(mq, width)),
        ("b_in", buf(mq, chunk, (n_ff,))), ("b_dn", buf(md, width, (n_ff,))), ("g_v", buf(mq, wide_v)),
        ("mixed", buf(mq, width)), ("cot", buf(mq, width)), ("x", (2 * rows, width)), ("k", (2 * rows, width)), ("v", (2 * rows, width)),
        ("q", (rows, width)), ("n1", (rows, width)), ("n2", (rows, width)), ("tr", (width, rows)), ("gmixed", (rows, width)), ("back", (2, rows, width)),
        ("turned", (2 * HEAD, 2 * rows)),
    ):
        sc.add(name, V(shape, low))
    for name, shape in (
        ("vec", (fsdp, 8, width)), ("lnp", (8, width)), ("sums", (8, width)), ("s_pair", (3, 8, width)), ("s_z", (fsdp, 8, width)),
        ("resid", (rows, width)), ("acc1", (rows, width)), ("acc2", (rows, width)), ("bias", (blocks + 2, 3 * BLOCK, BLOCK)), ("inner", (pairs, 8, 2 * BLOCK)), ("g_inner", (pairs, 8, 2 * BLOCK)), ("g_lse", (pairs, -(-blocks // 8) * 8, 2 * BLOCK)),
        ("dk_acc", (2 * rows, 2 * HEAD)), ("dv_acc", (2 * rows, 2 * HEAD)), ("lse", (pairs, -(-blocks // 8) * 8, 2 * BLOCK)),
    ):
        sc.add(name, V(shape, full))
    for name, shape in (
        ("l_sem", (9,)), ("lc_sem", (n_ff, fsdp + 1)), ("v_send", (5,)), ("v_recv", (5,)), ("g_send", (4, 5)), ("g_recv", (4, 5)),
        ("w_send", (2, rows // row_tiles(rows))), ("w_recv", (2, rows // row_tiles(rows))),
        ("gi_send", (n_ff, 5)), ("gi_recv", (n_ff, 5)), ("gd_send", (n_ff, 5)), ("gd_recv", (n_ff, 5)),
        ("ri_send", (n_ff, 8)), ("ri_recv", (n_ff, 8)), ("rd_send", (n_ff, 8)), ("rd_recv", (n_ff, 8)), ("rs_send", (5, 8)), ("rs_recv", (5, 8)),
        ("b_send", (3 + pairs,)), ("b_recv", (3 + pairs,)), ("e_send", (2, pairs, rows // row_tiles(rows))), ("e_recv", (2, pairs, rows // row_tiles(rows))),
    ):
        sc.add(name, D(shape))
    sc.add("ready", pltpu.SemaphoreType.REGULAR)
    groups = (("r_in", buf(mq, chunk), n_ff), ("r_dn", buf(md, width), n_ff), ("r_o", buf(mq, width), 0), ("r_q", buf(mq, width), 0), ("r_k", buf(mq, width), 0), ("r_v", buf(mq, wide_v), 0))
    for name, shape, lead in groups:
        for i, sub in enumerate(red_shapes(shape)):
            sc.add(f"{name}{i}", V((lead, *sub) if lead else sub, low))

    n_out = 10
    s = jax.ShapeDtypeStruct
    outs = (
        s((rows, width), low), s((rows, width), full), s((rows, width // 2), full),
        s((2, 2, mq, width), low), s((2, 2, mq, width), low), s((2, 2, mq, wide_v), low), s((2, 2, mq, width), low),
        s((n_ff, 2, 2, mq, chunk), low), s((n_ff, 2, 2, md, width), low), s((8, width), full),
    )

    def body(*refs):
        names = Scratch()
        names.names, names.shapes = sc.names, sc.shapes
        bound = names.bind(refs[N_IN + n_out :])
        for name, _, _ in groups:
            setattr(bound, name, [getattr(bound, f"{name}{i}") for i in range(4)])
        layer_kernel(fsdp, n_ff, bound, n_out, *refs)

    any_ = pl.BlockSpec(memory_space=pl.ANY)
    return pl.pallas_call(
        body, out_shape=outs, in_specs=[any_] * 9 + [VM] * 2 + [SM] * 2, out_specs=[any_] * 3 + [VM] * 7, scratch_shapes=sc.shapes,
        compiler_params=pltpu.CompilerParams(collective_id=3, has_side_effects=True, vmem_limit_bytes=63 << 20),
    )(inputs, first, cot, split(w_query), split(w_key), split(w_value), split(w_out), split(w_in), w_down.reshape(n_ff, 2, 2, md, width), norms, segs, trees, table)


def finish_kernel(o_in, g_in, f_in, vec, *refs):
    src, (o_out, g_out, f_out, *dst), rows_out = refs[:6], refs[6:15], refs[15]
    low, full, passed, sem, load = refs[16:22], refs[22:28], refs[28:31], refs[31], refs[32]
    copies = []

    def go(src, dst):
        c = pltpu.make_async_copy(src, dst, sem.at[len(copies)])
        c.start()
        copies.append(c)

    loads = [pltpu.make_async_copy(a, b, load.at[i]) for i, (a, b) in enumerate(zip((*src, g_in, o_in, f_in), (*low, *passed)))]
    for c in loads[6:] + loads[:6]:
        c.start()
    (l_in, l_dn, l_0, l_1, l_o, l_v), (d_in, d_dn, d_q, d_k, d_o, d_v) = low, full

    def done(i, mid):
        go(mid, dst[i])

    n_ff, width = l_in.shape[0], l_0.shape[1]
    half = width // 2
    for c, a, b in zip(loads[6:], passed, (g_out, o_out, f_out)):
        c.wait()
        go(a, b)
    loads[0].wait()
    for j in range(n_ff):
        for g in range(l_in.shape[2] // BLOCK):
            at = (g * n_ff + j) * BLOCK
            d_in[:, at:at + BLOCK] = f32(l_in[j, :, g * BLOCK:(g + 1) * BLOCK])
    done(0, d_in)
    loads[1].wait()
    for j in range(n_ff):
        d_dn[j * BLOCK:(j + 1) * BLOCK, :] = f32(l_dn[j])
    done(1, d_dn)
    loads[2].wait()
    loads[3].wait()
    rest = half - BLOCK
    for i, mid in ((2, d_q), (3, d_k)):
        s = i - 2
        mid[:, :half] = f32(l_0[:, s * half:(s + 1) * half])
        mid[:, half:half + rest] = f32(l_1[:, s * rest:(s + 1) * rest])
        mid[:, half + rest:] = f32(l_1[:, 2 * rest + s * BLOCK:2 * rest + (s + 1) * BLOCK])
        done(i, mid)
    loads[4].wait()
    d_o[...] = f32(l_o[...])
    done(4, d_o)
    loads[5].wait()
    d_v[...] = f32(l_v[:, :half])
    done(5, d_v)
    rows, width = rows_out.shape[1], vec.shape[1]
    turned = pltpu.roll(vec[...], lax.rem(width - lax.axis_index("fsdp") * rows, width), 1)
    rows_out[...] = turned[:, :rows]
    for c in copies:
        c.wait()


def finish_call(outputs, gin, gfirst, rq, rk, rv, ro, ri, rd, vec):
    rows, width = rq.shape
    full = jnp.float32
    s = jax.ShapeDtypeStruct
    grads = (ri, rd, rq, rk, ro, rv)
    shapes = [(rows, ri.shape[0] * ri.shape[2]), (rd.shape[0] * BLOCK, width), (rows, width), (rows, width), (rows, width), (rows, width // 2)]
    hbm = pl.BlockSpec(memory_space=pltpu.HBM)
    out = pl.pallas_call(
        finish_kernel,
        out_shape=(s(outputs.shape, outputs.dtype), s(gin.shape, full), s(gfirst.shape, full), *(s(a, full) for a in shapes), s((8, rows), full)),
        in_specs=[hbm] * 3 + [VM] + [hbm] * 6, out_specs=[hbm] * 9 + [VM],
        scratch_shapes=[*(pltpu.VMEM(a.shape, a.dtype) for a in grads), *(pltpu.VMEM(a, full) for a in shapes), *(pltpu.VMEM(a.shape, a.dtype) for a in (gin, outputs, gfirst)), pltpu.SemaphoreType.DMA((9,)), pltpu.SemaphoreType.DMA((9,))],
        compiler_params=pltpu.CompilerParams(vmem_limit_bytes=61 << 20),
    )(outputs, gin, gfirst, vec, *grads)
    din, ddn, dq, dk, do, dv = out[3:9]
    return out[0], out[1], out[2], dq, dk, dv, do, din, ddn, out[9]


def shifted(block, axis, distance):
    devices = range(lax.axis_size(axis))
    route = [(i - distance, i) for i in devices if i - distance in devices]
    return lax.ppermute(block, axis, route)


def reorder_rows(grad_block, fsdp_count, rep_count):
    return grad_block.reshape(fsdp_count, rep_count, -1).transpose(1, 0, 2).reshape(-1)


def packed_qkv(query, key, value):
    h, pad = query.shape[1] * 2 // 3, jnp.zeros_like(value[:, : value.shape[1] // 3])
    n = value.shape[1] * 2 // 3
    return jnp.concatenate([query[:, :h], key[:, :h], query[:, h:], value[:, :n], key[:, h:], value[:, n:], pad], axis=1)


def unpacked_qkv(first, second):
    h = first.shape[-1] // 2
    q = h // 2
    return (
        jnp.concatenate([first[..., :h], second[..., :q]], axis=-1),
        jnp.concatenate([first[..., h:], second[..., h : h + q]], axis=-1),
        jnp.concatenate([second[..., q:h], second[..., h + q : h + q + q // 2]], axis=-1),
    )


def gathered(fsdp, gain1, shift1, gain2, shift2, w_query, w_key, w_value, w_out, w_in, w_down):
    width = w_query.shape[1]
    n_ff = w_down.shape[0] // BLOCK
    packed = packed_qkv(w_query, w_key, w_value)
    full = [lax.all_gather(v, "fsdp", axis=0, tiled=True) for v in (packed, w_out, w_in, w_down)]
    vec = lax.all_gather(jnp.stack([gain1, shift1, gain2, shift2]), "fsdp", axis=1, tiled=True).astype(jnp.float32)
    half = packed.shape[1] // 2
    inner = full[2].reshape(width, fsdp, n_ff, BLOCK).transpose(2, 0, 1, 3).reshape(n_ff, width, -1)
    down = full[3].reshape(fsdp, n_ff, BLOCK, width).transpose(1, 0, 2, 3).reshape(n_ff, -1, width)
    return jnp.pad(vec, ((0, 4), (0, 0))), full[0][:, :half], full[0][:, half:], full[1], inner, down


def reduced(fsdp, sums, g1, g2, go, gin, gdn):
    width = go.shape[0]
    rows = width // fsdp
    n_ff = gin.shape[0]
    both = ("rep", "fsdp")
    rep = lax.axis_size("rep")

    def total(a):
        piece = lax.psum_scatter(reorder_rows(a.astype(jnp.float32), fsdp, rep), both, scatter_dimension=0, tiled=True)
        return lax.all_gather(piece.astype(jnp.bfloat16), "rep", axis=0, tiled=True)

    first, second, ro = (total(a).reshape(rows, -1) for a in (g1, g2, go))
    ri = total(gin.transpose(1, 0, 2)).reshape(rows, n_ff, -1).transpose(1, 0, 2)
    rd = total(gdn.reshape(n_ff, fsdp, BLOCK, width).transpose(1, 0, 2, 3)).reshape(n_ff, BLOCK, width)
    return lax.psum(sums, both), *unpacked_qkv(first, second), ro, ri, rd


def one_kernel(inputs, first_values, cotangent, segs, trees, table, gain1, shift1, gain2, shift2, w_query, w_key, w_value, w_out, w_in, w_down):
    fsdp = lax.axis_size("fsdp")
    rows, width = w_query.shape
    norms = jnp.concatenate([gain1, shift1, gain2, shift2]).reshape(4, rows)
    outputs, input_grad, first_grad, rq, rk, rv, ro, ri, rd, sums = layer_call(
        fsdp, inputs, first_values, cotangent, norms, w_query, w_key, w_value, w_out, w_in, w_down, segs, trees, table
    )
    rq, rk, rv, ro, ri, rd = (a.reshape(*a.shape[:-4], -1, a.shape[-1]) for a in (rq, rk, rv, ro, ri, rd))
    outputs, input_grad, first_grad, rq, rk, rv, ro, ri, rd, sums = finish_call(outputs, input_grad, first_grad, rq, rk, rv, ro, ri, rd, sums)
    return outputs, input_grad, first_grad, sums[0], sums[1], rq, rk, rv, ro, sums[2], sums[3], ri, rd


def several_kernels(reach, inputs, first_values, cotangent, segs, trees, table, gain1, shift1, gain2, shift2, w_query, w_key, w_value, w_out, w_in, w_down):
    row_count, width = inputs.shape
    fsdp = lax.axis_size("fsdp")
    lnp, w1, w2, wo, win, wdn = gathered(fsdp, gain1, shift1, gain2, shift2, w_query, w_key, w_value, w_out, w_in, w_down)
    x = jnp.concatenate([shifted(inputs, "fsdp", d) for d in range(reach, 0, -1)] + [inputs], axis=0)
    fv = jnp.concatenate([shifted(first_values, "fsdp", d) for d in range(reach, 0, -1)] + [first_values], axis=0)
    n1, q, k, v, mixed, lse, resid, n2 = forward_call(fsdp, reach, x, fv, lnp, w1, w2, wo, segs, trees, table)
    outputs, gin, gdn, go, gres, gmixed, sums = mlp_call(n2, cotangent, resid, mixed, lnp, win, wdn, wo)
    dq, dk, dv, wk, wv = backward_call(fsdp, reach, q, k, v, gmixed, mixed, lse, segs, trees, table)
    for d in range(1, reach + 1):
        early = slice((reach - d) * row_count, (reach - d + 1) * row_count)
        both = shifted(jnp.concatenate([wk[early], wv[early]], axis=1), "fsdp", -d).astype(jnp.float32)
        dk, dv = dk + both[:, :width], dv + both[:, width:]
    input_grad, first_grad, g1, g2, sums = projection_back_call(fsdp, reach, x, n1, dq, dk, dv, lnp, w1, w2, gres, sums)
    return outputs, input_grad, first_grad, *reduced(fsdp, sums, g1, g2, go, gin, gdn)


def on_device(
    inputs,
    first_values,
    cotangent,
    tree_ids,
    segment_ids,
    path_table,
    attn_gain,
    attn_shift,
    w_query,
    w_key,
    w_value,
    w_out,
    mlp_gain,
    mlp_shift,
    w_in,
    w_down,
):
    row_count, width = inputs.shape
    fsdp = lax.axis_size("fsdp")
    reach = 0
    for device_pos in range(fsdp):
        offset = device_pos * row_count % TREE_LEN
        reach = max(reach, (offset + row_count - 1) // row_count)
    marks = (segment_ids.reshape(-1, BLOCK), tree_ids, path_table)
    weights = (attn_gain, attn_shift, mlp_gain, mlp_shift, w_query, w_key, w_value, w_out, w_in, w_down)
    if lax.axis_size("rep") == 8 and reach == 1 and row_count == width:
        return one_kernel(inputs, first_values, cotangent, *marks, *weights)
    results = several_kernels(reach, inputs, first_values, cotangent, *marks, *weights)
    outputs, input_grad, first_grad, sums, d_q, d_k, d_v, d_o, d_in, d_dn = results
    rows = w_query.shape[0]
    sums = lax.dynamic_slice_in_dim(sums, lax.axis_index("fsdp") * rows, rows, 1)
    d_in = d_in.reshape(-1, rows, fsdp, BLOCK).transpose(1, 2, 0, 3).reshape(rows, -1)
    d_q, d_k, d_v, d_o, d_in, d_dn = (a.astype(jnp.float32) for a in (d_q, d_k, d_v, d_o, d_in, d_dn.reshape(-1, width)))
    return (outputs, input_grad, first_grad, sums[0], sums[1], d_q, d_k, d_v, d_o, sums[2], sums[3], d_in, d_dn)


def solution(mesh):
    placed = (
        P(("rep", "fsdp"), None),
        P(("rep", "fsdp"), None),
        P(("rep", "fsdp"), None),
        P("rep"),
        P("rep"),
        P("rep", None, None),
        P("fsdp"),
        P("fsdp"),
        P("fsdp", None),
        P("fsdp", None),
        P("fsdp", None),
        P("fsdp", None),
        P("fsdp"),
        P("fsdp"),
        P("fsdp", None),
        P("fsdp", None),
    )
    return jax.shard_map(
        on_device,
        mesh=mesh,
        in_specs=placed,
        out_specs=(
            P(("rep", "fsdp"), None),
            P(("rep", "fsdp"), None),
            P(("rep", "fsdp"), None),
            P("fsdp"),
            P("fsdp"),
            P("fsdp", None),
            P("fsdp", None),
            P("fsdp", None),
            P("fsdp", None),
            P("fsdp"),
            P("fsdp"),
            P("fsdp", None),
            P("fsdp", None),
        ),
        check_vma=False,
    )
```

```python
import functools

import jax
import jax.numpy as jnp
from jax import lax
from jax.experimental import pallas as pl
from jax.experimental.pallas import tpu as pltpu
from jax.sharding import PartitionSpec as P

MESH = pl.DeviceIdType.MESH

class Place:
    def __init__(self, fsdp):
        self.fsdp = fsdp
        r = lax.axis_index("rep")
        self.f = lax.axis_index("fsdp")
        self.k = lax.rem(r, 2)
        self.x = lax.rem(r // 2, 2)
        self.y = r // 4
        def rid(y, x, k): return (y * 2 + x) * 2 + k
        self.core = (rid(self.y, self.x, 1 - self.k), self.f)
        self.xn = (rid(self.y, 1 - self.x, self.k), self.f)
        self.yn = (rid(1 - self.y, self.x, self.k), self.f)
        self.r = r
        self.diagonal = (rid(1 - self.y, 1 - self.x, self.k), self.f)
        self.others = [lax.rem(self.f + j, fsdp) for j in range(1, fsdp)]
    def zdev(self, fo): return (self.r, fo)
    def barrier(self):
        bar = pltpu.get_barrier_semaphore()
        devs = [self.core, self.xn, self.yn, self.diagonal] + [self.zdev(o) for o in self.others]
        for d in devs:
            pl.semaphore_signal(bar, inc=1, device_id=d, device_id_type=MESH)
        pl.semaphore_wait(bar, len(devs))

def drain(view, sem):
    pltpu.make_async_copy(view, view, sem).wait()

class Gather:
    def __init__(self, pc, buf, send, recv, xfirst, direct=False):
        self.pc, self.buf, self.s, self.r, self.xf, self.direct = pc, buf, send, recv, xfirst, direct
        self.H = buf.shape[-1] // 2
        self.cols = pl.ds(pl.multiple_of(pc.k * self.H, 128), self.H)
    def push(self, view, stage, dev):
        pltpu.make_async_remote_copy(src_ref=view, dst_ref=view, send_sem=self.s.at[stage], recv_sem=self.r.at[stage], device_id=dev, device_id_type=MESH).start()
    def z_start(self):
        pc = self.pc
        v = self.buf.at[pc.f, pc.y, pc.x, :, self.cols]
        for o in pc.others: self.push(v, 0, pc.zdev(o))
    def three(self): return self.buf.at[pl.ds(0, self.pc.fsdp - 1), 0, 0, :, self.cols]
    def z_wait(self): drain(self.three(), self.r.at[0])
    def a_start(self):
        pc = self.pc
        for o in pc.others:
            v = self.buf.at[o, pc.y, pc.x, :, self.cols]
            self.push(v, 1, pc.xn); self.push(v, 2, pc.yn)
            if self.direct: self.push(v, 3, pc.diagonal)
    def a_wait(self):
        drain(self.three(), self.r.at[1]); drain(self.three(), self.r.at[2])
    def b_start(self):
        pc = self.pc
        if self.direct: return
        for o in pc.others:
            if self.xf: self.push(self.buf.at[o, 1 - pc.y, pc.x, :, self.cols], 3, pc.xn)
            else: self.push(self.buf.at[o, pc.y, 1 - pc.x, :, self.cols], 3, pc.yn)
    def b_wait(self): drain(self.three(), self.r.at[3])
    def c_start(self):
        pc = self.pc
        for o in pc.others: self.push(self.buf.at[o, :, :, :, self.cols], 4, pc.core)
    def big(self): return self.buf.at[pl.ds(0, self.pc.fsdp - 1), :, :, :, self.cols]
    def c_wait(self): drain(self.big(), self.r.at[4])
    def finish(self, first=0):
        for st in range(first, 4): drain(self.three(), self.s.at[st])
        drain(self.big(), self.s.at[4])

Gather.STAGES = [
    lambda g: (g.z_wait(), g.a_start()),
    lambda g: (g.a_wait(), g.b_start()),
    lambda g: (g.b_wait(), g.c_start()),
    lambda g: (g.c_wait(), g.finish()),
]


class Reduce:
    def __init__(self, pc, buf, r1, r2, r3, r4, res, send, recv, xfirst):
        self.pc, self.buf, self.r1, self.r2, self.r3, self.r4, self.res = pc, buf, r1, r2, r3, r4, res
        self.s, self.r, self.xf = send, recv, xfirst
        self.H = H = buf.shape[-1] // 2
        self.cols = pl.ds(pl.multiple_of(pc.k * H, 128), H)
        self.ocols = pl.ds(pl.multiple_of((1 - pc.k) * H, 128), H)
        self.F = buf.shape[0]
    def send(self, src, dst, stage, dev):
        pltpu.make_async_remote_copy(src_ref=src, dst_ref=dst, send_sem=self.s.at[stage], recv_sem=self.r.at[stage], device_id=dev, device_id_type=MESH).start()
    def p1(self):
        self.send(self.buf.at[:, :, :, :, self.ocols], self.r1, 0, self.pc.core)
    def p2(self):
        pc = self.pc
        drain(self.r1, self.r.at[0])
        @pl.loop(0, self.F * 4)
        def _(i):
            a, b, c = i // 4, lax.rem(i // 2, 2), lax.rem(i, 2)
            self.r1[a, b, c] = self.r1[a, b, c] + self.buf[a, b, c, :, self.cols]
        if self.xf: self.send(self.r1.at[:, :, 1 - pc.x], self.r2, 1, pc.xn)
        else: self.send(self.r1.at[:, 1 - pc.y], self.r2, 1, pc.yn)
    def p3(self):
        pc = self.pc
        drain(self.r2, self.r.at[1])
        @pl.loop(0, self.F * 2)
        def _(i):
            a, b = i // 2, lax.rem(i, 2)
            mine = self.r1[a, b, pc.x] if self.xf else self.r1[a, pc.y, b]
            self.r2[a, b] = self.r2[a, b] + mine
        if self.xf: self.send(self.r2.at[:, 1 - pc.y], self.r3, 2, pc.yn)
        else: self.send(self.r2.at[:, 1 - pc.x], self.r3, 2, pc.xn)
    def p4(self):
        pc = self.pc
        drain(self.r3, self.r.at[2])
        q = pc.y if self.xf else pc.x
        @pl.loop(0, self.F)
        def _(a):
            self.r3[a] = self.r3[a] + self.r2[a, q]
        for o in pc.others: self.send(self.r3.at[o], self.r4.at[pc.f], 3, pc.zdev(o))
    def p5(self):
        pc = self.pc
        drain(self.r4.at[pl.ds(0, self.F - 1)], self.r.at[3])
        tot = self.r3[pc.f].astype(jnp.float32)
        for o in pc.others: tot = tot + self.r4[o].astype(jnp.float32)
        self.res[pc.y, pc.x, :, self.cols] = tot.astype(jnp.bfloat16)
        v = self.res.at[pc.y, pc.x, :, self.cols]
        self.send(v, v, 4, pc.xn); self.send(v, v, 5, pc.yn)
    def p6(self):
        pc = self.pc
        v = self.res.at[0, 0, :, self.cols]
        drain(v, self.r.at[4]); drain(v, self.r.at[5])
        if self.xf:
            v = self.res.at[1 - pc.y, pc.x, :, self.cols]; self.send(v, v, 6, pc.xn)
        else:
            v = self.res.at[pc.y, 1 - pc.x, :, self.cols]; self.send(v, v, 6, pc.yn)
    def p7(self):
        drain(self.res.at[0, 0, :, self.cols], self.r.at[6])
        v = self.res.at[:, :, :, self.cols]
        self.send(v, v, 7, self.pc.core)
    def p8(self):
        drain(self.res.at[:, :, :, self.cols], self.r.at[7])
    def finish(self):
        drain(self.r1, self.s.at[0]); drain(self.r2, self.s.at[1]); drain(self.r3, self.s.at[2])
        drain(self.r4.at[pl.ds(0, self.F - 1)], self.s.at[3])
        v = self.res.at[0, 0, :, self.cols]
        for i in (4, 5, 6): drain(v, self.s.at[i])
        drain(self.res.at[:, :, :, self.cols], self.s.at[7])

Reduce.STAGES = [Reduce.p1, Reduce.p2, Reduce.p3, Reduce.p4, Reduce.p5, Reduce.p6, Reduce.p7, Reduce.p8]

def red_shapes(shape):
    f, _, _, m, c = shape
    return (f, 2, 2, m, c // 2), (f, 2, m, c // 2), (f, m, c // 2), (f, m, c // 2)


HEAD = 64
BLOCK = 128
TRUNK = 512
TREE_LEN = 1024


epsilon = 1e-05
far_below = -1e30


def nt(a, b):
    return lax.dot_general(a, b, (((1,), (1,)), ((), ())), preferred_element_type=jnp.float32)


def tn(a, b):
    return lax.dot_general(a, b, (((0,), (0,)), ((), ())), preferred_element_type=jnp.float32)


def mm(a, b):
    return jnp.dot(a, b, preferred_element_type=jnp.float32)


def bf(a):
    return a.astype(jnp.bfloat16)


def f32(a):
    return a.astype(jnp.float32)


def row_tiles(rows):
    return 256 if rows % 256 == 0 else 128


def normalized(v):
    center = v - jnp.mean(v, axis=1, keepdims=True)
    inv = lax.rsqrt(jnp.mean(center * center, axis=1, keepdims=True) + epsilon)
    return center * inv, inv


class Span:
    def __init__(self, fsdp, rows, reach, f):
        self.rows, self.reach, self.f = rows, reach, f
        self.window = reach * rows
        self.blocks = rows // BLOCK
        self.first = f * self.blocks
        tree = TREE_LEN // BLOCK
        self.tree = tree
        self.start = (self.first // tree) * TREE_LEN - f * rows + self.window

    def kind(self, i):
        return lax.rem(self.first + i, self.tree)

    def base(self, i):
        return pl.multiple_of(((self.first + i) // self.tree) * TREE_LEN - self.f * self.rows + self.window, BLOCK)


def rows_at(start, size):
    return pl.ds(pl.multiple_of(start, BLOCK), size)


def make_bias(span, segs, trees, table, bias, extra=0):
    @pl.loop(0, span.blocks + extra)
    def _(i):
        b = span.kind(i)
        first = ((span.first + i) // span.tree) * span.tree
        q_pos = b * BLOCK + lax.broadcasted_iota(jnp.int32, (1, BLOCK), 1)
        own = segs[pl.ds(span.first + i, 1), :]

        def put(slot, key, related):
            k_pos = key * BLOCK + lax.broadcasted_iota(jnp.int32, (BLOCK, 1), 0)
            column = jnp.broadcast_to(f32(segs[pl.ds(first + key, 1), :]), (BLOCK, BLOCK)).T
            seen = (k_pos <= q_pos) & (column == f32(related))
            bias[i, pl.ds(slot, BLOCK), :] = jnp.where(seen, 0.0, far_below)

        put(256, b, own)

        @pl.when(b >= 6)
        def _():
            tree = trees[first * BLOCK]
            parent = jnp.zeros_like(own)
            rows = table[tree]
            for leaf in range(table.shape[1]):
                parent = jnp.where(own == leaf, rows[leaf:leaf + 1, 1:2], parent)
            put(0, 4, parent)
            put(BLOCK, 5, parent)


def by_kind(b, body, lent=None):
    for n in range(TRUNK // BLOCK):

        @pl.when(b == n)
        def _():
            body([(0, n * BLOCK, None)][: n] + [(None, BLOCK, 256)])

    branch_parts = [(0, 512, None), (None, BLOCK, 256)]
    leaf_parts = [(0, 512, None), (512, 256, 0), (None, BLOCK, 256)]
    if lent is None:

        @pl.when((b >= 4) & (b < 6))
        def _():
            body(branch_parts)

        @pl.when(b >= 6)
        def _():
            body(leaf_parts)

    else:
        for upto in (0, 512, 768):

            if upto < 768:

                @pl.when((b >= 4) & (b < 6) & (lent == upto))
                def _():
                    body(branch_parts, upto)

            @pl.when((b >= 6) & (lent == upto))
            def _():
                body(leaf_parts, upto)


def stacked(pair):
    low = lax.broadcasted_iota(jnp.int32, (1, 2 * HEAD), 1) < HEAD
    zero = jnp.zeros_like(pair)
    return jnp.concatenate([jnp.where(low, pair, zero), jnp.where(low, zero, pair)], axis=0)


def unstacked_t(wide):
    both = jnp.concatenate([wide[:HEAD, :BLOCK], wide[HEAD:, BLOCK:]], axis=0)
    return both.T


def part_rows(span, i, b, part):
    key, count, slot = part
    return rows_at(span.base(i) + (b * BLOCK if key is None else key), count)


def part_scores(q2, k, bias, i, part):
    s = nt(k, q2)
    slot = part[2]
    if slot is not None:
        one = bias[i, pl.ds(slot, part[1]), :]
        s = s + jnp.concatenate([one, one], axis=1)
    return s


def pair_cols(p):
    return pl.ds(pl.multiple_of(p * 2 * HEAD, 2 * HEAD), 2 * HEAD)


def transpose_pair(src, p, start, stop, dst):
    step = row_tiles(src.shape[0])

    @pl.loop(start // step, stop // step)
    def _(j):
        dst[:, pl.ds(pl.multiple_of(j * step, step), step)] = src[rows_at(j * step, step), pair_cols(p)].T


def group_cols(p, j, n):
    return pl.ds(pl.multiple_of((p * n + j) * 2 * HEAD, 2 * HEAD), 2 * HEAD)


GROUP = 2


def attend_group(span, p, lo, hi, q, k, v, bias, mixed, lse):
    @pl.loop(lo, hi)
    def _(i):
        b = span.kind(i)
        own = rows_at(i * BLOCK, BLOCK)

        def body(parts):
            rows = [part_rows(span, i, b, part) for part in parts]
            state = []
            for j in range(GROUP):
                cols = group_cols(p, j, GROUP)
                q2 = stacked(q[own, cols])
                state.append((j, cols, [part_scores(q2, k[r, cols], bias, i, part) for r, part in zip(rows, parts)]))
            for j, cols, scores in state:
                top = functools.reduce(jnp.maximum, [jnp.max(s, axis=0, keepdims=True) for s in scores])
                expo = [jnp.exp(s - top) for s in scores]
                total = sum(jnp.sum(e, axis=0, keepdims=True) for e in expo)
                out = sum(tn(v[r, cols], bf(e)) for r, e in zip(rows, expo))
                mixed[own, cols] = bf(unstacked_t(out * (1.0 / total)))
                lse[p * GROUP + j, pl.ds(i, 1), :] = top + jnp.log(total)

        by_kind(b, body)


def norm_tile(x, gain, shift):
    hat, _ = normalized(f32(x))
    return bf(hat * gain + shift)


def project(span, x, fv, lnp, w1, w2, n1, q, k, v):
    gain, shift = lnp[0:1, :], lnp[1:2, :]
    tile = row_tiles(span.rows)
    third = w1.shape[1] // 4
    half = 2 * third
    scale = HEAD ** (-0.5)

    @pl.loop(span.window // tile, (span.window + span.rows) // tile)
    def _(t):
        rows = rows_at(t * tile, tile)
        n = norm_tile(x[rows, :], gain, shift)
        own = rows_at(t * tile - span.window, tile)
        n1[own, :] = n
        a = mm(n, w1[...])
        q[own, :half] = bf(f32(bf(a[:, :half])) * scale)
        k[rows, :half] = bf(a[:, half:])
        a = mm(n, w2[...])
        q[own, half:] = bf(f32(bf(a[:, :third])) * scale)
        k[rows, half:] = bf(a[:, half:half + third])
        v[rows, :third] = bf(a[:, third:half])
        v[rows, third:third + BLOCK] = bf(a[:, half + third:half + third + BLOCK])
        v[rows, third + BLOCK:] = fv[rows, :]

    @pl.loop(span.start // tile, span.window // tile)
    def _(t):
        rows = rows_at(t * tile, tile)
        n = norm_tile(x[rows, :], gain, shift)
        k[rows, :half] = bf(mm(n, w1[:, half:]))
        a = mm(n, w2[:, third:])
        v[rows, :third] = bf(a[:, :third])
        k[rows, half:] = bf(a[:, third:half])
        v[rows, third:third + BLOCK] = bf(a[:, half:half + BLOCK])
        v[rows, third + BLOCK:] = fv[rows, :]


def branch_out(span, x, lnp, mixed, wo, resid, n2):
    gain, shift = lnp[2:3, :], lnp[3:4, :]
    tile = row_tiles(span.rows)

    @pl.loop(0, span.rows // tile)
    def _(t):
        rows = rows_at(t * tile, tile)
        r = f32(x[rows_at(span.window + t * tile, tile), :]) + mm(mixed[rows, :], wo[...])
        resid[rows, :] = r
        hat, _ = normalized(r)
        n2[rows, :] = bf(hat * gain + shift)


def forward_kernel(fsdp, reach, x, fv, lnp, w1, w2, wo, segs, trees, table, n1, q, k, v, mixed, lse, resid, n2, bias):
    span = Span(fsdp, q.shape[0], reach, lax.axis_index("fsdp"))
    rows = q.shape[0]
    make_bias(span, segs, trees, table, bias)
    project(span, x, fv, lnp, w1, w2, n1, q, k, v)

    @pl.loop(0, q.shape[1] // (2 * HEAD) // GROUP)
    def _(p):
        attend_group(span, p, 0, span.blocks, q, k, v, bias, mixed, lse)

    branch_out(span, x, lnp, mixed, wo, resid, n2)


VM = pl.BlockSpec(memory_space=pltpu.VMEM)
SM = pl.BlockSpec(memory_space=pltpu.SMEM)


def forward_call(fsdp, reach, x, fv, lnp, w1, w2, wo, segs, trees, table):
    window, width = x.shape
    rows = window // (reach + 1)
    s = jax.ShapeDtypeStruct
    low, full = jnp.bfloat16, jnp.float32
    pairs, blocks = width // (2 * HEAD), rows // BLOCK
    outs = (
        s((rows, width), low), s((rows, width), low), s((window, width), low), s((window, width), low), s((rows, width), low),
        s((pairs, -(-blocks // 8) * 8, 2 * BLOCK), full), s((rows, width), full), s((rows, width), low),
    )
    return pl.pallas_call(
        functools.partial(forward_kernel, fsdp, reach),
        out_shape=outs, in_specs=[VM] * 7 + [SM, VM], out_specs=[VM] * 8,
        scratch_shapes=[pltpu.VMEM((blocks, 3 * BLOCK, BLOCK), full)],
        compiler_params=pltpu.CompilerParams(vmem_limit_bytes=50 << 20),
    )(x, fv, lnp, w1, w2, wo, segs, trees, table)


GELU_A = 0.7978845608028654
GELU_B = 0.044715


def gelu_both(u):
    sq = u * u
    t = jnp.tanh(GELU_A * u * (1.0 + GELU_B * sq))
    half = 0.5 * (1.0 + t)
    slope = half + 0.5 * u * (1.0 - t * t) * (GELU_A * (1.0 + 3.0 * GELU_B * sq))
    return u * half, slope


def transpose_all(src, dst):
    cols = src.shape[1] // BLOCK

    @pl.loop(0, src.shape[0] // BLOCK)
    def _(j):
        rows = rows_at(j * BLOCK, BLOCK)
        for c in range(cols):
            dst[c * BLOCK:(c + 1) * BLOCK, rows] = src[rows, c * BLOCK:(c + 1) * BLOCK].T


def mlp_chunk(rows, n2, n2_t, cot, win, wdn, out_acc, gn2_acc, hid, gact, gin, gdn, between=lambda: None):
    tile = 384 if rows % 384 == 0 else row_tiles(rows)

    @pl.loop(0, rows // tile)
    def _(t):
        r = rows_at(t * tile, tile)
        h, slope = gelu_both(mm(n2[r, :], win()))
        h = bf(h)
        hid[r, :] = h
        out_acc[r, :] += mm(h, wdn())
        g = bf(nt(cot[r, :], wdn()) * slope)
        gact[r, :] = g
        gn2_acc[r, :] += nt(g, win())

    between()
    gdn(bf(tn(hid[...], cot[...])))
    gin(bf(mm(n2_t[...], gact[...])))


def norm_back(hat, inv, grad, gain):
    e = grad * gain
    return inv * (e - jnp.mean(e, axis=1, keepdims=True) - hat * jnp.mean(e * hat, axis=1, keepdims=True))


def second_norm_back(rows, lnp, resid, cot, gn2, gres, gbranch, sums):
    tile = row_tiles(rows)
    sums[...] = jnp.zeros_like(sums)

    @pl.loop(0, rows // tile)
    def _(t):
        r = rows_at(t * tile, tile)
        hat, inv = normalized(resid[r, :])
        g = gn2[r, :]
        gr = f32(cot[r, :]) + norm_back(hat, inv, g, lnp[2:3, :])
        gres[r, :] = gr
        gbranch[r, :] = bf(gr)
        sums[2:3, :] += jnp.sum(g * hat, axis=0, keepdims=True)
        sums[3:4, :] += jnp.sum(g, axis=0, keepdims=True)


def branch_back(rows, gbranch, wo, gmixed):
    tile = row_tiles(rows)

    @pl.loop(0, rows // tile)
    def _(t):
        r = rows_at(t * tile, tile)
        gmixed[r, :] = bf(nt(gbranch[r, :], wo[...]))


def mlp_kernel(n2, cot, resid, mixed, lnp, win, wdn, wo, outputs, gin, gdn, go, gres, gmixed, sums, n2_t, out_acc, gn2_acc, hid, gact, gbranch):
    rows = n2.shape[0]
    transpose_all(n2, n2_t)
    out_acc[...] = resid[...]
    gn2_acc[...] = jnp.zeros_like(gn2_acc)

    @pl.loop(0, win.shape[0])
    def _(c):
        def put_in(v):
            gin[c] = v

        def put_dn(v):
            gdn[c] = v

        mlp_chunk(rows, n2, n2_t, cot, lambda: win[c], lambda: wdn[c], out_acc, gn2_acc, hid, gact, put_in, put_dn)

    outputs[...] = bf(out_acc[...])
    second_norm_back(rows, lnp, resid, cot, gn2_acc, gres, gbranch, sums)
    branch_back(rows, gbranch, wo, gmixed)
    go[...] = bf(tn(mixed[...], gbranch[...]))


def mlp_call(n2, cot, resid, mixed, lnp, win, wdn, wo):
    rows, width = n2.shape
    n_ff, _, cols = win.shape
    s, low, full = jax.ShapeDtypeStruct, jnp.bfloat16, jnp.float32
    outs = (
        s((rows, width), low), s(win.shape, low), s(wdn.shape, low), s((width, width), low), s((rows, width), full),
        s((rows, width), low), s((8, width), full),
    )
    return pl.pallas_call(
        mlp_kernel, out_shape=outs, in_specs=[VM] * 8, out_specs=[VM] * 7,
        scratch_shapes=[
            pltpu.VMEM((width, rows), low), pltpu.VMEM((rows, width), full), pltpu.VMEM((rows, width), full),
            pltpu.VMEM((rows, cols), low), pltpu.VMEM((rows, cols), low), pltpu.VMEM((rows, width), low),
        ],
        compiler_params=pltpu.CompilerParams(vmem_limit_bytes=58 << 20),
    )(n2, cot, resid, mixed, lnp, win, wdn, wo)


def attend_back_group(span, p, lo, hi, q, k, v, gmixed, bias, lse, inner, dk_acc, dv_acc, dq, lent=None):
    @pl.loop(lo, hi)
    def _(i):
        b = span.kind(i)
        own = rows_at(i * BLOCK, BLOCK)

        def body(parts, upto=0):
            rows = [part_rows(span, i, b, part) for part in parts]
            state = []
            for j in range(GROUP):
                cols = group_cols(p, j, GROUP)
                q2, g2 = stacked(q[own, cols]), stacked(gmixed[own, cols])
                state.append((j, cols, q2, g2, [part_scores(q2, k[r, cols], bias, i, part) for r, part in zip(rows, parts)]))
            for j, cols, q2, g2, scores in state:
                l, mean = lse[p * GROUP + j, pl.ds(i, 1), :], inner[p * GROUP + j, pl.ds(i, 1), :]
                probs = [jnp.exp(s - l) for s in scores]
                gs = [bf(a * (nt(v[r, cols], g2) - mean)) for a, r in zip(probs, rows)]
                out = sum(tn(k[r, cols], g) for r, g in zip(rows, gs))
                dq[own, cols] = bf(unstacked_t(out) * HEAD ** (-0.5))
                at = slice(j * 2 * HEAD, (j + 1) * 2 * HEAD)
                for r, a, g, part in zip(rows, probs, gs, parts):
                    if part[0] is not None and part[0] < upto:
                        continue
                    dk_acc[r, at] += mm(g, q2)
                    dv_acc[r, at] += mm(bf(a), g2)

        by_kind(b, body, None if lent is None else jnp.where(i < span.tree - span.kind(0), lent, 0))


def clear_rows(span, *refs):
    @pl.loop(span.start // BLOCK, (span.window + span.rows) // BLOCK)
    def _(j):
        r = rows_at(j * BLOCK, BLOCK)
        for ref in refs:
            ref[r, :] = jnp.zeros((BLOCK, ref.shape[1]), jnp.float32)


def head_sums(gmixed, mixed, inner):
    width = mixed.shape[1]
    heads = lax.broadcasted_iota(jnp.int32, (16, width), 0)
    cols = lax.broadcasted_iota(jnp.int32, (16, width), 1)
    pick = bf(((cols >= heads * HEAD) & (cols < heads * HEAD + HEAD)).astype(jnp.float32))
    tile = row_tiles(mixed.shape[0])
    for t in range(mixed.shape[0] // tile):
        r = slice(t * tile, (t + 1) * tile)
        each = f32(gmixed[r, :]) * f32(mixed[r, :])
        high = bf(each)
        sums = nt(pick, high) + nt(pick, bf(each - f32(high)))
        for j in range(tile // BLOCK):
            at, i = slice(j * BLOCK, (j + 1) * BLOCK), t * (tile // BLOCK) + j
            for p in range(width // (2 * HEAD)):
                inner[p, i:i + 1, :] = jnp.concatenate([sums[2 * p:2 * p + 1, at], sums[2 * p + 1:2 * p + 2, at]], axis=1)


def borrowed_back(span, p, cols, j, parts, q, g, k, v, bias, lse, inner, dk, dv):
    join = lambda of: jnp.concatenate([of(0), of(1)], axis=0)
    q2 = join(lambda n: stacked(q[rows_at((j + n) * BLOCK, BLOCK), cols]))
    g2 = join(lambda n: stacked(g[rows_at((j + n) * BLOCK, BLOCK), cols]))
    row = lambda ref: jnp.concatenate([ref[p, pl.ds(j, 1), :], ref[p, pl.ds(j + 1, 1), :]], axis=1)
    l, mean = row(lse), row(inner)
    base = span.base(span.blocks - 1)
    for key, count, slot in parts:
        rows, own = rows_at(base + key, count), rows_at(base - span.window + key, count)
        s = nt(k[rows, cols], q2)
        if slot is not None:
            both = [bias[span.blocks + n, pl.ds(slot, count), :] for n in range(2)]
            s = s + jnp.concatenate([both[0], both[0], both[1], both[1]], axis=1)
        probs = jnp.exp(s - l)
        gs = bf(probs * (nt(v[rows, cols], g2) - mean))
        dk[own, cols] += mm(gs, q2)
        dv[own, cols] += mm(bf(probs), g2)


def backward_kernel(fsdp, reach, q, k, v, gmixed, mixed, lse, segs, trees, table, dq, dk, dv, wk, wv, bias, inner, dk_acc, dv_acc):
    span = Span(fsdp, q.shape[0], reach, lax.axis_index("fsdp"))
    make_bias(span, segs, trees, table, bias)
    head_sums(gmixed, mixed, inner)
    wk[...] = jnp.zeros_like(wk)
    wv[...] = jnp.zeros_like(wv)

    size = GROUP * 2 * HEAD

    @pl.loop(0, q.shape[1] // size)
    def _(p):
        cols = pl.ds(pl.multiple_of(p * size, size), size)
        clear_rows(span, dk_acc, dv_acc)
        attend_back_group(span, p, 0, span.blocks, q, k, v, gmixed, bias, lse, inner, dk_acc, dv_acc, dq)
        dk[:, cols] = dk_acc[span.window:, :]
        dv[:, cols] = dv_acc[span.window:, :]

        @pl.loop(span.start // BLOCK, span.window // BLOCK)
        def _(j):
            r = rows_at(j * BLOCK, BLOCK)
            wk[r, cols] = bf(dk_acc[r, :])
            wv[r, cols] = bf(dv_acc[r, :])


def backward_call(fsdp, reach, q, k, v, gmixed, mixed, lse, segs, trees, table):
    window, width = k.shape
    rows = q.shape[0]
    s, low, full = jax.ShapeDtypeStruct, jnp.bfloat16, jnp.float32
    early = window - rows
    outs = (s((rows, width), low), s((rows, width), full), s((rows, width), full), s((early, width), low), s((early, width), low))
    return pl.pallas_call(
        functools.partial(backward_kernel, fsdp, reach), out_shape=outs, in_specs=[VM] * 7 + [SM, VM], out_specs=[VM] * 5,
        scratch_shapes=[
            pltpu.VMEM((rows // BLOCK, 3 * BLOCK, BLOCK), full), pltpu.VMEM(lse.shape, full),
            pltpu.VMEM((window, GROUP * 2 * HEAD), full), pltpu.VMEM((window, GROUP * 2 * HEAD), full),
        ],
        compiler_params=pltpu.CompilerParams(vmem_limit_bytes=58 << 20),
    )(q, k, v, gmixed, mixed, lse, segs, trees, table)


def projection_back(span, x, n1, dq, dk, dv, lnp, w1, w2, gres, gin, gfirst, g1, g2, sums, n1_t, cat1, cat2):
    rows = span.rows
    third = w1.shape[1] // 4
    half = 2 * third
    fresh = third + BLOCK
    tile = row_tiles(rows)
    transpose_all(n1, n1_t)

    @pl.loop(0, rows // tile)
    def _(t):
        r = rows_at(t * tile, tile)
        cat1[r, :half] = dq[r, :half]
        cat1[r, half:] = bf(dk[r, :half])
        cat2[r, :third] = dq[r, half:]
        cat2[r, third:half] = bf(dv[r, :third])
        cat2[r, half:half + third] = bf(dk[r, half:])
        cat2[r, half + third:half + third + BLOCK] = bf(dv[r, third:fresh])
        cat2[r, half + third + BLOCK:] = jnp.zeros((tile, BLOCK), jnp.bfloat16)
        gfirst[r, :] = dv[r, fresh:]

    g1[...] = bf(mm(n1_t[...], cat1[...]))
    g2[...] = bf(mm(n1_t[...], cat2[...]))

    @pl.loop(0, rows // tile)
    def _(t):
        r = rows_at(t * tile, tile)
        g = nt(cat1[r, :], w1[...]) + nt(cat2[r, :], w2[...])
        hat, inv = normalized(f32(x[rows_at(span.window + t * tile, tile), :]))
        gin[r, :] = gres[r, :] + norm_back(hat, inv, g, lnp[0:1, :])
        sums[0:1, :] += jnp.sum(g * hat, axis=0, keepdims=True)
        sums[1:2, :] += jnp.sum(g, axis=0, keepdims=True)


def projection_back_kernel(fsdp, reach, x, n1, dq, dk, dv, lnp, w1, w2, gres, sums_in, gin, gfirst, g1, g2, sums, n1_t, cat1, cat2):
    span = Span(fsdp, dq.shape[0], reach, lax.axis_index("fsdp"))
    sums[...] = sums_in[...]
    projection_back(span, x, n1, dq, dk, dv, lnp, w1, w2, gres, gin, gfirst, g1, g2, sums, n1_t, cat1, cat2)


def projection_back_call(fsdp, reach, x, n1, dq, dk, dv, lnp, w1, w2, gres, sums):
    rows, width = dq.shape
    s, low, full = jax.ShapeDtypeStruct, jnp.bfloat16, jnp.float32
    outs = (s((rows, width), full), s((rows, width // 2), full), s(w1.shape, low), s(w2.shape, low), s((8, width), full))
    return pl.pallas_call(
        functools.partial(projection_back_kernel, fsdp, reach), out_shape=outs, in_specs=[VM] * 10, out_specs=[VM] * 5,
        scratch_shapes=[pltpu.VMEM((width, rows), low), pltpu.VMEM((rows, w1.shape[1]), low), pltpu.VMEM((rows, w1.shape[1]), low)],
        compiler_params=pltpu.CompilerParams(vmem_limit_bytes=58 << 20),
    )(x, n1, dq, dk, dv, lnp, w1, w2, gres, sums)


def gather_steps(items, u):
    for s, stage in enumerate(Gather.STAGES[:3]):
        c = u - s

        @pl.when((c >= 0) & (c < items.count))
        def _():
            for g in items(c):
                stage(g)


REDUCE_AT = (0, 1, 3, 4, 6, 7, 8)


def reduce_steps(items, u):
    for s, stage in enumerate(Reduce.STAGES[:7]):
        c = u - REDUCE_AT[s]

        @pl.when((c >= 0) & (c < items.count))
        def _():
            for g in items(c):
                stage(g)


class Chunks:
    def __init__(self, count, make):
        self.count, self.make = count, make

    def __call__(self, c):
        return self.make(c)


N_IN = 13


class Scratch:
    def __init__(self):
        self.names, self.shapes = [], []

    def add(self, name, shape):
        self.names.append(name)
        self.shapes.append(shape)

    def bind(self, refs):
        for name, ref in zip(self.names, refs):
            setattr(self, name, ref)
        return self


def layer_kernel(fsdp, n_ff, scratch, n_out, *refs):
    (inputs, first, cot_in, a_q, a_k, a_v, a_o, a_in, a_dn, norms, segs, trees, table) = refs[:N_IN]
    (outputs, gin, gfirst, rs_q, rs_k, rs_v, rs_o, rs_in, rs_dn, rs_vec) = refs[N_IN : N_IN + n_out]
    m = scratch.bind(refs[N_IN + n_out :])
    pc = Place(fsdp)
    f = pc.f
    rows, width = cot_in.shape
    span = Span(fsdp, rows, 1, f)
    tile = row_tiles(rows)
    tiles = rows // tile
    last = fsdp - 1
    flat = lambda ref: ref.reshape(-1, ref.shape[-1])
    w_q, w_k, w_v, w_o = (flat(b) for b in (m.b_q, m.b_k, m.b_v, m.b_o))
    mixed, cot = m.mixed.reshape(rows, width), m.cot.reshape(rows, width)
    x, q, k, v, n1, n2, tr = m.x, m.q, m.k, m.v, m.n1, m.n2, m.tr

    kind, next_kind = span.kind(0), lax.rem(span.first + span.blocks, span.tree)
    guest = kind >= 4
    host = (f < last) & (next_kind >= 4)
    lent_keys = jnp.where(kind == 6, 768, jnp.where(kind == 4, 512, 0))
    size = GROUP * 2 * HEAD

    def run_cols(p):
        return pl.ds(pl.multiple_of(p * size, size), size)

    def lend(i, src, dst):
        return pltpu.make_async_remote_copy(src_ref=src, dst_ref=dst, send_sem=m.b_send.at[i], recv_sem=m.b_recv.at[i], device_id=(pc.r, f - 1), device_id_type=MESH)

    most = 4 * BLOCK
    gq, gg = x.at[pl.ds(0, most)], x.at[pl.ds(most, most)]

    def sized(own, act):
        for start in (4, 6):
            ok = (f > 0) & (kind == start) if own else (f < last) & (next_kind == start)

            @pl.when(ok)
            def _():
                act((8 - start) * BLOCK)

    def lent_q(n):
        return lend(0, q.at[pl.ds(0, n)], gq.at[pl.ds(0, n)])

    def lent_rows():
        return [lend(1, m.lse, m.g_lse), lend(2, m.inner, m.g_inner)]

    def lent_run(p, n):
        return lend(3 + p, n2.at[pl.ds(0, n), run_cols(p)], gg.at[pl.ds(0, n), run_cols(p)])

    def local(src, dst, sem):
        c = pltpu.make_async_copy(src, dst, sem)
        c.start()
        return c

    half = width // 2
    lw = [
        local(a, b.at[f, :, :, :, pl.ds(0, a.shape[-1])], m.l_sem.at[1 + i])
        for i, (a, b) in enumerate(((a_q, m.b_q), (a_k, m.b_k), (a_v, m.b_v), (a_o, m.b_o)))
    ]
    lx = local(inputs, x.at[pl.ds(rows, rows)], m.l_sem.at[5])
    lf = local(first, v.at[pl.ds(rows, rows), pl.ds(width // 2, width // 2)], m.l_sem.at[6])
    lc = local(cot_in, cot, m.l_sem.at[7])
    group = a_in.shape[-1] // fsdp

    def own_chunk(c, act):
        for g in range(fsdp):
            cols = pl.ds(pl.multiple_of(g * group + c * BLOCK, BLOCK), BLOCK)
            act(pltpu.make_async_copy(a_in.at[:, :, :, cols], m.b_in.at[c, f, :, :, :, pl.ds(g * BLOCK, BLOCK)], m.lc_sem.at[c, g]))
        act(pltpu.make_async_copy(a_dn.at[c], m.b_dn.at[c, f], m.lc_sem.at[c, fsdp]))

    @pl.loop(0, n_ff)
    def _(c):
        own_chunk(c, lambda d: d.start())

    pad = m.b_v.shape[-1] - half
    m.b_v[f, :, :, :, half:] = jnp.zeros((2, 2, m.b_v.shape[3], pad), jnp.bfloat16)
    own_norms = jnp.concatenate([f32(norms[...]), jnp.zeros((4, norms.shape[1]), jnp.float32)], axis=0)
    own_norms = jnp.concatenate([own_norms, jnp.zeros((8, width - norms.shape[1]), jnp.float32)], axis=1)
    m.vec[f] = pltpu.roll(own_norms, f * norms.shape[1], 1)
    pc.barrier()
    for o in pc.others:
        pltpu.make_async_remote_copy(
            src_ref=m.vec.at[f], dst_ref=m.vec.at[f], send_sem=m.v_send.at[0], recv_sem=m.v_recv.at[0], device_id=pc.zdev(o), device_id_type=MESH
        ).start()
    gat = [Gather(pc, b, m.g_send.at[i], m.g_recv.at[i], xf, i < 3) for i, (b, xf) in enumerate(((m.b_q, True), (m.b_k, False), (m.b_v, True), (m.b_o, False)))]
    for l, g in zip(lw, gat):
        l.wait()
        g.z_start()

    next_start = Span(fsdp, rows, 1, f + 1).start

    def window(t):
        r, own = pl.ds(t * tile, tile), pl.ds(rows + t * tile, tile)
        nxt = (pc.r, f + 1)
        return [
            pltpu.make_async_remote_copy(src_ref=x.at[own], dst_ref=x.at[r], send_sem=m.w_send.at[0, t], recv_sem=m.w_recv.at[0, t], device_id=nxt, device_id_type=MESH),
            pltpu.make_async_remote_copy(
                src_ref=v.at[own, pl.ds(half, half)], dst_ref=v.at[r, pl.ds(half, half)], send_sem=m.w_send.at[1, t], recv_sem=m.w_recv.at[1, t], device_id=nxt, device_id_type=MESH
            ),
        ]

    ff = Chunks(
        n_ff,
        lambda c: [Gather(pc, m.b_in.at[c], m.gi_send.at[c], m.gi_recv.at[c], True), Gather(pc, m.b_dn.at[c], m.gd_send.at[c], m.gd_recv.at[c], False)],
    )

    make_bias(span, segs, trees, table, m.bias, jnp.where((f < last) & (next_kind == 6), 2, 0))
    for g in gat:
        drain(g.three(), g.s.at[0])
    lx.wait()
    lf.wait()
    for t in range(tiles):

        @pl.when((f < last) & (t * tile >= next_start))
        def _():
            for c in window(t):
                c.start()


    for g in gat[:3]:
        g.z_wait()
        g.a_start()
    v3 = m.vec.at[pl.ds(0, last)]
    drain(v3, m.v_recv.at[0])
    drain(v3, m.v_send.at[0])
    m.lnp[...] = functools.reduce(lambda a, b: a + b, [m.vec[j] for j in range(fsdp)])
    gain, shift = m.lnp[0:1, :], m.lnp[1:2, :]

    @pl.loop(0, tiles)
    def _(t):
        n1[rows_at(t * tile, tile), :] = norm_tile(x[rows_at(rows + t * tile, tile), :], gain, shift)

    for g in gat[:3]:
        g.a_wait()
        g.b_start()
    for g in gat[:3]:
        g.b_wait()
        g.c_start()
    for g in gat[:3]:
        g.c_wait()

    @pl.loop(0, tiles)
    def _(t):
        r, own = rows_at(rows + t * tile, tile), rows_at(t * tile, tile)
        n = n1[own, :]
        q[own, :] = bf(f32(bf(mm(n, w_q[...]))) * HEAD ** (-0.5))
        k[r, :] = bf(mm(n, w_k[...]))
        v[r, :half] = bf(mm(n, w_v[:, :half]))

    pairs = width // (2 * HEAD)
    here = lax.rem(span.tree - lax.rem(span.first, span.tree), span.tree)
    here = jnp.minimum(here, span.blocks)
    border = span.base(here)

    groups = pairs // GROUP

    @pl.loop(0, groups)
    def _(p):
        attend_group(span, p, here, span.blocks, q, k, v, m.bias, mixed, m.lse)

    for t in range(tiles):

        @pl.when((f < last) & (t * tile >= next_start))
        def _():
            for c in window(t):
                c.wait_send()

    @pl.loop(0, n_ff)
    def _(c):
        own_chunk(c, lambda d: d.wait())
        for g in ff(c):
            g.z_start()

    for stage in Gather.STAGES[:3]:
        stage(gat[3])

    for t in range(tiles):

        @pl.when(t * tile >= span.start)
        def _():
            r = pl.ds(t * tile, tile)
            drain(x.at[r], m.w_recv.at[0, t])
            drain(v.at[r, pl.ds(half, half)], m.w_recv.at[1, t])
            n = norm_tile(x[r, :], gain, shift)
            k[r, :] = bf(mm(n, w_k[...]))
            v[r, :half] = bf(mm(n, w_v[:, :half]))


    @pl.loop(0, 2 * groups)
    def _(s):
        p, part = s // 2, lax.rem(s, 2)
        middle = here // 2
        attend_group(span, p, part * middle, jnp.where(part == 0, middle, here), q, k, v, m.bias, mixed, m.lse)
        gather_steps(ff, s - 2 * groups + 2)

    gat[3].c_wait()
    branch_out(span, x, m.lnp, mixed, w_o, m.resid, n2)
    @pl.when(host)
    def _():
        pl.semaphore_signal(m.freed, inc=1, device_id=(pc.r, f + 1), device_id_type=MESH)

    gather_steps(ff, 2)
    for g in gat:
        g.finish(1)

    lc.wait()
    transpose_all(n2, tr)
    m.acc1[...] = m.resid[...]
    m.acc2[...] = jnp.zeros_like(m.acc2)
    red = Chunks(
        n_ff,
        lambda c: [
            Reduce(pc, m.b_in.at[c], *(a.at[c] for a in m.r_in), rs_in.at[c], m.ri_send.at[c], m.ri_recv.at[c], True),
            Reduce(pc, m.b_dn.at[c], *(a.at[c] for a in m.r_dn), rs_dn.at[c], m.rd_send.at[c], m.rd_recv.at[c], False),
        ],
    )
    hid, gact = m.back.at[0, :, pl.ds(0, fsdp * BLOCK)], m.back.at[1, :, pl.ds(0, fsdp * BLOCK)]

    @pl.loop(0, n_ff)
    def _(c):
        for g in ff(c):
            Gather.STAGES[3](g)

        b_in, b_dn = flat(m.b_in.at[c]), flat(m.b_dn.at[c])

        def put_in(val):
            b_in[...] = val

        def put_dn(val):
            b_dn[...] = val

        mlp_chunk(rows, n2, tr, cot, lambda: b_in[...], lambda: b_dn[...], m.acc1, m.acc2, hid, gact, put_in, put_dn, lambda: gather_steps(ff, c + 3))
        reduce_steps(red, c)

        @pl.when(guest & (c == 2))
        def _():
            pl.semaphore_wait(m.freed, 1)
            sized(True, lambda n: lent_q(n).start())


    @pl.loop(0, tiles)
    def _(t):
        r = rows_at(t * tile, tile)
        m.back[0, r, :] = bf(m.acc1[r, :])

    lo = local(m.back.at[0], outputs, m.l_sem.at[0])
    m.sums[...] = jnp.zeros_like(m.sums)
    second_norm_back(rows, m.lnp, m.resid, cot, m.acc2, m.resid, n2, m.sums)
    d_o = flat(m.cot)

    @pl.loop(0, width // tile)
    def _(t):
        r = rows_at(t * tile, tile)
        d_o[r, :] = bf(tn(mixed[:, pl.ds(pl.multiple_of(t * tile, tile), tile)], n2[...]))

    gmixed = n2
    branch_back(rows, n2, w_o, gmixed)
    head_sums(gmixed, mixed, m.inner)

    @pl.when(guest)
    def _():
        for c in lent_rows():
            c.start()

    sized(True, lambda n: lent_run(0, n).start())
    lo.wait()

    @pl.when((f < last) & jnp.logical_not(host))
    def _():
        pl.semaphore_signal(m.ready, inc=1, device_id=(pc.r, f + 1), device_id_type=MESH)

    sized(True, lambda n: lent_q(n).wait_send())

    transpose_all(n1, tr)
    mid, end = half + (pairs // 2 - GROUP) * BLOCK, width
    wide = 2 * (mid - half)
    rest = lambda ref: (ref.at[..., pl.ds(0, wide)], ref.at[..., pl.ds(wide, width - wide)])
    narrow = lambda refs, i: [ref.at[..., pl.ds(0, wide // 2) if i == 0 else pl.ds(wide // 2, half - wide // 2)] for ref in refs]
    buf1, buf2 = rest(m.b_o)
    res1, res2 = rest(rs_k)
    stat = [
        Reduce(pc, b, *scr, res, m.rs_send.at[i], m.rs_recv.at[i], xf)
        for i, (b, scr, res, xf) in enumerate(
            (
                (m.cot, m.r_o, rs_o, True), (m.mixed, m.r_q, rs_q, False), (m.g_v, m.r_v, rs_v, True),
                (buf1, narrow(m.r_k, 0), res1, True), (buf2, narrow(m.r_k, 1), res2, False),
            )
        )
    ]
    red_o, red_0, red_v, red_1, red_2 = stat

    def early(t, p):
        r, cols = pl.ds(t * tile, tile), run_cols(p)
        prev = (pc.r, f - 1)
        return [
            pltpu.make_async_remote_copy(
                src_ref=x.at[pl.ds(j * rows + t * tile, tile), cols], dst_ref=m.back.at[j, r, cols], send_sem=m.e_send.at[j, p, t], recv_sem=m.e_recv.at[j, p, t],
                device_id=prev, device_id_type=MESH,
            )
            for j in range(2)
        ]

    dk, dv = m.acc1, m.acc2

    def complete(g):
        cols = pl.ds(g * size, size)
        fresh = min(size, max(0, half - g * size))
        for t in range(tiles):
            r = pl.ds(t * tile, tile)

            @pl.when((f < last) & jnp.logical_not(host) & (t * tile >= next_start))
            def _():
                for j, own in enumerate((dk, dv)):
                    drain(m.back.at[j, r, cols], m.e_recv.at[j, g, t])
                    own[r, cols] += f32(m.back[j, r, cols])

            k[r, cols] = bf(dk[r, cols])
            if fresh:
                v[r, g * size:g * size + fresh] = bf(dv[r, g * size:g * size + fresh])

    def weight_grad(dst, at, grad, lo, hi):
        @pl.loop(0, width // tile)
        def _(t):
            r = rows_at(t * tile, tile)
            dst[r, at:at + hi - lo] = bf(mm(tr[r, :], grad[pl.ds(0, rows), lo:hi]))

    d_0, d_v, d_1 = flat(m.mixed), flat(m.g_v), w_o

    def run_0():
        complete(0)
        complete(1)
        weight_grad(d_0, 0, q, 0, half)
        weight_grad(d_0, half, k, 0, half)
        red_0.p1()
        d_v[:, half:] = jnp.zeros((width, d_v.shape[1] - half), jnp.bfloat16)
        weight_grad(d_v, 0, v, 0, half)
        red_v.p1()

    @pl.loop(0, 2 * groups)
    def _(s):
        p, part = s // 2, lax.rem(s, 2)
        cols = run_cols(p)
        middle = span.blocks // 2

        @pl.when(part == 0)
        def _():
            clear_rows(span, m.dk_acc, m.dv_acc)

        attend_back_group(
            span, p, part * middle, jnp.where(part == 0, middle, span.blocks), q, k, v, gmixed, m.bias, m.lse, m.inner, m.dk_acc, m.dv_acc, q, lent_keys
        )

        reduce_steps(red, n_ff + s)

        @pl.when((part == 0) & (p < groups - 1))
        def _():
            sized(True, lambda n: lent_run(p + 1, n).start())

        @pl.when(s == 1)
        def _():
            @pl.when((f > 0) & jnp.logical_not(guest))
            def _():
                pl.semaphore_wait(m.ready, 1)

        @pl.when(part == 1)
        def _():
            dk[:, cols] = m.dk_acc[rows:, :]
            dv[:, cols] = m.dv_acc[rows:, :]
            for t in range(tiles):

                @pl.when((f > 0) & jnp.logical_not(guest) & (t * tile >= span.start))
                def _():
                    r = pl.ds(t * tile, tile)
                    x[r, cols] = bf(m.dk_acc[r, :])
                    x[pl.ds(rows + t * tile, tile), cols] = bf(m.dv_acc[r, :])
                    for c in early(t, p):
                        c.start()

        @pl.when(host & (part == 1))
        def _():
            @pl.when(p == 0)
            def _():
                sized(False, lambda n: lent_q(n).wait_recv())
                for c in lent_rows():
                    c.wait_recv()

            sized(False, lambda n: lent_run(p, n).wait_recv())
            for j in range(GROUP):
                at = (span, p * GROUP + j, group_cols(p, j, GROUP))
                rest = (gq, gg, k, v, m.bias, m.g_lse, m.g_inner, dk, dv)
                trunk = ((0, 256, None), (256, 256, None))

                @pl.when(next_kind == 6)
                def _():
                    borrowed_back(*at, 0, (*trunk, (512, 256, 0)), *rest)

                @pl.when(next_kind == 4)
                def _():
                    @pl.loop(0, 2)
                    def _(n):
                        borrowed_back(*at, 2 * n, trunk, *rest)

        for i in range(4):

            @pl.when(s == REDUCE_AT[i])
            def _():
                Reduce.STAGES[i](red_o)

        @pl.when(s == 2 * groups - 2)
        def _():
            run_0()

        @pl.when(s == 2 * groups - 1)
        def _():
            red_0.p2()
            red_v.p2()

    weight_grad(d_1, 0, q, half, mid)
    weight_grad(d_1, mid - half, k, half, mid)
    red_1.p1()
    weight_grad(d_1, wide, q, mid, end)
    red_0.p3()
    red_v.p3()
    red_o.p5()
    complete(groups - 1)
    weight_grad(d_1, wide + end - mid, k, mid, end)
    red_2.p1()
    gf = local(dv.at[:, pl.ds(half, half)], gfirst, m.l_sem.at[1])
    lx = local(inputs, n1, m.l_sem.at[2])
    red_1.p2()
    red_2.p2()
    red_0.p4()
    red_v.p4()

    @pl.loop(0, tiles)
    def _(t):
        r = rows_at(t * tile, tile)
        dk[r, :] = nt(q[r, :], w_q[...]) + nt(k[r, :], w_k[...]) + nt(v[r, :half], w_v[:, :half])

    red_2.p3()
    red_1.p3()
    reduce_steps(red, n_ff + pairs)
    red_o.p6()
    lx.wait()

    @pl.loop(0, tiles)
    def _(t):
        r = rows_at(t * tile, tile)
        g = dk[r, :]
        hat, inv = normalized(f32(n1[r, :]))
        m.resid[r, :] += norm_back(hat, inv, g, m.lnp[0:1, :])
        m.sums[0:1, :] += jnp.sum(g * hat, axis=0, keepdims=True)
        m.sums[1:2, :] += jnp.sum(g, axis=0, keepdims=True)

    gi = local(m.resid, gin, m.l_sem.at[3])

    def exchange(src, dst, i, dev):
        c = pltpu.make_async_remote_copy(src_ref=src, dst_ref=dst, send_sem=m.v_send.at[i], recv_sem=m.v_recv.at[i], device_id=dev, device_id_type=MESH)
        c.start()
        return c

    cur = m.sums
    work = [
        (red_2.p4, red_1.p4, red_0.p5, red_v.p5), (red_0.p6, red_v.p6), (red_2.p5, red_1.p5, red_0.p7, red_v.p7),
    ]
    for i, dev in enumerate((pc.core, pc.xn, pc.yn)):
        c = exchange(cur, m.s_pair.at[i], 1 + i, dev)
        for step in work[i]:
            step()
        c.wait()
        m.s_pair[i] = m.s_pair[i] + cur[...]
        cur = m.s_pair.at[i]
    for o in pc.others:
        exchange(cur, m.s_z.at[f], 4, pc.zdev(o))
    red_2.p6()
    red_1.p6()
    red_o.p7()
    for u in range(n_ff + pairs + 1, n_ff + REDUCE_AT[-1]):
        reduce_steps(red, u)
    red_2.p7()
    red_1.p7()
    z3 = m.s_z.at[pl.ds(0, last)]
    drain(z3, m.v_recv.at[4])
    drain(z3, m.v_send.at[4])
    m.s_z[f] = cur[...]
    rs_vec[...] = functools.reduce(lambda a, b: a + b, [m.s_z[j] for j in range(fsdp)])
    for g in stat:
        g.p8()
        g.finish()

    @pl.loop(0, n_ff)
    def _(c):
        for g in red(c):
            g.p8()
            g.finish()

    @pl.loop(0, groups)
    def _(p):
        for t in range(tiles):

            @pl.when((f > 0) & jnp.logical_not(guest) & (t * tile >= span.start))
            def _():
                for c in early(t, p):
                    c.wait_send()

    def sent(n):
        for c in lent_rows():
            c.wait_send()
        for p in range(groups):
            lent_run(p, n).wait_send()

    sized(True, sent)
    gf.wait()
    gi.wait()


def layer_call(fsdp, inputs, first, cot, norms, w_query, w_key, w_value, w_out, w_in, w_down, segs, trees, table):
    rows, width = inputs.shape
    shard = w_query.shape[0]
    n_ff = w_down.shape[0] // BLOCK
    low, full = jnp.bfloat16, jnp.float32
    mq, md = shard // 4, BLOCK // 4
    pairs, blocks = width // (2 * HEAD), rows // BLOCK
    wide_v = width // 2 + BLOCK
    split = lambda a: a.reshape(2, 2, mq, a.shape[1])
    buf = lambda m, c, lead=(): (*lead, fsdp, 2, 2, m, c)
    chunk = fsdp * BLOCK
    sc = Scratch()
    V, D = pltpu.VMEM, pltpu.SemaphoreType.DMA
    for name, shape in (
        ("b_q", buf(mq, width)), ("b_k", buf(mq, width)), ("b_v", buf(mq, wide_v)), ("b_o", buf(mq, width)),
        ("b_in", buf(mq, chunk, (n_ff,))), ("b_dn", buf(md, width, (n_ff,))), ("g_v", buf(mq, wide_v)),
        ("mixed", buf(mq, width)), ("cot", buf(mq, width)), ("x", (2 * rows, width)), ("k", (2 * rows, width)), ("v", (2 * rows, width)),
        ("q", (rows, width)), ("n1", (rows, width)), ("n2", (rows, width)), ("tr", (width, rows)), ("back", (2, rows, width)),
    ):
        sc.add(name, V(shape, low))
    for name, shape in (
        ("vec", (fsdp, 8, width)), ("lnp", (8, width)), ("sums", (8, width)), ("s_pair", (3, 8, width)), ("s_z", (fsdp, 8, width)),
        ("resid", (rows, width)), ("acc1", (rows, width)), ("acc2", (rows, width)), ("bias", (blocks + 2, 3 * BLOCK, BLOCK)), ("inner", (pairs, 8, 2 * BLOCK)), ("g_inner", (pairs, 8, 2 * BLOCK)), ("g_lse", (pairs, -(-blocks // 8) * 8, 2 * BLOCK)),
        ("dk_acc", (2 * rows, GROUP * 2 * HEAD)), ("dv_acc", (2 * rows, GROUP * 2 * HEAD)), ("lse", (pairs, -(-blocks // 8) * 8, 2 * BLOCK)),
    ):
        sc.add(name, V(shape, full))
    for name, shape in (
        ("l_sem", (9,)), ("lc_sem", (n_ff, fsdp + 1)), ("v_send", (5,)), ("v_recv", (5,)), ("g_send", (4, 5)), ("g_recv", (4, 5)),
        ("w_send", (2, rows // row_tiles(rows))), ("w_recv", (2, rows // row_tiles(rows))),
        ("gi_send", (n_ff, 5)), ("gi_recv", (n_ff, 5)), ("gd_send", (n_ff, 5)), ("gd_recv", (n_ff, 5)),
        ("ri_send", (n_ff, 8)), ("ri_recv", (n_ff, 8)), ("rd_send", (n_ff, 8)), ("rd_recv", (n_ff, 8)), ("rs_send", (5, 8)), ("rs_recv", (5, 8)),
        ("b_send", (3 + pairs,)), ("b_recv", (3 + pairs,)), ("e_send", (2, pairs // GROUP, rows // row_tiles(rows))), ("e_recv", (2, pairs // GROUP, rows // row_tiles(rows))),
    ):
        sc.add(name, D(shape))
    sc.add("ready", pltpu.SemaphoreType.REGULAR)
    sc.add("freed", pltpu.SemaphoreType.REGULAR)
    groups = (("r_in", buf(mq, chunk), n_ff), ("r_dn", buf(md, width), n_ff), ("r_o", buf(mq, width), 0), ("r_q", buf(mq, width), 0), ("r_k", buf(mq, width), 0), ("r_v", buf(mq, wide_v), 0))
    for name, shape, lead in groups:
        for i, sub in enumerate(red_shapes(shape)):
            sc.add(f"{name}{i}", V((lead, *sub) if lead else sub, low))

    n_out = 10
    s = jax.ShapeDtypeStruct
    outs = (
        s((rows, width), low), s((rows, width), full), s((rows, width // 2), full),
        s((2, 2, mq, width), low), s((2, 2, mq, width), low), s((2, 2, mq, wide_v), low), s((2, 2, mq, width), low),
        s((n_ff, 2, 2, mq, chunk), low), s((n_ff, 2, 2, md, width), low), s((8, width), full),
    )

    def body(*refs):
        names = Scratch()
        names.names, names.shapes = sc.names, sc.shapes
        bound = names.bind(refs[N_IN + n_out :])
        for name, _, _ in groups:
            setattr(bound, name, [getattr(bound, f"{name}{i}") for i in range(4)])
        layer_kernel(fsdp, n_ff, bound, n_out, *refs)

    any_ = pl.BlockSpec(memory_space=pl.ANY)
    return pl.pallas_call(
        body, out_shape=outs, in_specs=[any_] * 9 + [VM] * 2 + [SM, VM], out_specs=[any_] * 3 + [VM] * 7, scratch_shapes=sc.shapes,
        compiler_params=pltpu.CompilerParams(collective_id=3, has_side_effects=True, vmem_limit_bytes=63 << 20),
    )(inputs, first, cot, split(w_query), split(w_key), split(w_value), split(w_out), split(w_in), w_down.reshape(n_ff, 2, 2, md, width), norms, segs, trees, table)


def finish_kernel(o_in, g_in, f_in, vec, *refs):
    src, (o_out, g_out, f_out, *dst), rows_out = refs[:6], refs[6:15], refs[15]
    low, full, passed, sem, load = refs[16:22], refs[22:28], refs[28:31], refs[31], refs[32]
    copies = []

    def go(src, dst):
        c = pltpu.make_async_copy(src, dst, sem.at[len(copies)])
        c.start()
        copies.append(c)

    loads = [pltpu.make_async_copy(a, b, load.at[i]) for i, (a, b) in enumerate(zip((*src, g_in, o_in, f_in), (*low, *passed)))]
    for c in loads[6:] + loads[:6]:
        c.start()
    (l_in, l_dn, l_0, l_1, l_o, l_v), (d_in, d_dn, d_q, d_k, d_o, d_v) = low, full

    def done(i, mid):
        go(mid, dst[i])

    n_ff, width = l_in.shape[0], l_0.shape[1]
    half = width // 2
    for c, a, b in zip(loads[6:], passed, (g_out, o_out, f_out)):
        c.wait()
        go(a, b)
    loads[0].wait()
    for j in range(n_ff):
        for g in range(l_in.shape[2] // BLOCK):
            at = (g * n_ff + j) * BLOCK
            d_in[:, at:at + BLOCK] = f32(l_in[j, :, g * BLOCK:(g + 1) * BLOCK])
    done(0, d_in)
    loads[1].wait()
    for j in range(n_ff):
        d_dn[j * BLOCK:(j + 1) * BLOCK, :] = f32(l_dn[j])
    done(1, d_dn)
    loads[2].wait()
    loads[3].wait()
    rest = half - GROUP * BLOCK
    tail = half - rest
    for i, mid in ((2, d_q), (3, d_k)):
        s = i - 2
        mid[:, :half] = f32(l_0[:, s * half:(s + 1) * half])
        mid[:, half:half + rest] = f32(l_1[:, s * rest:(s + 1) * rest])
        mid[:, half + rest:] = f32(l_1[:, 2 * rest + s * tail:2 * rest + (s + 1) * tail])
        done(i, mid)
    loads[4].wait()
    d_o[...] = f32(l_o[...])
    done(4, d_o)
    loads[5].wait()
    d_v[...] = f32(l_v[:, :half])
    done(5, d_v)
    rows, width = rows_out.shape[1], vec.shape[1]
    turned = pltpu.roll(vec[...], lax.rem(width - lax.axis_index("fsdp") * rows, width), 1)
    rows_out[...] = turned[:, :rows]
    for c in copies:
        c.wait()


def finish_call(outputs, gin, gfirst, rq, rk, rv, ro, ri, rd, vec):
    rows, width = rq.shape
    full = jnp.float32
    s = jax.ShapeDtypeStruct
    grads = (ri, rd, rq, rk, ro, rv)
    shapes = [(rows, ri.shape[0] * ri.shape[2]), (rd.shape[0] * BLOCK, width), (rows, width), (rows, width), (rows, width), (rows, width // 2)]
    hbm = pl.BlockSpec(memory_space=pltpu.HBM)
    out = pl.pallas_call(
        finish_kernel,
        out_shape=(s(outputs.shape, outputs.dtype), s(gin.shape, full), s(gfirst.shape, full), *(s(a, full) for a in shapes), s((8, rows), full)),
        in_specs=[hbm] * 3 + [VM] + [hbm] * 6, out_specs=[hbm] * 9 + [VM],
        scratch_shapes=[*(pltpu.VMEM(a.shape, a.dtype) for a in grads), *(pltpu.VMEM(a, full) for a in shapes), *(pltpu.VMEM(a.shape, a.dtype) for a in (gin, outputs, gfirst)), pltpu.SemaphoreType.DMA((9,)), pltpu.SemaphoreType.DMA((9,))],
        compiler_params=pltpu.CompilerParams(vmem_limit_bytes=61 << 20),
    )(outputs, gin, gfirst, vec, *grads)
    din, ddn, dq, dk, do, dv = out[3:9]
    return out[0], out[1], out[2], dq, dk, dv, do, din, ddn, out[9]


def shifted(block, axis, distance):
    devices = range(lax.axis_size(axis))
    route = [(i - distance, i) for i in devices if i - distance in devices]
    return lax.ppermute(block, axis, route)


def reorder_rows(grad_block, fsdp_count, rep_count):
    return grad_block.reshape(fsdp_count, rep_count, -1).transpose(1, 0, 2).reshape(-1)


def packed_qkv(query, key, value):
    h, pad = query.shape[1] * 2 // 3, jnp.zeros_like(value[:, : value.shape[1] // 3])
    n = value.shape[1] * 2 // 3
    return jnp.concatenate([query[:, :h], key[:, :h], query[:, h:], value[:, :n], key[:, h:], value[:, n:], pad], axis=1)


def unpacked_qkv(first, second):
    h = first.shape[-1] // 2
    q = h // 2
    return (
        jnp.concatenate([first[..., :h], second[..., :q]], axis=-1),
        jnp.concatenate([first[..., h:], second[..., h : h + q]], axis=-1),
        jnp.concatenate([second[..., q:h], second[..., h + q : h + q + q // 2]], axis=-1),
    )


def gathered(fsdp, gain1, shift1, gain2, shift2, w_query, w_key, w_value, w_out, w_in, w_down):
    width = w_query.shape[1]
    n_ff = w_down.shape[0] // BLOCK
    packed = packed_qkv(w_query, w_key, w_value)
    full = [lax.all_gather(v, "fsdp", axis=0, tiled=True) for v in (packed, w_out, w_in, w_down)]
    vec = lax.all_gather(jnp.stack([gain1, shift1, gain2, shift2]), "fsdp", axis=1, tiled=True).astype(jnp.float32)
    half = packed.shape[1] // 2
    inner = full[2].reshape(width, fsdp, n_ff, BLOCK).transpose(2, 0, 1, 3).reshape(n_ff, width, -1)
    down = full[3].reshape(fsdp, n_ff, BLOCK, width).transpose(1, 0, 2, 3).reshape(n_ff, -1, width)
    return jnp.pad(vec, ((0, 4), (0, 0))), full[0][:, :half], full[0][:, half:], full[1], inner, down


def reduced(fsdp, sums, g1, g2, go, gin, gdn):
    width = go.shape[0]
    rows = width // fsdp
    n_ff = gin.shape[0]
    both = ("rep", "fsdp")
    rep = lax.axis_size("rep")

    def total(a):
        piece = lax.psum_scatter(reorder_rows(a.astype(jnp.float32), fsdp, rep), both, scatter_dimension=0, tiled=True)
        return lax.all_gather(piece.astype(jnp.bfloat16), "rep", axis=0, tiled=True)

    first, second, ro = (total(a).reshape(rows, -1) for a in (g1, g2, go))
    ri = total(gin.transpose(1, 0, 2)).reshape(rows, n_ff, -1).transpose(1, 0, 2)
    rd = total(gdn.reshape(n_ff, fsdp, BLOCK, width).transpose(1, 0, 2, 3)).reshape(n_ff, BLOCK, width)
    return lax.psum(sums, both), *unpacked_qkv(first, second), ro, ri, rd


def one_kernel(inputs, first_values, cotangent, segs, trees, table, gain1, shift1, gain2, shift2, w_query, w_key, w_value, w_out, w_in, w_down):
    fsdp = lax.axis_size("fsdp")
    rows, width = w_query.shape
    norms = jnp.concatenate([gain1, shift1, gain2, shift2]).reshape(4, rows)
    outputs, input_grad, first_grad, rq, rk, rv, ro, ri, rd, sums = layer_call(
        fsdp, inputs, first_values, cotangent, norms, w_query, w_key, w_value, w_out, w_in, w_down, segs, trees, table
    )
    rq, rk, rv, ro, ri, rd = (a.reshape(*a.shape[:-4], -1, a.shape[-1]) for a in (rq, rk, rv, ro, ri, rd))
    outputs, input_grad, first_grad, rq, rk, rv, ro, ri, rd, sums = finish_call(outputs, input_grad, first_grad, rq, rk, rv, ro, ri, rd, sums)
    return outputs, input_grad, first_grad, sums[0], sums[1], rq, rk, rv, ro, sums[2], sums[3], ri, rd


def several_kernels(reach, inputs, first_values, cotangent, segs, trees, table, gain1, shift1, gain2, shift2, w_query, w_key, w_value, w_out, w_in, w_down):
    row_count, width = inputs.shape
    fsdp = lax.axis_size("fsdp")
    lnp, w1, w2, wo, win, wdn = gathered(fsdp, gain1, shift1, gain2, shift2, w_query, w_key, w_value, w_out, w_in, w_down)
    x = jnp.concatenate([shifted(inputs, "fsdp", d) for d in range(reach, 0, -1)] + [inputs], axis=0)
    fv = jnp.concatenate([shifted(first_values, "fsdp", d) for d in range(reach, 0, -1)] + [first_values], axis=0)
    n1, q, k, v, mixed, lse, resid, n2 = forward_call(fsdp, reach, x, fv, lnp, w1, w2, wo, segs, trees, table)
    outputs, gin, gdn, go, gres, gmixed, sums = mlp_call(n2, cotangent, resid, mixed, lnp, win, wdn, wo)
    dq, dk, dv, wk, wv = backward_call(fsdp, reach, q, k, v, gmixed, mixed, lse, segs, trees, table)
    for d in range(1, reach + 1):
        early = slice((reach - d) * row_count, (reach - d + 1) * row_count)
        both = shifted(jnp.concatenate([wk[early], wv[early]], axis=1), "fsdp", -d).astype(jnp.float32)
        dk, dv = dk + both[:, :width], dv + both[:, width:]
    input_grad, first_grad, g1, g2, sums = projection_back_call(fsdp, reach, x, n1, dq, dk, dv, lnp, w1, w2, gres, sums)
    return outputs, input_grad, first_grad, *reduced(fsdp, sums, g1, g2, go, gin, gdn)


def on_device(
    inputs,
    first_values,
    cotangent,
    tree_ids,
    segment_ids,
    path_table,
    attn_gain,
    attn_shift,
    w_query,
    w_key,
    w_value,
    w_out,
    mlp_gain,
    mlp_shift,
    w_in,
    w_down,
):
    row_count, width = inputs.shape
    fsdp = lax.axis_size("fsdp")
    reach = 0
    for device_pos in range(fsdp):
        offset = device_pos * row_count % TREE_LEN
        reach = max(reach, (offset + row_count - 1) // row_count)
    marks = (segment_ids.reshape(-1, BLOCK), tree_ids, path_table)
    weights = (attn_gain, attn_shift, mlp_gain, mlp_shift, w_query, w_key, w_value, w_out, w_in, w_down)
    if lax.axis_size("rep") == 8 and reach == 1 and row_count == width:
        return one_kernel(inputs, first_values, cotangent, *marks, *weights)
    results = several_kernels(reach, inputs, first_values, cotangent, *marks, *weights)
    outputs, input_grad, first_grad, sums, d_q, d_k, d_v, d_o, d_in, d_dn = results
    rows = w_query.shape[0]
    sums = lax.dynamic_slice_in_dim(sums, lax.axis_index("fsdp") * rows, rows, 1)
    d_in = d_in.reshape(-1, rows, fsdp, BLOCK).transpose(1, 2, 0, 3).reshape(rows, -1)
    d_q, d_k, d_v, d_o, d_in, d_dn = (a.astype(jnp.float32) for a in (d_q, d_k, d_v, d_o, d_in, d_dn.reshape(-1, width)))
    return (outputs, input_grad, first_grad, sums[0], sums[1], d_q, d_k, d_v, d_o, sums[2], sums[3], d_in, d_dn)


def solution(mesh):
    placed = (
        P(("rep", "fsdp"), None),
        P(("rep", "fsdp"), None),
        P(("rep", "fsdp"), None),
        P("rep"),
        P("rep"),
        P("rep", None, None),
        P("fsdp"),
        P("fsdp"),
        P("fsdp", None),
        P("fsdp", None),
        P("fsdp", None),
        P("fsdp", None),
        P("fsdp"),
        P("fsdp"),
        P("fsdp", None),
        P("fsdp", None),
    )
    return jax.shard_map(
        on_device,
        mesh=mesh,
        in_specs=placed,
        out_specs=(
            P(("rep", "fsdp"), None),
            P(("rep", "fsdp"), None),
            P(("rep", "fsdp"), None),
            P("fsdp"),
            P("fsdp"),
            P("fsdp", None),
            P("fsdp", None),
            P("fsdp", None),
            P("fsdp", None),
            P("fsdp"),
            P("fsdp"),
            P("fsdp", None),
            P("fsdp", None),
        ),
        check_vma=False,
    )
```

```python
import functools

import jax
import jax.numpy as jnp
from jax import lax
from jax.experimental import pallas as pl
from jax.experimental.pallas import tpu as pltpu
from jax.sharding import PartitionSpec as P

MESH = pl.DeviceIdType.MESH

class Place:
    def __init__(self, fsdp):
        self.fsdp = fsdp
        r = lax.axis_index("rep")
        self.f = lax.axis_index("fsdp")
        self.k = lax.rem(r, 2)
        self.x = lax.rem(r // 2, 2)
        self.y = r // 4
        def rid(y, x, k): return (y * 2 + x) * 2 + k
        self.core = (rid(self.y, self.x, 1 - self.k), self.f)
        self.xn = (rid(self.y, 1 - self.x, self.k), self.f)
        self.yn = (rid(1 - self.y, self.x, self.k), self.f)
        self.r = r
        self.diagonal = (rid(1 - self.y, 1 - self.x, self.k), self.f)
        self.others = [lax.rem(self.f + j, fsdp) for j in range(1, fsdp)]
    def zdev(self, fo): return (self.r, fo)
    def barrier(self):
        bar = pltpu.get_barrier_semaphore()
        devs = [self.core, self.xn, self.yn, self.diagonal] + [self.zdev(o) for o in self.others]
        for d in devs:
            pl.semaphore_signal(bar, inc=1, device_id=d, device_id_type=MESH)
        pl.semaphore_wait(bar, len(devs))

def drain(view, sem):
    pltpu.make_async_copy(view, view, sem).wait()

class Gather:
    def __init__(self, pc, buf, send, recv, xfirst, direct=False):
        self.pc, self.buf, self.s, self.r, self.xf, self.direct = pc, buf, send, recv, xfirst, direct
        self.H = buf.shape[-1] // 2
        self.cols = pl.ds(pl.multiple_of(pc.k * self.H, 128), self.H)
    def push(self, view, stage, dev):
        pltpu.make_async_remote_copy(src_ref=view, dst_ref=view, send_sem=self.s.at[stage], recv_sem=self.r.at[stage], device_id=dev, device_id_type=MESH).start()
    def z_start(self):
        pc = self.pc
        v = self.buf.at[pc.f, pc.y, pc.x, :, self.cols]
        for o in pc.others: self.push(v, 0, pc.zdev(o))
    def three(self): return self.buf.at[pl.ds(0, self.pc.fsdp - 1), 0, 0, :, self.cols]
    def z_wait(self): drain(self.three(), self.r.at[0])
    def a_start(self):
        pc = self.pc
        for o in pc.others:
            v = self.buf.at[o, pc.y, pc.x, :, self.cols]
            self.push(v, 1, pc.xn); self.push(v, 2, pc.yn)
            if self.direct: self.push(v, 3, pc.diagonal)
    def a_wait(self):
        drain(self.three(), self.r.at[1]); drain(self.three(), self.r.at[2])
    def b_start(self):
        pc = self.pc
        if self.direct: return
        for o in pc.others:
            if self.xf: self.push(self.buf.at[o, 1 - pc.y, pc.x, :, self.cols], 3, pc.xn)
            else: self.push(self.buf.at[o, pc.y, 1 - pc.x, :, self.cols], 3, pc.yn)
    def b_wait(self): drain(self.three(), self.r.at[3])
    def c_start(self):
        pc = self.pc
        for o in pc.others: self.push(self.buf.at[o, :, :, :, self.cols], 4, pc.core)
    def big(self): return self.buf.at[pl.ds(0, self.pc.fsdp - 1), :, :, :, self.cols]
    def c_wait(self): drain(self.big(), self.r.at[4])
    def finish(self, first=0):
        for st in range(first, 4): drain(self.three(), self.s.at[st])
        drain(self.big(), self.s.at[4])

Gather.STAGES = [
    lambda g: (g.z_wait(), g.a_start()),
    lambda g: (g.a_wait(), g.b_start()),
    lambda g: (g.b_wait(), g.c_start()),
    lambda g: (g.c_wait(), g.finish()),
]


class Reduce:
    def __init__(self, pc, buf, r1, r2, r3, r4, res, send, recv, xfirst):
        self.pc, self.buf, self.r1, self.r2, self.r3, self.r4, self.res = pc, buf, r1, r2, r3, r4, res
        self.s, self.r, self.xf = send, recv, xfirst
        self.H = H = buf.shape[-1] // 2
        self.cols = pl.ds(pl.multiple_of(pc.k * H, 128), H)
        self.ocols = pl.ds(pl.multiple_of((1 - pc.k) * H, 128), H)
        self.F = buf.shape[0]
    def send(self, src, dst, stage, dev):
        pltpu.make_async_remote_copy(src_ref=src, dst_ref=dst, send_sem=self.s.at[stage], recv_sem=self.r.at[stage], device_id=dev, device_id_type=MESH).start()
    def p1(self):
        self.send(self.buf.at[:, :, :, :, self.ocols], self.r1, 0, self.pc.core)
    def p2(self):
        pc = self.pc
        drain(self.r1, self.r.at[0])
        @pl.loop(0, self.F * 4)
        def _(i):
            a, b, c = i // 4, lax.rem(i // 2, 2), lax.rem(i, 2)
            self.r1[a, b, c] = self.r1[a, b, c] + self.buf[a, b, c, :, self.cols]
        if self.xf: self.send(self.r1.at[:, :, 1 - pc.x], self.r2, 1, pc.xn)
        else: self.send(self.r1.at[:, 1 - pc.y], self.r2, 1, pc.yn)
    def p3(self):
        pc = self.pc
        drain(self.r2, self.r.at[1])
        @pl.loop(0, self.F * 2)
        def _(i):
            a, b = i // 2, lax.rem(i, 2)
            mine = self.r1[a, b, pc.x] if self.xf else self.r1[a, pc.y, b]
            self.r2[a, b] = self.r2[a, b] + mine
        if self.xf: self.send(self.r2.at[:, 1 - pc.y], self.r3, 2, pc.yn)
        else: self.send(self.r2.at[:, 1 - pc.x], self.r3, 2, pc.xn)
    def p4(self):
        pc = self.pc
        drain(self.r3, self.r.at[2])
        q = pc.y if self.xf else pc.x
        @pl.loop(0, self.F)
        def _(a):
            self.r3[a] = self.r3[a] + self.r2[a, q]
        for o in pc.others: self.send(self.r3.at[o], self.r4.at[pc.f], 3, pc.zdev(o))
    def p5(self):
        pc = self.pc
        drain(self.r4.at[pl.ds(0, self.F - 1)], self.r.at[3])
        tot = self.r3[pc.f].astype(jnp.float32)
        for o in pc.others: tot = tot + self.r4[o].astype(jnp.float32)
        self.res[pc.y, pc.x, :, self.cols] = tot.astype(jnp.bfloat16)
        v = self.res.at[pc.y, pc.x, :, self.cols]
        self.send(v, v, 4, pc.xn); self.send(v, v, 5, pc.yn)
    def p6(self):
        pc = self.pc
        v = self.res.at[0, 0, :, self.cols]
        drain(v, self.r.at[4]); drain(v, self.r.at[5])
        if self.xf:
            v = self.res.at[1 - pc.y, pc.x, :, self.cols]; self.send(v, v, 6, pc.xn)
        else:
            v = self.res.at[pc.y, 1 - pc.x, :, self.cols]; self.send(v, v, 6, pc.yn)
    def p7(self):
        drain(self.res.at[0, 0, :, self.cols], self.r.at[6])
        v = self.res.at[:, :, :, self.cols]
        self.send(v, v, 7, self.pc.core)
    def p8(self):
        drain(self.res.at[:, :, :, self.cols], self.r.at[7])
    def finish(self):
        drain(self.r1, self.s.at[0]); drain(self.r2, self.s.at[1]); drain(self.r3, self.s.at[2])
        drain(self.r4.at[pl.ds(0, self.F - 1)], self.s.at[3])
        v = self.res.at[0, 0, :, self.cols]
        for i in (4, 5, 6): drain(v, self.s.at[i])
        drain(self.res.at[:, :, :, self.cols], self.s.at[7])

Reduce.STAGES = [Reduce.p1, Reduce.p2, Reduce.p3, Reduce.p4, Reduce.p5, Reduce.p6, Reduce.p7, Reduce.p8]

def red_shapes(shape):
    f, _, _, m, c = shape
    return (f, 2, 2, m, c // 2), (f, 2, m, c // 2), (f, m, c // 2), (f, m, c // 2)


HEAD = 64
BLOCK = 128
TRUNK = 512
TREE_LEN = 1024


epsilon = 1e-05
far_below = -1e30


def nt(a, b):
    return lax.dot_general(a, b, (((1,), (1,)), ((), ())), preferred_element_type=jnp.float32)


def tn(a, b):
    return lax.dot_general(a, b, (((0,), (0,)), ((), ())), preferred_element_type=jnp.float32)


def mm(a, b):
    return jnp.dot(a, b, preferred_element_type=jnp.float32)


def bf(a):
    return a.astype(jnp.bfloat16)


def f32(a):
    return a.astype(jnp.float32)


def row_tiles(rows):
    return 256 if rows % 256 == 0 else 128


def normalized(v):
    center = v - jnp.mean(v, axis=1, keepdims=True)
    inv = lax.rsqrt(jnp.mean(center * center, axis=1, keepdims=True) + epsilon)
    return center * inv, inv


class Span:
    def __init__(self, fsdp, rows, reach, f):
        self.rows, self.reach, self.f = rows, reach, f
        self.window = reach * rows
        self.blocks = rows // BLOCK
        self.first = f * self.blocks
        tree = TREE_LEN // BLOCK
        self.tree = tree
        self.start = (self.first // tree) * TREE_LEN - f * rows + self.window

    def kind(self, i):
        return lax.rem(self.first + i, self.tree)

    def base(self, i):
        return pl.multiple_of(((self.first + i) // self.tree) * TREE_LEN - self.f * self.rows + self.window, BLOCK)


def rows_at(start, size):
    return pl.ds(pl.multiple_of(start, BLOCK), size)


def make_bias(span, segs, trees, table, bias, extra=0):
    @pl.loop(0, span.blocks + extra)
    def _(i):
        b = span.kind(i)
        first = ((span.first + i) // span.tree) * span.tree
        q_pos = b * BLOCK + lax.broadcasted_iota(jnp.int32, (1, BLOCK), 1)
        own = segs[pl.ds(span.first + i, 1), :]

        def put(slot, key, related):
            k_pos = key * BLOCK + lax.broadcasted_iota(jnp.int32, (BLOCK, 1), 0)
            column = jnp.broadcast_to(f32(segs[pl.ds(first + key, 1), :]), (BLOCK, BLOCK)).T
            seen = (k_pos <= q_pos) & (column == f32(related))
            bias[i, pl.ds(slot, BLOCK), :] = jnp.where(seen, 0.0, far_below)

        put(256, b, own)

        @pl.when(b >= 6)
        def _():
            tree = trees[first * BLOCK]
            parent = jnp.zeros_like(own)
            rows = table[tree]
            for leaf in range(table.shape[1]):
                parent = jnp.where(own == leaf, rows[leaf:leaf + 1, 1:2], parent)
            put(0, 4, parent)
            put(BLOCK, 5, parent)


def by_kind(b, body, lent=None):
    for n in range(TRUNK // BLOCK):

        @pl.when(b == n)
        def _():
            body([(0, n * BLOCK, None)][: n] + [(None, BLOCK, 256)])

    branch_parts = [(0, 512, None), (None, BLOCK, 256)]
    leaf_parts = [(0, 512, None), (512, 256, 0), (None, BLOCK, 256)]
    if lent is None:

        @pl.when((b >= 4) & (b < 6))
        def _():
            body(branch_parts)

        @pl.when(b >= 6)
        def _():
            body(leaf_parts)

    else:
        for upto in (0, 512, 768):

            if upto < 768:

                @pl.when((b >= 4) & (b < 6) & (lent == upto))
                def _():
                    body(branch_parts, upto)

            @pl.when((b >= 6) & (lent == upto))
            def _():
                body(leaf_parts, upto)


def stacked(pair):
    low = lax.broadcasted_iota(jnp.int32, (1, 2 * HEAD), 1) < HEAD
    zero = jnp.zeros_like(pair)
    return jnp.concatenate([jnp.where(low, pair, zero), jnp.where(low, zero, pair)], axis=0)


def unstacked_t(wide):
    both = jnp.concatenate([wide[:HEAD, :BLOCK], wide[HEAD:, BLOCK:]], axis=0)
    return both.T


def part_rows(span, i, b, part):
    key, count, slot = part
    return rows_at(span.base(i) + (b * BLOCK if key is None else key), count)


def part_scores(q2, k, bias, i, part):
    s = nt(k, q2)
    slot = part[2]
    if slot is not None:
        one = bias[i, pl.ds(slot, part[1]), :]
        s = s + jnp.concatenate([one, one], axis=1)
    return s


def pair_cols(p):
    return pl.ds(pl.multiple_of(p * 2 * HEAD, 2 * HEAD), 2 * HEAD)


def transpose_pair(src, p, start, stop, dst):
    step = row_tiles(src.shape[0])

    @pl.loop(start // step, stop // step)
    def _(j):
        dst[:, pl.ds(pl.multiple_of(j * step, step), step)] = src[rows_at(j * step, step), pair_cols(p)].T


def group_cols(p, j, n):
    return pl.ds(pl.multiple_of((p * n + j) * 2 * HEAD, 2 * HEAD), 2 * HEAD)


GROUP = 2


def attend_group(span, p, lo, hi, q, k, v, bias, mixed, lse):
    @pl.loop(lo, hi)
    def _(i):
        b = span.kind(i)
        own = rows_at(i * BLOCK, BLOCK)

        def body(parts):
            rows = [part_rows(span, i, b, part) for part in parts]
            state = []
            for j in range(GROUP):
                cols = group_cols(p, j, GROUP)
                q2 = stacked(q[own, cols])
                state.append((j, cols, [part_scores(q2, k[r, cols], bias, i, part) for r, part in zip(rows, parts)]))
            for j, cols, scores in state:
                top = functools.reduce(jnp.maximum, [jnp.max(s, axis=0, keepdims=True) for s in scores])
                expo = [jnp.exp(s - top) for s in scores]
                total = sum(jnp.sum(e, axis=0, keepdims=True) for e in expo)
                out = sum(tn(v[r, cols], bf(e)) for r, e in zip(rows, expo))
                mixed[own, cols] = bf(unstacked_t(out * (1.0 / total)))
                lse[p * GROUP + j, pl.ds(i, 1), :] = top + jnp.log(total)

        by_kind(b, body)


def norm_tile(x, gain, shift):
    hat, _ = normalized(f32(x))
    return bf(hat * gain + shift)


def project(span, x, fv, lnp, w1, w2, n1, q, k, v):
    gain, shift = lnp[0:1, :], lnp[1:2, :]
    tile = row_tiles(span.rows)
    third = w1.shape[1] // 4
    half = 2 * third
    scale = HEAD ** (-0.5)

    @pl.loop(span.window // tile, (span.window + span.rows) // tile)
    def _(t):
        rows = rows_at(t * tile, tile)
        n = norm_tile(x[rows, :], gain, shift)
        own = rows_at(t * tile - span.window, tile)
        n1[own, :] = n
        a = mm(n, w1[...])
        q[own, :half] = bf(f32(bf(a[:, :half])) * scale)
        k[rows, :half] = bf(a[:, half:])
        a = mm(n, w2[...])
        q[own, half:] = bf(f32(bf(a[:, :third])) * scale)
        k[rows, half:] = bf(a[:, half:half + third])
        v[rows, :third] = bf(a[:, third:half])
        v[rows, third:third + BLOCK] = bf(a[:, half + third:half + third + BLOCK])
        v[rows, third + BLOCK:] = fv[rows, :]

    @pl.loop(span.start // tile, span.window // tile)
    def _(t):
        rows = rows_at(t * tile, tile)
        n = norm_tile(x[rows, :], gain, shift)
        k[rows, :half] = bf(mm(n, w1[:, half:]))
        a = mm(n, w2[:, third:])
        v[rows, :third] = bf(a[:, :third])
        k[rows, half:] = bf(a[:, third:half])
        v[rows, third:third + BLOCK] = bf(a[:, half:half + BLOCK])
        v[rows, third + BLOCK:] = fv[rows, :]


def branch_out(span, x, lnp, mixed, wo, resid, n2):
    gain, shift = lnp[2:3, :], lnp[3:4, :]
    tile = row_tiles(span.rows)

    @pl.loop(0, span.rows // tile)
    def _(t):
        rows = rows_at(t * tile, tile)
        r = f32(x[rows_at(span.window + t * tile, tile), :]) + mm(mixed[rows, :], wo[...])
        resid[rows, :] = r
        hat, _ = normalized(r)
        n2[rows, :] = bf(hat * gain + shift)


def forward_kernel(fsdp, reach, x, fv, lnp, w1, w2, wo, segs, trees, table, n1, q, k, v, mixed, lse, resid, n2, bias):
    span = Span(fsdp, q.shape[0], reach, lax.axis_index("fsdp"))
    rows = q.shape[0]
    make_bias(span, segs, trees, table, bias)
    project(span, x, fv, lnp, w1, w2, n1, q, k, v)

    @pl.loop(0, q.shape[1] // (2 * HEAD) // GROUP)
    def _(p):
        attend_group(span, p, 0, span.blocks, q, k, v, bias, mixed, lse)

    branch_out(span, x, lnp, mixed, wo, resid, n2)


VM = pl.BlockSpec(memory_space=pltpu.VMEM)
SM = pl.BlockSpec(memory_space=pltpu.SMEM)


def forward_call(fsdp, reach, x, fv, lnp, w1, w2, wo, segs, trees, table):
    window, width = x.shape
    rows = window // (reach + 1)
    s = jax.ShapeDtypeStruct
    low, full = jnp.bfloat16, jnp.float32
    pairs, blocks = width // (2 * HEAD), rows // BLOCK
    outs = (
        s((rows, width), low), s((rows, width), low), s((window, width), low), s((window, width), low), s((rows, width), low),
        s((pairs, -(-blocks // 8) * 8, 2 * BLOCK), full), s((rows, width), full), s((rows, width), low),
    )
    return pl.pallas_call(
        functools.partial(forward_kernel, fsdp, reach),
        out_shape=outs, in_specs=[VM] * 7 + [SM, VM], out_specs=[VM] * 8,
        scratch_shapes=[pltpu.VMEM((blocks, 3 * BLOCK, BLOCK), full)],
        compiler_params=pltpu.CompilerParams(vmem_limit_bytes=50 << 20),
    )(x, fv, lnp, w1, w2, wo, segs, trees, table)


GELU_A = 0.7978845608028654
GELU_B = 0.044715


def gelu_both(u):
    sq = u * u
    t = jnp.tanh(GELU_A * u * (1.0 + GELU_B * sq))
    half = 0.5 * (1.0 + t)
    slope = half + 0.5 * u * (1.0 - t * t) * (GELU_A * (1.0 + 3.0 * GELU_B * sq))
    return u * half, slope


def transpose_all(src, dst):
    cols = src.shape[1] // BLOCK

    @pl.loop(0, src.shape[0] // BLOCK)
    def _(j):
        rows = rows_at(j * BLOCK, BLOCK)
        for c in range(cols):
            dst[c * BLOCK:(c + 1) * BLOCK, rows] = src[rows, c * BLOCK:(c + 1) * BLOCK].T


def mlp_chunk(rows, n2, n2_t, cot, win, wdn, out_acc, gn2_acc, hid, gact, gin, gdn, between=lambda: None):
    tile = 384 if rows % 384 == 0 else row_tiles(rows)

    @pl.loop(0, rows // tile)
    def _(t):
        r = rows_at(t * tile, tile)
        h, slope = gelu_both(mm(n2[r, :], win()))
        h = bf(h)
        hid[r, :] = h
        out_acc[r, :] += mm(h, wdn())
        g = bf(nt(cot[r, :], wdn()) * slope)
        gact[r, :] = g
        gn2_acc[r, :] += nt(g, win())

    between()
    gdn(bf(tn(hid[...], cot[...])))
    gin(bf(mm(n2_t[...], gact[...])))


def norm_back(hat, inv, grad, gain):
    e = grad * gain
    return inv * (e - jnp.mean(e, axis=1, keepdims=True) - hat * jnp.mean(e * hat, axis=1, keepdims=True))


def second_norm_back(rows, lnp, resid, cot, gn2, gres, gbranch, sums):
    tile = row_tiles(rows)
    sums[...] = jnp.zeros_like(sums)

    @pl.loop(0, rows // tile)
    def _(t):
        r = rows_at(t * tile, tile)
        hat, inv = normalized(resid[r, :])
        g = gn2[r, :]
        gr = f32(cot[r, :]) + norm_back(hat, inv, g, lnp[2:3, :])
        gres[r, :] = gr
        gbranch[r, :] = bf(gr)
        sums[2:3, :] += jnp.sum(g * hat, axis=0, keepdims=True)
        sums[3:4, :] += jnp.sum(g, axis=0, keepdims=True)


def branch_back(rows, gbranch, wo, gmixed):
    tile = row_tiles(rows)

    @pl.loop(0, rows // tile)
    def _(t):
        r = rows_at(t * tile, tile)
        gmixed[r, :] = bf(nt(gbranch[r, :], wo[...]))


def mlp_kernel(n2, cot, resid, mixed, lnp, win, wdn, wo, outputs, gin, gdn, go, gres, gmixed, sums, n2_t, out_acc, gn2_acc, hid, gact, gbranch):
    rows = n2.shape[0]
    transpose_all(n2, n2_t)
    out_acc[...] = resid[...]
    gn2_acc[...] = jnp.zeros_like(gn2_acc)

    @pl.loop(0, win.shape[0])
    def _(c):
        def put_in(v):
            gin[c] = v

        def put_dn(v):
            gdn[c] = v

        mlp_chunk(rows, n2, n2_t, cot, lambda: win[c], lambda: wdn[c], out_acc, gn2_acc, hid, gact, put_in, put_dn)

    outputs[...] = bf(out_acc[...])
    second_norm_back(rows, lnp, resid, cot, gn2_acc, gres, gbranch, sums)
    branch_back(rows, gbranch, wo, gmixed)
    go[...] = bf(tn(mixed[...], gbranch[...]))


def mlp_call(n2, cot, resid, mixed, lnp, win, wdn, wo):
    rows, width = n2.shape
    n_ff, _, cols = win.shape
    s, low, full = jax.ShapeDtypeStruct, jnp.bfloat16, jnp.float32
    outs = (
        s((rows, width), low), s(win.shape, low), s(wdn.shape, low), s((width, width), low), s((rows, width), full),
        s((rows, width), low), s((8, width), full),
    )
    return pl.pallas_call(
        mlp_kernel, out_shape=outs, in_specs=[VM] * 8, out_specs=[VM] * 7,
        scratch_shapes=[
            pltpu.VMEM((width, rows), low), pltpu.VMEM((rows, width), full), pltpu.VMEM((rows, width), full),
            pltpu.VMEM((rows, cols), low), pltpu.VMEM((rows, cols), low), pltpu.VMEM((rows, width), low),
        ],
        compiler_params=pltpu.CompilerParams(vmem_limit_bytes=58 << 20),
    )(n2, cot, resid, mixed, lnp, win, wdn, wo)


def attend_back_group(span, p, lo, hi, q, k, v, gmixed, bias, lse, inner, dk_acc, dv_acc, dq, lent=None):
    @pl.loop(lo, hi)
    def _(i):
        b = span.kind(i)
        own = rows_at(i * BLOCK, BLOCK)

        def body(parts, upto=0):
            rows = [part_rows(span, i, b, part) for part in parts]
            state = []
            for j in range(GROUP):
                cols = group_cols(p, j, GROUP)
                q2, g2 = stacked(q[own, cols]), stacked(gmixed[own, cols])
                state.append((j, cols, q2, g2, [part_scores(q2, k[r, cols], bias, i, part) for r, part in zip(rows, parts)]))
            for j, cols, q2, g2, scores in state:
                l, mean = lse[p * GROUP + j, pl.ds(i, 1), :], inner[p * GROUP + j, pl.ds(i, 1), :]
                probs = [jnp.exp(s - l) for s in scores]
                gs = [bf(a * (nt(v[r, cols], g2) - mean)) for a, r in zip(probs, rows)]
                out = sum(tn(k[r, cols], g) for r, g in zip(rows, gs))
                dq[own, cols] = bf(unstacked_t(out) * HEAD ** (-0.5))
                at = slice(j * 2 * HEAD, (j + 1) * 2 * HEAD)
                for r, a, g, part in zip(rows, probs, gs, parts):
                    if part[0] is not None and part[0] < upto:
                        continue
                    dk_acc[r, at] += mm(g, q2)
                    dv_acc[r, at] += mm(bf(a), g2)

        by_kind(b, body, None if lent is None else jnp.where(i < span.tree - span.kind(0), lent, 0))


def clear_rows(span, *refs):
    @pl.loop(span.start // BLOCK, (span.window + span.rows) // BLOCK)
    def _(j):
        r = rows_at(j * BLOCK, BLOCK)
        for ref in refs:
            ref[r, :] = jnp.zeros((BLOCK, ref.shape[1]), jnp.float32)


def head_sums(gmixed, mixed, inner):
    width = mixed.shape[1]
    heads = lax.broadcasted_iota(jnp.int32, (16, width), 0)
    cols = lax.broadcasted_iota(jnp.int32, (16, width), 1)
    pick = bf(((cols >= heads * HEAD) & (cols < heads * HEAD + HEAD)).astype(jnp.float32))
    tile = row_tiles(mixed.shape[0])
    for t in range(mixed.shape[0] // tile):
        r = slice(t * tile, (t + 1) * tile)
        each = f32(gmixed[r, :]) * f32(mixed[r, :])
        high = bf(each)
        sums = nt(pick, high) + nt(pick, bf(each - f32(high)))
        for j in range(tile // BLOCK):
            at, i = slice(j * BLOCK, (j + 1) * BLOCK), t * (tile // BLOCK) + j
            for p in range(width // (2 * HEAD)):
                inner[p, i:i + 1, :] = jnp.concatenate([sums[2 * p:2 * p + 1, at], sums[2 * p + 1:2 * p + 2, at]], axis=1)


def borrowed_back(span, p, cols, j, parts, q, g, k, v, bias, lse, inner, dk, dv):
    join = lambda of: jnp.concatenate([of(0), of(1)], axis=0)
    q2 = join(lambda n: stacked(q[rows_at((j + n) * BLOCK, BLOCK), cols]))
    g2 = join(lambda n: stacked(g[rows_at((j + n) * BLOCK, BLOCK), cols]))
    row = lambda ref: jnp.concatenate([ref[p, pl.ds(j, 1), :], ref[p, pl.ds(j + 1, 1), :]], axis=1)
    l, mean = row(lse), row(inner)
    base = span.base(span.blocks - 1)
    for key, count, slot in parts:
        rows, own = rows_at(base + key, count), rows_at(base - span.window + key, count)
        s = nt(k[rows, cols], q2)
        if slot is not None:
            both = [bias[span.blocks + n, pl.ds(slot, count), :] for n in range(2)]
            s = s + jnp.concatenate([both[0], both[0], both[1], both[1]], axis=1)
        probs = jnp.exp(s - l)
        gs = bf(probs * (nt(v[rows, cols], g2) - mean))
        dk[own, cols] += mm(gs, q2)
        dv[own, cols] += mm(bf(probs), g2)


def backward_kernel(fsdp, reach, q, k, v, gmixed, mixed, lse, segs, trees, table, dq, dk, dv, wk, wv, bias, inner, dk_acc, dv_acc):
    span = Span(fsdp, q.shape[0], reach, lax.axis_index("fsdp"))
    make_bias(span, segs, trees, table, bias)
    head_sums(gmixed, mixed, inner)
    wk[...] = jnp.zeros_like(wk)
    wv[...] = jnp.zeros_like(wv)

    size = GROUP * 2 * HEAD

    @pl.loop(0, q.shape[1] // size)
    def _(p):
        cols = pl.ds(pl.multiple_of(p * size, size), size)
        clear_rows(span, dk_acc, dv_acc)
        attend_back_group(span, p, 0, span.blocks, q, k, v, gmixed, bias, lse, inner, dk_acc, dv_acc, dq)
        dk[:, cols] = dk_acc[span.window:, :]
        dv[:, cols] = dv_acc[span.window:, :]

        @pl.loop(span.start // BLOCK, span.window // BLOCK)
        def _(j):
            r = rows_at(j * BLOCK, BLOCK)
            wk[r, cols] = bf(dk_acc[r, :])
            wv[r, cols] = bf(dv_acc[r, :])


def backward_call(fsdp, reach, q, k, v, gmixed, mixed, lse, segs, trees, table):
    window, width = k.shape
    rows = q.shape[0]
    s, low, full = jax.ShapeDtypeStruct, jnp.bfloat16, jnp.float32
    early = window - rows
    outs = (s((rows, width), low), s((rows, width), full), s((rows, width), full), s((early, width), low), s((early, width), low))
    return pl.pallas_call(
        functools.partial(backward_kernel, fsdp, reach), out_shape=outs, in_specs=[VM] * 7 + [SM, VM], out_specs=[VM] * 5,
        scratch_shapes=[
            pltpu.VMEM((rows // BLOCK, 3 * BLOCK, BLOCK), full), pltpu.VMEM(lse.shape, full),
            pltpu.VMEM((window, GROUP * 2 * HEAD), full), pltpu.VMEM((window, GROUP * 2 * HEAD), full),
        ],
        compiler_params=pltpu.CompilerParams(vmem_limit_bytes=58 << 20),
    )(q, k, v, gmixed, mixed, lse, segs, trees, table)


def projection_back(span, x, n1, dq, dk, dv, lnp, w1, w2, gres, gin, gfirst, g1, g2, sums, n1_t, cat1, cat2):
    rows = span.rows
    third = w1.shape[1] // 4
    half = 2 * third
    fresh = third + BLOCK
    tile = row_tiles(rows)
    transpose_all(n1, n1_t)

    @pl.loop(0, rows // tile)
    def _(t):
        r = rows_at(t * tile, tile)
        cat1[r, :half] = dq[r, :half]
        cat1[r, half:] = bf(dk[r, :half])
        cat2[r, :third] = dq[r, half:]
        cat2[r, third:half] = bf(dv[r, :third])
        cat2[r, half:half + third] = bf(dk[r, half:])
        cat2[r, half + third:half + third + BLOCK] = bf(dv[r, third:fresh])
        cat2[r, half + third + BLOCK:] = jnp.zeros((tile, BLOCK), jnp.bfloat16)
        gfirst[r, :] = dv[r, fresh:]

    g1[...] = bf(mm(n1_t[...], cat1[...]))
    g2[...] = bf(mm(n1_t[...], cat2[...]))

    @pl.loop(0, rows // tile)
    def _(t):
        r = rows_at(t * tile, tile)
        g = nt(cat1[r, :], w1[...]) + nt(cat2[r, :], w2[...])
        hat, inv = normalized(f32(x[rows_at(span.window + t * tile, tile), :]))
        gin[r, :] = gres[r, :] + norm_back(hat, inv, g, lnp[0:1, :])
        sums[0:1, :] += jnp.sum(g * hat, axis=0, keepdims=True)
        sums[1:2, :] += jnp.sum(g, axis=0, keepdims=True)


def projection_back_kernel(fsdp, reach, x, n1, dq, dk, dv, lnp, w1, w2, gres, sums_in, gin, gfirst, g1, g2, sums, n1_t, cat1, cat2):
    span = Span(fsdp, dq.shape[0], reach, lax.axis_index("fsdp"))
    sums[...] = sums_in[...]
    projection_back(span, x, n1, dq, dk, dv, lnp, w1, w2, gres, gin, gfirst, g1, g2, sums, n1_t, cat1, cat2)


def projection_back_call(fsdp, reach, x, n1, dq, dk, dv, lnp, w1, w2, gres, sums):
    rows, width = dq.shape
    s, low, full = jax.ShapeDtypeStruct, jnp.bfloat16, jnp.float32
    outs = (s((rows, width), full), s((rows, width // 2), full), s(w1.shape, low), s(w2.shape, low), s((8, width), full))
    return pl.pallas_call(
        functools.partial(projection_back_kernel, fsdp, reach), out_shape=outs, in_specs=[VM] * 10, out_specs=[VM] * 5,
        scratch_shapes=[pltpu.VMEM((width, rows), low), pltpu.VMEM((rows, w1.shape[1]), low), pltpu.VMEM((rows, w1.shape[1]), low)],
        compiler_params=pltpu.CompilerParams(vmem_limit_bytes=58 << 20),
    )(x, n1, dq, dk, dv, lnp, w1, w2, gres, sums)


def gather_steps(items, u):
    for s, stage in enumerate(Gather.STAGES[:3]):
        c = u - s

        @pl.when((c >= 0) & (c < items.count))
        def _():
            for g in items(c):
                stage(g)


REDUCE_AT = (0, 1, 3, 5, 7, 8, 9)


def reduce_steps(items, u):
    for s, stage in enumerate(Reduce.STAGES[:7]):
        c = u - REDUCE_AT[s]

        @pl.when((c >= 0) & (c < items.count))
        def _():
            for g in items(c):
                stage(g)


class Chunks:
    def __init__(self, count, make):
        self.count, self.make = count, make

    def __call__(self, c):
        return self.make(c)


N_IN = 13


class Scratch:
    def __init__(self):
        self.names, self.shapes = [], []

    def add(self, name, shape):
        self.names.append(name)
        self.shapes.append(shape)

    def bind(self, refs):
        for name, ref in zip(self.names, refs):
            setattr(self, name, ref)
        return self


def layer_kernel(fsdp, n_ff, scratch, n_out, *refs):
    (inputs, first, cot_in, a_q, a_k, a_v, a_o, a_in, a_dn, norms, segs, trees, table) = refs[:N_IN]
    (outputs, gin, gfirst, rs_q, rs_k, rs_v, rs_o, rs_in, rs_dn, rs_vec) = refs[N_IN : N_IN + n_out]
    m = scratch.bind(refs[N_IN + n_out :])
    pc = Place(fsdp)
    f = pc.f
    rows, width = cot_in.shape
    span = Span(fsdp, rows, 1, f)
    tile = row_tiles(rows)
    tiles = rows // tile
    last = fsdp - 1
    flat = lambda ref: ref.reshape(-1, ref.shape[-1])
    w_q, w_k, w_v, w_o = (flat(b) for b in (m.b_q, m.b_k, m.b_v, m.b_o))
    mixed, cot = m.mixed.reshape(rows, width), m.cot.reshape(rows, width)
    x, q, k, v, n1, n2, tr = m.x, m.q, m.k, m.v, m.n1, m.n2, m.tr

    kind, next_kind = span.kind(0), lax.rem(span.first + span.blocks, span.tree)
    guest = kind >= 4
    host = (f < last) & (next_kind >= 4)
    lent_keys = jnp.where(kind == 6, 768, jnp.where(kind == 4, 512, 0))
    size = GROUP * 2 * HEAD

    def run_cols(p):
        return pl.ds(pl.multiple_of(p * size, size), size)

    def lend(i, src, dst):
        return pltpu.make_async_remote_copy(src_ref=src, dst_ref=dst, send_sem=m.b_send.at[i], recv_sem=m.b_recv.at[i], device_id=(pc.r, f - 1), device_id_type=MESH)

    most = 4 * BLOCK
    gq, gg = x.at[pl.ds(0, most)], x.at[pl.ds(most, most)]

    def sized(own, act):
        for start in (4, 6):
            ok = (f > 0) & (kind == start) if own else (f < last) & (next_kind == start)

            @pl.when(ok)
            def _():
                act((8 - start) * BLOCK)

    def lent_q(n):
        return lend(0, q.at[pl.ds(0, n)], gq.at[pl.ds(0, n)])

    def lent_rows():
        return [lend(1, m.lse, m.g_lse), lend(2, m.inner, m.g_inner)]

    def lent_run(p, n):
        return lend(3 + p, n2.at[pl.ds(0, n), run_cols(p)], gg.at[pl.ds(0, n), run_cols(p)])

    def local(src, dst, sem):
        c = pltpu.make_async_copy(src, dst, sem)
        c.start()
        return c

    half = width // 2
    lw = [
        local(a, b.at[f, :, :, :, pl.ds(0, a.shape[-1])], m.l_sem.at[1 + i])
        for i, (a, b) in enumerate(((a_q, m.b_q), (a_k, m.b_k), (a_v, m.b_v), (a_o, m.b_o)))
    ]
    lx = local(inputs, x.at[pl.ds(rows, rows)], m.l_sem.at[5])
    lf = local(first, v.at[pl.ds(rows, rows), pl.ds(width // 2, width // 2)], m.l_sem.at[6])
    lc = local(cot_in, cot, m.l_sem.at[7])
    group = a_in.shape[-1] // fsdp

    def own_chunk(c, act):
        for g in range(fsdp):
            cols = pl.ds(pl.multiple_of(g * group + c * BLOCK, BLOCK), BLOCK)
            act(pltpu.make_async_copy(a_in.at[:, :, :, cols], m.b_in.at[c, f, :, :, :, pl.ds(g * BLOCK, BLOCK)], m.lc_sem.at[c, g]))
        act(pltpu.make_async_copy(a_dn.at[c], m.b_dn.at[c, f], m.lc_sem.at[c, fsdp]))

    @pl.loop(0, n_ff)
    def _(c):
        own_chunk(c, lambda d: d.start())

    pad = m.b_v.shape[-1] - half
    m.b_v[f, :, :, :, half:] = jnp.zeros((2, 2, m.b_v.shape[3], pad), jnp.bfloat16)
    own_norms = jnp.concatenate([f32(norms[...]), jnp.zeros((4, norms.shape[1]), jnp.float32)], axis=0)
    own_norms = jnp.concatenate([own_norms, jnp.zeros((8, width - norms.shape[1]), jnp.float32)], axis=1)
    m.vec[f] = pltpu.roll(own_norms, f * norms.shape[1], 1)
    pc.barrier()
    for o in pc.others:
        pltpu.make_async_remote_copy(
            src_ref=m.vec.at[f], dst_ref=m.vec.at[f], send_sem=m.v_send.at[0], recv_sem=m.v_recv.at[0], device_id=pc.zdev(o), device_id_type=MESH
        ).start()
    gat = [Gather(pc, b, m.g_send.at[i], m.g_recv.at[i], xf, i < 3) for i, (b, xf) in enumerate(((m.b_q, True), (m.b_k, False), (m.b_v, True), (m.b_o, False)))]
    for l, g in zip(lw, gat):
        l.wait()
        g.z_start()

    next_start = Span(fsdp, rows, 1, f + 1).start

    def window(t):
        r, own = pl.ds(t * tile, tile), pl.ds(rows + t * tile, tile)
        nxt = (pc.r, f + 1)
        return [
            pltpu.make_async_remote_copy(src_ref=x.at[own], dst_ref=x.at[r], send_sem=m.w_send.at[0, t], recv_sem=m.w_recv.at[0, t], device_id=nxt, device_id_type=MESH),
            pltpu.make_async_remote_copy(
                src_ref=v.at[own, pl.ds(half, half)], dst_ref=v.at[r, pl.ds(half, half)], send_sem=m.w_send.at[1, t], recv_sem=m.w_recv.at[1, t], device_id=nxt, device_id_type=MESH
            ),
        ]

    ff = Chunks(
        n_ff,
        lambda c: [Gather(pc, m.b_in.at[c], m.gi_send.at[c], m.gi_recv.at[c], True), Gather(pc, m.b_dn.at[c], m.gd_send.at[c], m.gd_recv.at[c], False)],
    )

    make_bias(span, segs, trees, table, m.bias, jnp.where((f < last) & (next_kind == 6), 2, 0))
    for g in gat:
        drain(g.three(), g.s.at[0])
    lx.wait()
    lf.wait()
    for t in range(tiles):

        @pl.when((f < last) & (t * tile >= next_start))
        def _():
            for c in window(t):
                c.start()


    for g in gat[:3]:
        g.z_wait()
        g.a_start()
    v3 = m.vec.at[pl.ds(0, last)]
    drain(v3, m.v_recv.at[0])
    drain(v3, m.v_send.at[0])
    m.lnp[...] = functools.reduce(lambda a, b: a + b, [m.vec[j] for j in range(fsdp)])
    gain, shift = m.lnp[0:1, :], m.lnp[1:2, :]

    @pl.loop(0, tiles)
    def _(t):
        n1[rows_at(t * tile, tile), :] = norm_tile(x[rows_at(rows + t * tile, tile), :], gain, shift)

    for g in gat[:3]:
        g.a_wait()
        g.b_start()
    for g in gat[:3]:
        g.b_wait()
        g.c_start()
    for g in gat[:3]:
        g.c_wait()

    @pl.loop(0, tiles)
    def _(t):
        r, own = rows_at(rows + t * tile, tile), rows_at(t * tile, tile)
        n = n1[own, :]
        q[own, :] = bf(f32(bf(mm(n, w_q[...]))) * HEAD ** (-0.5))
        k[r, :] = bf(mm(n, w_k[...]))
        v[r, :half] = bf(mm(n, w_v[:, :half]))

    pairs = width // (2 * HEAD)
    here = lax.rem(span.tree - lax.rem(span.first, span.tree), span.tree)
    here = jnp.minimum(here, span.blocks)
    border = span.base(here)

    groups = pairs // GROUP

    @pl.loop(0, groups)
    def _(p):
        attend_group(span, p, here, span.blocks, q, k, v, m.bias, mixed, m.lse)

    for t in range(tiles):

        @pl.when((f < last) & (t * tile >= next_start))
        def _():
            for c in window(t):
                c.wait_send()

    @pl.loop(0, n_ff)
    def _(c):
        own_chunk(c, lambda d: d.wait())
        for g in ff(c):
            g.z_start()

    for stage in Gather.STAGES[:3]:
        stage(gat[3])

    for t in range(tiles):

        @pl.when(t * tile >= span.start)
        def _():
            r = pl.ds(t * tile, tile)
            drain(x.at[r], m.w_recv.at[0, t])
            drain(v.at[r, pl.ds(half, half)], m.w_recv.at[1, t])
            n = norm_tile(x[r, :], gain, shift)
            k[r, :] = bf(mm(n, w_k[...]))
            v[r, :half] = bf(mm(n, w_v[:, :half]))


    @pl.loop(0, 2 * groups)
    def _(s):
        p, part = s // 2, lax.rem(s, 2)
        middle = here // 2
        attend_group(span, p, part * middle, jnp.where(part == 0, middle, here), q, k, v, m.bias, mixed, m.lse)
        gather_steps(ff, s - 2 * groups + 2)

    gat[3].c_wait()
    branch_out(span, x, m.lnp, mixed, w_o, m.resid, n2)
    @pl.when(host)
    def _():
        pl.semaphore_signal(m.freed, inc=1, device_id=(pc.r, f + 1), device_id_type=MESH)

    gather_steps(ff, 2)
    for g in gat:
        g.finish(1)

    lc.wait()
    transpose_all(n2, tr)
    m.acc1[...] = m.resid[...]
    m.acc2[...] = jnp.zeros_like(m.acc2)
    red = Chunks(
        n_ff,
        lambda c: [
            Reduce(pc, m.b_in.at[c], *(a.at[c] for a in m.r_in), rs_in.at[c], m.ri_send.at[c], m.ri_recv.at[c], True),
            Reduce(pc, m.b_dn.at[c], *(a.at[c] for a in m.r_dn), rs_dn.at[c], m.rd_send.at[c], m.rd_recv.at[c], False),
        ],
    )
    hid, gact = m.back.at[0, :, pl.ds(0, fsdp * BLOCK)], m.back.at[1, :, pl.ds(0, fsdp * BLOCK)]

    @pl.loop(0, n_ff)
    def _(c):
        for g in ff(c):
            Gather.STAGES[3](g)

        b_in, b_dn = flat(m.b_in.at[c]), flat(m.b_dn.at[c])

        def put_in(val):
            b_in[...] = val

        def put_dn(val):
            b_dn[...] = val

        mlp_chunk(rows, n2, tr, cot, lambda: b_in[...], lambda: b_dn[...], m.acc1, m.acc2, hid, gact, put_in, put_dn, lambda: gather_steps(ff, c + 3))
        reduce_steps(red, c)

        @pl.when(guest & (c == 2))
        def _():
            pl.semaphore_wait(m.freed, 1)
            sized(True, lambda n: lent_q(n).start())


    @pl.loop(0, tiles)
    def _(t):
        r = rows_at(t * tile, tile)
        m.back[0, r, :] = bf(m.acc1[r, :])

    lo = local(m.back.at[0], outputs, m.l_sem.at[0])
    m.sums[...] = jnp.zeros_like(m.sums)
    second_norm_back(rows, m.lnp, m.resid, cot, m.acc2, m.resid, n2, m.sums)
    d_o = flat(m.cot)

    @pl.loop(0, width // tile)
    def _(t):
        r = rows_at(t * tile, tile)
        d_o[r, :] = bf(tn(mixed[:, pl.ds(pl.multiple_of(t * tile, tile), tile)], n2[...]))

    gmixed = n2
    branch_back(rows, n2, w_o, gmixed)
    head_sums(gmixed, mixed, m.inner)

    @pl.when(guest)
    def _():
        for c in lent_rows():
            c.start()

    sized(True, lambda n: lent_run(0, n).start())
    lo.wait()

    @pl.when((f < last) & jnp.logical_not(host))
    def _():
        pl.semaphore_signal(m.ready, inc=1, device_id=(pc.r, f + 1), device_id_type=MESH)

    sized(True, lambda n: lent_q(n).wait_send())

    transpose_all(n1, tr)
    mid, end = half + (pairs // 2 - GROUP) * BLOCK, width
    wide = 2 * (mid - half)
    rest = lambda ref: (ref.at[..., pl.ds(0, wide)], ref.at[..., pl.ds(wide, width - wide)])
    narrow = lambda refs, i: [ref.at[..., pl.ds(0, wide // 2) if i == 0 else pl.ds(wide // 2, half - wide // 2)] for ref in refs]
    buf1, buf2 = rest(m.b_o)
    res1, res2 = rest(rs_k)
    stat = [
        Reduce(pc, b, *scr, res, m.rs_send.at[i], m.rs_recv.at[i], xf)
        for i, (b, scr, res, xf) in enumerate(
            (
                (m.cot, m.r_o, rs_o, True), (m.mixed, m.r_q, rs_q, False), (m.g_v, m.r_v, rs_v, True),
                (buf1, narrow(m.r_k, 0), res1, True), (buf2, narrow(m.r_k, 1), res2, False),
            )
        )
    ]
    red_o, red_0, red_v, red_1, red_2 = stat

    def early(t, p):
        r, cols = pl.ds(t * tile, tile), run_cols(p)
        prev = (pc.r, f - 1)
        return [
            pltpu.make_async_remote_copy(
                src_ref=x.at[pl.ds(j * rows + t * tile, tile), cols], dst_ref=m.back.at[j, r, cols], send_sem=m.e_send.at[j, p, t], recv_sem=m.e_recv.at[j, p, t],
                device_id=prev, device_id_type=MESH,
            )
            for j in range(2)
        ]

    dk, dv = m.acc1, m.acc2

    def complete(g):
        cols = pl.ds(g * size, size)
        fresh = min(size, max(0, half - g * size))
        for t in range(tiles):
            r = pl.ds(t * tile, tile)

            @pl.when((f < last) & jnp.logical_not(host) & (t * tile >= next_start))
            def _():
                for j, own in enumerate((dk, dv)):
                    drain(m.back.at[j, r, cols], m.e_recv.at[j, g, t])
                    own[r, cols] += f32(m.back[j, r, cols])

            k[r, cols] = bf(dk[r, cols])
            if fresh:
                v[r, g * size:g * size + fresh] = bf(dv[r, g * size:g * size + fresh])

    def weight_grad(dst, at, grad, lo, hi):
        @pl.loop(0, width // tile)
        def _(t):
            r = rows_at(t * tile, tile)
            dst[r, at:at + hi - lo] = bf(mm(tr[r, :], grad[pl.ds(0, rows), lo:hi]))

    d_0, d_v, d_1 = flat(m.mixed), flat(m.g_v), w_o

    def run_0():
        complete(0)
        complete(1)
        weight_grad(d_0, 0, q, 0, half)
        weight_grad(d_0, half, k, 0, half)
        red_0.p1()
        d_v[:, half:] = jnp.zeros((width, d_v.shape[1] - half), jnp.bfloat16)
        weight_grad(d_v, 0, v, 0, half)
        red_v.p1()

    @pl.loop(0, 2 * groups)
    def _(s):
        p, part = s // 2, lax.rem(s, 2)
        cols = run_cols(p)
        middle = span.blocks // 2

        @pl.when(part == 0)
        def _():
            clear_rows(span, m.dk_acc, m.dv_acc)

        attend_back_group(
            span, p, part * middle, jnp.where(part == 0, middle, span.blocks), q, k, v, gmixed, m.bias, m.lse, m.inner, m.dk_acc, m.dv_acc, q, lent_keys
        )

        reduce_steps(red, n_ff + s)

        @pl.when((part == 0) & (p < groups - 1))
        def _():
            sized(True, lambda n: lent_run(p + 1, n).start())

        @pl.when(s == 1)
        def _():
            @pl.when((f > 0) & jnp.logical_not(guest))
            def _():
                pl.semaphore_wait(m.ready, 1)

        @pl.when(part == 1)
        def _():
            dk[:, cols] = m.dk_acc[rows:, :]
            dv[:, cols] = m.dv_acc[rows:, :]
            for t in range(tiles):

                @pl.when((f > 0) & jnp.logical_not(guest) & (t * tile >= span.start))
                def _():
                    r = pl.ds(t * tile, tile)
                    x[r, cols] = bf(m.dk_acc[r, :])
                    x[pl.ds(rows + t * tile, tile), cols] = bf(m.dv_acc[r, :])
                    for c in early(t, p):
                        c.start()

        @pl.when(host & (part == 1))
        def _():
            @pl.when(p == 0)
            def _():
                sized(False, lambda n: lent_q(n).wait_recv())
                for c in lent_rows():
                    c.wait_recv()

            sized(False, lambda n: lent_run(p, n).wait_recv())
            for j in range(GROUP):
                at = (span, p * GROUP + j, group_cols(p, j, GROUP))
                rest = (gq, gg, k, v, m.bias, m.g_lse, m.g_inner, dk, dv)
                trunk = ((0, 256, None), (256, 256, None))

                @pl.when(next_kind == 6)
                def _():
                    borrowed_back(*at, 0, (*trunk, (512, 256, 0)), *rest)

                @pl.when(next_kind == 4)
                def _():
                    @pl.loop(0, 2)
                    def _(n):
                        borrowed_back(*at, 2 * n, trunk, *rest)

        for i in range(4):

            @pl.when(s == REDUCE_AT[i])
            def _():
                Reduce.STAGES[i](red_o)

        @pl.when(s == 2 * groups - 2)
        def _():
            run_0()

        @pl.when(s == 2 * groups - 1)
        def _():
            red_0.p2()
            red_v.p2()

    weight_grad(d_1, 0, q, half, mid)
    weight_grad(d_1, mid - half, k, half, mid)
    red_1.p1()
    weight_grad(d_1, wide, q, mid, end)
    red_0.p3()
    red_v.p3()
    red_o.p5()
    complete(groups - 1)
    weight_grad(d_1, wide + end - mid, k, mid, end)
    red_2.p1()
    gf = local(dv.at[:, pl.ds(half, half)], gfirst, m.l_sem.at[1])
    lx = local(inputs, n1, m.l_sem.at[2])
    red_1.p2()
    red_2.p2()
    red_0.p4()
    red_v.p4()

    @pl.loop(0, tiles)
    def _(t):
        r = rows_at(t * tile, tile)
        dk[r, :] = nt(q[r, :], w_q[...]) + nt(k[r, :], w_k[...]) + nt(v[r, :half], w_v[:, :half])

    red_2.p3()
    red_1.p3()
    reduce_steps(red, n_ff + pairs)
    red_o.p6()
    lx.wait()

    @pl.loop(0, tiles)
    def _(t):
        r = rows_at(t * tile, tile)
        g = dk[r, :]
        hat, inv = normalized(f32(n1[r, :]))
        m.resid[r, :] += norm_back(hat, inv, g, m.lnp[0:1, :])
        m.sums[0:1, :] += jnp.sum(g * hat, axis=0, keepdims=True)
        m.sums[1:2, :] += jnp.sum(g, axis=0, keepdims=True)

    gi = local(m.resid, gin, m.l_sem.at[3])

    def exchange(src, dst, i, dev):
        c = pltpu.make_async_remote_copy(src_ref=src, dst_ref=dst, send_sem=m.v_send.at[i], recv_sem=m.v_recv.at[i], device_id=dev, device_id_type=MESH)
        c.start()
        return c

    cur = m.sums
    work = [
        (red_2.p4, red_1.p4, red_0.p5, red_v.p5), (red_0.p6, red_v.p6), (red_2.p5, red_1.p5, red_0.p7, red_v.p7),
    ]
    for i, dev in enumerate((pc.core, pc.xn, pc.yn)):
        c = exchange(cur, m.s_pair.at[i], 1 + i, dev)
        for step in work[i]:
            step()
        c.wait()
        m.s_pair[i] = m.s_pair[i] + cur[...]
        cur = m.s_pair.at[i]
    for o in pc.others:
        exchange(cur, m.s_z.at[f], 4, pc.zdev(o))
    red_2.p6()
    red_1.p6()
    red_o.p7()
    for u in range(n_ff + pairs + 1, n_ff + REDUCE_AT[-1]):
        reduce_steps(red, u)
    red_2.p7()
    red_1.p7()
    z3 = m.s_z.at[pl.ds(0, last)]
    drain(z3, m.v_recv.at[4])
    drain(z3, m.v_send.at[4])
    m.s_z[f] = cur[...]
    rs_vec[...] = functools.reduce(lambda a, b: a + b, [m.s_z[j] for j in range(fsdp)])
    for g in stat:
        g.p8()
        g.finish()

    @pl.loop(0, n_ff)
    def _(c):
        for g in red(c):
            g.p8()
            g.finish()

    @pl.loop(0, groups)
    def _(p):
        for t in range(tiles):

            @pl.when((f > 0) & jnp.logical_not(guest) & (t * tile >= span.start))
            def _():
                for c in early(t, p):
                    c.wait_send()

    def sent(n):
        for c in lent_rows():
            c.wait_send()
        for p in range(groups):
            lent_run(p, n).wait_send()

    sized(True, sent)
    gf.wait()
    gi.wait()


def layer_call(fsdp, inputs, first, cot, norms, w_query, w_key, w_value, w_out, w_in, w_down, segs, trees, table):
    rows, width = inputs.shape
    shard = w_query.shape[0]
    n_ff = w_down.shape[0] // BLOCK
    low, full = jnp.bfloat16, jnp.float32
    mq, md = shard // 4, BLOCK // 4
    pairs, blocks = width // (2 * HEAD), rows // BLOCK
    wide_v = width // 2 + BLOCK
    split = lambda a: a.reshape(2, 2, mq, a.shape[1])
    buf = lambda m, c, lead=(): (*lead, fsdp, 2, 2, m, c)
    chunk = fsdp * BLOCK
    sc = Scratch()
    V, D = pltpu.VMEM, pltpu.SemaphoreType.DMA
    for name, shape in (
        ("b_q", buf(mq, width)), ("b_k", buf(mq, width)), ("b_v", buf(mq, wide_v)), ("b_o", buf(mq, width)),
        ("b_in", buf(mq, chunk, (n_ff,))), ("b_dn", buf(md, width, (n_ff,))), ("g_v", buf(mq, wide_v)),
        ("mixed", buf(mq, width)), ("cot", buf(mq, width)), ("x", (2 * rows, width)), ("k", (2 * rows, width)), ("v", (2 * rows, width)),
        ("q", (rows, width)), ("n1", (rows, width)), ("n2", (rows, width)), ("tr", (width, rows)), ("back", (2, rows, width)),
    ):
        sc.add(name, V(shape, low))
    for name, shape in (
        ("vec", (fsdp, 8, width)), ("lnp", (8, width)), ("sums", (8, width)), ("s_pair", (3, 8, width)), ("s_z", (fsdp, 8, width)),
        ("resid", (rows, width)), ("acc1", (rows, width)), ("acc2", (rows, width)), ("bias", (blocks + 2, 3 * BLOCK, BLOCK)), ("inner", (pairs, 8, 2 * BLOCK)), ("g_inner", (pairs, 8, 2 * BLOCK)), ("g_lse", (pairs, -(-blocks // 8) * 8, 2 * BLOCK)),
        ("dk_acc", (2 * rows, GROUP * 2 * HEAD)), ("dv_acc", (2 * rows, GROUP * 2 * HEAD)), ("lse", (pairs, -(-blocks // 8) * 8, 2 * BLOCK)),
    ):
        sc.add(name, V(shape, full))
    for name, shape in (
        ("l_sem", (9,)), ("lc_sem", (n_ff, fsdp + 1)), ("v_send", (5,)), ("v_recv", (5,)), ("g_send", (4, 5)), ("g_recv", (4, 5)),
        ("w_send", (2, rows // row_tiles(rows))), ("w_recv", (2, rows // row_tiles(rows))),
        ("gi_send", (n_ff, 5)), ("gi_recv", (n_ff, 5)), ("gd_send", (n_ff, 5)), ("gd_recv", (n_ff, 5)),
        ("ri_send", (n_ff, 8)), ("ri_recv", (n_ff, 8)), ("rd_send", (n_ff, 8)), ("rd_recv", (n_ff, 8)), ("rs_send", (5, 8)), ("rs_recv", (5, 8)),
        ("b_send", (3 + pairs,)), ("b_recv", (3 + pairs,)), ("e_send", (2, pairs // GROUP, rows // row_tiles(rows))), ("e_recv", (2, pairs // GROUP, rows // row_tiles(rows))),
    ):
        sc.add(name, D(shape))
    sc.add("ready", pltpu.SemaphoreType.REGULAR)
    sc.add("freed", pltpu.SemaphoreType.REGULAR)
    groups = (("r_in", buf(mq, chunk), n_ff), ("r_dn", buf(md, width), n_ff), ("r_o", buf(mq, width), 0), ("r_q", buf(mq, width), 0), ("r_k", buf(mq, width), 0), ("r_v", buf(mq, wide_v), 0))
    for name, shape, lead in groups:
        for i, sub in enumerate(red_shapes(shape)):
            sc.add(f"{name}{i}", V((lead, *sub) if lead else sub, low))

    n_out = 10
    s = jax.ShapeDtypeStruct
    outs = (
        s((rows, width), low), s((rows, width), full), s((rows, width // 2), full),
        s((2, 2, mq, width), low), s((2, 2, mq, width), low), s((2, 2, mq, wide_v), low), s((2, 2, mq, width), low),
        s((n_ff, 2, 2, mq, chunk), low), s((n_ff, 2, 2, md, width), low), s((8, width), full),
    )

    def body(*refs):
        names = Scratch()
        names.names, names.shapes = sc.names, sc.shapes
        bound = names.bind(refs[N_IN + n_out :])
        for name, _, _ in groups:
            setattr(bound, name, [getattr(bound, f"{name}{i}") for i in range(4)])
        layer_kernel(fsdp, n_ff, bound, n_out, *refs)

    any_ = pl.BlockSpec(memory_space=pl.ANY)
    return pl.pallas_call(
        body, out_shape=outs, in_specs=[any_] * 9 + [VM] * 2 + [SM, VM], out_specs=[any_] * 3 + [VM] * 7, scratch_shapes=sc.shapes,
        compiler_params=pltpu.CompilerParams(collective_id=3, has_side_effects=True, vmem_limit_bytes=63 << 20),
    )(inputs, first, cot, split(w_query), split(w_key), split(w_value), split(w_out), split(w_in), w_down.reshape(n_ff, 2, 2, md, width), norms, segs, trees, table)


def finish_kernel(o_in, g_in, f_in, vec, *refs):
    src, (o_out, g_out, f_out, *dst), rows_out = refs[:6], refs[6:15], refs[15]
    low, full, passed, sem, load = refs[16:22], refs[22:28], refs[28:31], refs[31], refs[32]
    copies = []

    def go(src, dst):
        c = pltpu.make_async_copy(src, dst, sem.at[len(copies)])
        c.start()
        copies.append(c)

    loads = [pltpu.make_async_copy(a, b, load.at[i]) for i, (a, b) in enumerate(zip((*src, g_in, o_in, f_in), (*low, *passed)))]
    for c in loads[6:] + loads[:6]:
        c.start()
    (l_in, l_dn, l_0, l_1, l_o, l_v), (d_in, d_dn, d_q, d_k, d_o, d_v) = low, full

    def done(i, mid):
        go(mid, dst[i])

    n_ff, width = l_in.shape[0], l_0.shape[1]
    half = width // 2
    for c, a, b in zip(loads[6:], passed, (g_out, o_out, f_out)):
        c.wait()
        go(a, b)
    loads[0].wait()
    for j in range(n_ff):
        for g in range(l_in.shape[2] // BLOCK):
            at = (g * n_ff + j) * BLOCK
            d_in[:, at:at + BLOCK] = f32(l_in[j, :, g * BLOCK:(g + 1) * BLOCK])
    done(0, d_in)
    loads[1].wait()
    for j in range(n_ff):
        d_dn[j * BLOCK:(j + 1) * BLOCK, :] = f32(l_dn[j])
    done(1, d_dn)
    loads[2].wait()
    loads[3].wait()
    rest = half - GROUP * BLOCK
    tail = half - rest
    for i, mid in ((2, d_q), (3, d_k)):
        s = i - 2
        mid[:, :half] = f32(l_0[:, s * half:(s + 1) * half])
        mid[:, half:half + rest] = f32(l_1[:, s * rest:(s + 1) * rest])
        mid[:, half + rest:] = f32(l_1[:, 2 * rest + s * tail:2 * rest + (s + 1) * tail])
        done(i, mid)
    loads[4].wait()
    d_o[...] = f32(l_o[...])
    done(4, d_o)
    loads[5].wait()
    d_v[...] = f32(l_v[:, :half])
    done(5, d_v)
    rows, width = rows_out.shape[1], vec.shape[1]
    turned = pltpu.roll(vec[...], lax.rem(width - lax.axis_index("fsdp") * rows, width), 1)
    rows_out[...] = turned[:, :rows]
    for c in copies:
        c.wait()


def finish_call(outputs, gin, gfirst, rq, rk, rv, ro, ri, rd, vec):
    rows, width = rq.shape
    full = jnp.float32
    s = jax.ShapeDtypeStruct
    grads = (ri, rd, rq, rk, ro, rv)
    shapes = [(rows, ri.shape[0] * ri.shape[2]), (rd.shape[0] * BLOCK, width), (rows, width), (rows, width), (rows, width), (rows, width // 2)]
    hbm = pl.BlockSpec(memory_space=pltpu.HBM)
    out = pl.pallas_call(
        finish_kernel,
        out_shape=(s(outputs.shape, outputs.dtype), s(gin.shape, full), s(gfirst.shape, full), *(s(a, full) for a in shapes), s((8, rows), full)),
        in_specs=[hbm] * 3 + [VM] + [hbm] * 6, out_specs=[hbm] * 9 + [VM],
        scratch_shapes=[*(pltpu.VMEM(a.shape, a.dtype) for a in grads), *(pltpu.VMEM(a, full) for a in shapes), *(pltpu.VMEM(a.shape, a.dtype) for a in (gin, outputs, gfirst)), pltpu.SemaphoreType.DMA((9,)), pltpu.SemaphoreType.DMA((9,))],
        compiler_params=pltpu.CompilerParams(vmem_limit_bytes=61 << 20),
    )(outputs, gin, gfirst, vec, *grads)
    din, ddn, dq, dk, do, dv = out[3:9]
    return out[0], out[1], out[2], dq, dk, dv, do, din, ddn, out[9]


def shifted(block, axis, distance):
    devices = range(lax.axis_size(axis))
    route = [(i - distance, i) for i in devices if i - distance in devices]
    return lax.ppermute(block, axis, route)


def reorder_rows(grad_block, fsdp_count, rep_count):
    return grad_block.reshape(fsdp_count, rep_count, -1).transpose(1, 0, 2).reshape(-1)


def packed_qkv(query, key, value):
    h, pad = query.shape[1] * 2 // 3, jnp.zeros_like(value[:, : value.shape[1] // 3])
    n = value.shape[1] * 2 // 3
    return jnp.concatenate([query[:, :h], key[:, :h], query[:, h:], value[:, :n], key[:, h:], value[:, n:], pad], axis=1)


def unpacked_qkv(first, second):
    h = first.shape[-1] // 2
    q = h // 2
    return (
        jnp.concatenate([first[..., :h], second[..., :q]], axis=-1),
        jnp.concatenate([first[..., h:], second[..., h : h + q]], axis=-1),
        jnp.concatenate([second[..., q:h], second[..., h + q : h + q + q // 2]], axis=-1),
    )


def gathered(fsdp, gain1, shift1, gain2, shift2, w_query, w_key, w_value, w_out, w_in, w_down):
    width = w_query.shape[1]
    n_ff = w_down.shape[0] // BLOCK
    packed = packed_qkv(w_query, w_key, w_value)
    full = [lax.all_gather(v, "fsdp", axis=0, tiled=True) for v in (packed, w_out, w_in, w_down)]
    vec = lax.all_gather(jnp.stack([gain1, shift1, gain2, shift2]), "fsdp", axis=1, tiled=True).astype(jnp.float32)
    half = packed.shape[1] // 2
    inner = full[2].reshape(width, fsdp, n_ff, BLOCK).transpose(2, 0, 1, 3).reshape(n_ff, width, -1)
    down = full[3].reshape(fsdp, n_ff, BLOCK, width).transpose(1, 0, 2, 3).reshape(n_ff, -1, width)
    return jnp.pad(vec, ((0, 4), (0, 0))), full[0][:, :half], full[0][:, half:], full[1], inner, down


def reduced(fsdp, sums, g1, g2, go, gin, gdn):
    width = go.shape[0]
    rows = width // fsdp
    n_ff = gin.shape[0]
    both = ("rep", "fsdp")
    rep = lax.axis_size("rep")

    def total(a):
        piece = lax.psum_scatter(reorder_rows(a.astype(jnp.float32), fsdp, rep), both, scatter_dimension=0, tiled=True)
        return lax.all_gather(piece.astype(jnp.bfloat16), "rep", axis=0, tiled=True)

    first, second, ro = (total(a).reshape(rows, -1) for a in (g1, g2, go))
    ri = total(gin.transpose(1, 0, 2)).reshape(rows, n_ff, -1).transpose(1, 0, 2)
    rd = total(gdn.reshape(n_ff, fsdp, BLOCK, width).transpose(1, 0, 2, 3)).reshape(n_ff, BLOCK, width)
    return lax.psum(sums, both), *unpacked_qkv(first, second), ro, ri, rd


def one_kernel(inputs, first_values, cotangent, segs, trees, table, gain1, shift1, gain2, shift2, w_query, w_key, w_value, w_out, w_in, w_down):
    fsdp = lax.axis_size("fsdp")
    rows, width = w_query.shape
    norms = jnp.concatenate([gain1, shift1, gain2, shift2]).reshape(4, rows)
    outputs, input_grad, first_grad, rq, rk, rv, ro, ri, rd, sums = layer_call(
        fsdp, inputs, first_values, cotangent, norms, w_query, w_key, w_value, w_out, w_in, w_down, segs, trees, table
    )
    rq, rk, rv, ro, ri, rd = (a.reshape(*a.shape[:-4], -1, a.shape[-1]) for a in (rq, rk, rv, ro, ri, rd))
    outputs, input_grad, first_grad, rq, rk, rv, ro, ri, rd, sums = finish_call(outputs, input_grad, first_grad, rq, rk, rv, ro, ri, rd, sums)
    return outputs, input_grad, first_grad, sums[0], sums[1], rq, rk, rv, ro, sums[2], sums[3], ri, rd


def several_kernels(reach, inputs, first_values, cotangent, segs, trees, table, gain1, shift1, gain2, shift2, w_query, w_key, w_value, w_out, w_in, w_down):
    row_count, width = inputs.shape
    fsdp = lax.axis_size("fsdp")
    lnp, w1, w2, wo, win, wdn = gathered(fsdp, gain1, shift1, gain2, shift2, w_query, w_key, w_value, w_out, w_in, w_down)
    x = jnp.concatenate([shifted(inputs, "fsdp", d) for d in range(reach, 0, -1)] + [inputs], axis=0)
    fv = jnp.concatenate([shifted(first_values, "fsdp", d) for d in range(reach, 0, -1)] + [first_values], axis=0)
    n1, q, k, v, mixed, lse, resid, n2 = forward_call(fsdp, reach, x, fv, lnp, w1, w2, wo, segs, trees, table)
    outputs, gin, gdn, go, gres, gmixed, sums = mlp_call(n2, cotangent, resid, mixed, lnp, win, wdn, wo)
    dq, dk, dv, wk, wv = backward_call(fsdp, reach, q, k, v, gmixed, mixed, lse, segs, trees, table)
    for d in range(1, reach + 1):
        early = slice((reach - d) * row_count, (reach - d + 1) * row_count)
        both = shifted(jnp.concatenate([wk[early], wv[early]], axis=1), "fsdp", -d).astype(jnp.float32)
        dk, dv = dk + both[:, :width], dv + both[:, width:]
    input_grad, first_grad, g1, g2, sums = projection_back_call(fsdp, reach, x, n1, dq, dk, dv, lnp, w1, w2, gres, sums)
    return outputs, input_grad, first_grad, *reduced(fsdp, sums, g1, g2, go, gin, gdn)


def on_device(
    inputs,
    first_values,
    cotangent,
    tree_ids,
    segment_ids,
    path_table,
    attn_gain,
    attn_shift,
    w_query,
    w_key,
    w_value,
    w_out,
    mlp_gain,
    mlp_shift,
    w_in,
    w_down,
):
    row_count, width = inputs.shape
    fsdp = lax.axis_size("fsdp")
    reach = 0
    for device_pos in range(fsdp):
        offset = device_pos * row_count % TREE_LEN
        reach = max(reach, (offset + row_count - 1) // row_count)
    marks = (segment_ids.reshape(-1, BLOCK), tree_ids, path_table)
    weights = (attn_gain, attn_shift, mlp_gain, mlp_shift, w_query, w_key, w_value, w_out, w_in, w_down)
    if lax.axis_size("rep") == 8 and reach == 1 and row_count == width:
        return one_kernel(inputs, first_values, cotangent, *marks, *weights)
    results = several_kernels(reach, inputs, first_values, cotangent, *marks, *weights)
    outputs, input_grad, first_grad, sums, d_q, d_k, d_v, d_o, d_in, d_dn = results
    rows = w_query.shape[0]
    sums = lax.dynamic_slice_in_dim(sums, lax.axis_index("fsdp") * rows, rows, 1)
    d_in = d_in.reshape(-1, rows, fsdp, BLOCK).transpose(1, 2, 0, 3).reshape(rows, -1)
    d_q, d_k, d_v, d_o, d_in, d_dn = (a.astype(jnp.float32) for a in (d_q, d_k, d_v, d_o, d_in, d_dn.reshape(-1, width)))
    return (outputs, input_grad, first_grad, sums[0], sums[1], d_q, d_k, d_v, d_o, sums[2], sums[3], d_in, d_dn)


def solution(mesh):
    placed = (
        P(("rep", "fsdp"), None),
        P(("rep", "fsdp"), None),
        P(("rep", "fsdp"), None),
        P("rep"),
        P("rep"),
        P("rep", None, None),
        P("fsdp"),
        P("fsdp"),
        P("fsdp", None),
        P("fsdp", None),
        P("fsdp", None),
        P("fsdp", None),
        P("fsdp"),
        P("fsdp"),
        P("fsdp", None),
        P("fsdp", None),
    )
    return jax.shard_map(
        on_device,
        mesh=mesh,
        in_specs=placed,
        out_specs=(
            P(("rep", "fsdp"), None),
            P(("rep", "fsdp"), None),
            P(("rep", "fsdp"), None),
            P("fsdp"),
            P("fsdp"),
            P("fsdp", None),
            P("fsdp", None),
            P("fsdp", None),
            P("fsdp", None),
            P("fsdp"),
            P("fsdp"),
            P("fsdp", None),
            P("fsdp", None),
        ),
        check_vma=False,
    )
```
